32 devices in a mesh: dp: 8 (over z, y), mp: 4 (over x, core).
Axes of the slice: x: 2, y: 2, z: 4, core: 2. Of those that a mesh axis runs over, the one named last changes fastest.
Arguments:
- tokens: bfloat16 [16384, 1024], P(('dp', 'mp')), may hold values from -6 to 6
- segment_ids: int32 [16384], P(('dp', 'mp')), may hold values from 0 to 63, never falling along the last dimension, each value on 1 to 512 neighbouring positions
- w_qkv: bfloat16 [3, 1024, 1024], P(None, None, 'mp'), may hold values from -0.1875 to 0.1875
- b_qv: bfloat16 [2, 1024], P(None, 'mp'), may hold values from -1.75 to 1.75
- w_out: bfloat16 [1024, 1024], P('mp'), may hold values from -2 to 2
- b_out: bfloat16 [1024], replicated, may hold values from -1.75 to 1.75
- w_up: bfloat16 [1024, 4096], P(None, 'mp'), may hold values from -0.1875 to 0.1875
- b_up: bfloat16 [4096], P('mp'), may hold values from -1.75 to 1.75
- w_down: bfloat16 [4096, 1024], P('mp'), may hold values from -0.125 to 0.125
- b_down: bfloat16 [1024], replicated, may hold values from -1.75 to 1.75
- ln_gain: float32 [2, 1024], replicated, may hold values from 0.5 to 1.5
- ln_bias: float32 [2, 1024], replicated, may hold values from -1.75 to 1.75
- out_grad: bfloat16 [16384, 1024], P(('dp', 'mp')), may hold values from -6 to 6
Outputs:
- block_out: bfloat16 [16384, 1024], P(('dp', 'mp'))
- grad_in: float32 [16384, 1024], P(('dp', 'mp'))
- grad_qkv: float32 [3, 1024, 1024], P(None, None, 'mp')
- grad_bqv: float32 [2, 1024], P(None, 'mp')
- grad_wout: float32 [1024, 1024], P('mp')
- grad_bout: float32 [1024], replicated
- grad_up: float32 [1024, 4096], P(None, 'mp')
- grad_bup: float32 [4096], P('mp')
- grad_down: float32 [4096, 1024], P('mp')
- grad_bdown: float32 [1024], replicated
- grad_gain: float32 [2, 1024], replicated
- grad_shift: float32 [2, 1024], replicated
The draws below stay inside these ranges and needn't reach their ends.
Inputs may be any that keep to these rules, and one draw needn't show every extreme that they name: `segment_ids`: along all frames in order, segment numbers never fall; each segment covers 1 to 512 frames and one covers exactly 512; attention never crosses a row of 1024 frames.
All inputs are finite; a program needn't handle non-finite values.
Results may differ from the reference program's by a relative error of at most 0.02.
Values may be sent and summed in bfloat16 or wider, within the bound.
No kernel may reach another device: no remote copies, remote signals or barrier semaphores. Data moves between devices by JAX's collectives and lax.ppermute only.
A program may use at most 192 MiB of HBM per device.

```python
import math
from functools import partial
import jax
import jax.numpy as jnp
import numpy as np
from jax import lax

D = 1024
HEADS = 16
HD = 64
FF = 4096
LEN = 1024
QBLK = 512
ROWS_DEV = 2
TOKENS = 16384
N_DP = 8


def steps_of(key, extent, shards, smallest, high):
    factor_of = 1.0
    for axis_at, shards_of in shards:
        draws = jax.random.uniform(jax.random.fold_in(jax.random.fold_in(key, 6), axis_at), (shards_of,), jnp.float32, smallest / len(shards), high / len(shards))
        factor_of = factor_of * jnp.repeat(jnp.exp(draws), extent[axis_at] // shards_of).reshape((-1,) + (1,) * (len(extent) - 1 - axis_at))
    return factor_of


def length_profile(count, total, limit, lean):
    weights = [(1 << 20) // math.isqrt(standing ** lean) + 1 for standing in range(2, count + 1)]
    surplus, counts = total - limit - (count - 1), [1] * (count - 1)
    while surplus > 0:
        candidates = [i for i in range(count - 1) if counts[i] < limit]
        mass, left = sum([weights[i] for i in candidates]), surplus
        for i in candidates:
            extra = min(limit - counts[i], max(1, left * weights[i] // mass), surplus)
            counts[i] = counts[i] + extra
            surplus = surplus - extra
    return np.array([limit] + counts)


def ragged(key, amount, total, bound, lean):
    if amount == 2:
        one = jax.random.randint(key, (), max(1, total - bound), min(bound, total - 1) + 1)
        return jnp.stack([one, total - one])
    lengths = jnp.asarray(length_profile(amount, total, bound, lean), jnp.int32)
    twos = (amount - 1) // 2
    source_of, receiver = lengths[1:1 + 2 * twos:2], lengths[2:2 + 2 * twos:2]
    margin = jnp.minimum(source_of - 1, bound - receiver)
    shifted = jax.random.randint(jax.random.fold_in(key, 1), (twos,), 0, 1 << 20) % (margin + 1)
    lengths = lengths.at[1:1 + 2 * twos:2].set(source_of - shifted).at[2:2 + 2 * twos:2].set(receiver + shifted)
    return lengths[jax.random.permutation(jax.random.fold_in(key, 2), amount)]


def noise(rng, dims, deviation, most, cuts=(), kind=jnp.bfloat16):
    drawn = jax.random.normal(rng, dims, jnp.float32) * deviation
    if len(cuts) > 0:
        drawn = steps_of(rng, dims, cuts, -0.22, 0.18) * drawn
    return jnp.clip(drawn, min=-most, max=most).astype(kind)


def setup_inputs(seed: int = 0) -> dict:
    seeds = jax.random.split(jax.random.key(seed), 14)
    tokens = noise(seeds[0], (TOKENS, D), 1.0, 6.0, ((0, 32),))
    segment_ids = jnp.searchsorted(jnp.cumsum(ragged(seeds[1], TOKENS * 4 // LEN, TOKENS, LEN // 2, 2)), jnp.arange(TOKENS), side="right").astype(jnp.int32)
    w_qkv = noise(seeds[2], (3, D, D), D ** -0.5, 0.1875, ((2, 4),))
    b_qv = noise(seeds[3], (2, D), 0.3, 1.75, ((1, 4),))
    w_out = noise(seeds[4], (D, D), (max(D // 128, 4)) ** -0.5, 2.0, ((0, 4),))
    b_out = noise(seeds[5], (D,), 0.3, 1.75)
    w_up = noise(seeds[6], (D, FF), D ** -0.5, 0.1875, ((1, 4),))
    b_up = noise(seeds[7], (FF,), 0.3, 1.75, ((0, 4),))
    w_down = noise(seeds[8], (FF, D), (FF // 2) ** -0.5, 0.125, ((0, 4),))
    b_down = noise(seeds[9], (D,), 0.3, 1.75)
    ln_gain = jnp.clip(1.0 + 0.1 * jax.random.normal(seeds[10], (2, D), jnp.float32), 0.5, 1.5)
    ln_bias = noise(seeds[11], (2, D), 0.3, 1.75, (), jnp.float32)
    out_grad = noise(seeds[12], (TOKENS, D), 1.0, 6.0, ((0, 32),))
    return {"tokens": tokens, "segment_ids": segment_ids, "w_qkv": w_qkv, "b_qv": b_qv, "w_out": w_out, "b_out": b_out, "w_up": w_up, "b_up": b_up, "w_down": w_down, "b_down": b_down, "ln_gain": ln_gain, "ln_bias": ln_bias, "out_grad": out_grad}


@jax.custom_vjp
def low(v):
    return lax.optimization_barrier(v.astype(jnp.bfloat16)).astype(jnp.float32)

@jax.custom_vjp
def low_back(v):
    return v

def low_keep(v):
    return (low(v), None)

def low_pass(kept, grad):
    return (grad,)

def back_keep(v):
    return (v, None)

def back_low(kept, grad):
    return (low(grad),)
low.defvjp(low_keep, low_pass)
low_back.defvjp(back_keep, back_low)
EPS = 1e-05
HIGH = lax.Precision.HIGHEST

def hdot(left, right):
    return jnp.dot(left, right, precision=HIGH, preferred_element_type=jnp.float32)

def norm_rows(values, gain, shift):
    center = values - lax.optimization_barrier(jnp.mean(values, axis=-1, keepdims=True))
    spread = lax.optimization_barrier(jnp.mean(center * center, axis=-1, keepdims=True))
    return center * lax.rsqrt(spread + EPS) * gain + shift

def attend_block(query, keys, values, seg_q, seg_k, offset):
    scores = jnp.einsum('qhd,khd->hqk', query, keys, precision=HIGH) * HD ** (-0.5)
    scores = low_back(scores)
    q_pos = offset + jnp.arange(query.shape[0], dtype=jnp.int32)
    k_pos = jnp.arange(keys.shape[0], dtype=jnp.int32)
    allowed = (seg_q[:, None] == seg_k[None, :]) & (k_pos[None, :] <= q_pos[:, None])
    scores = jnp.where(allowed[None], scores, -1e+30)
    top = lax.optimization_barrier(jnp.max(scores, axis=-1, keepdims=True))
    expd = jnp.exp(scores - top)
    probs = expd / lax.optimization_barrier(jnp.sum(expd, axis=-1, keepdims=True))
    weights = low(probs)
    return jnp.einsum('hqk,khd->qhd', weights, values, precision=HIGH)

def attend_row(query, keys, values, seg):
    pieces = []
    for block in range(LEN // QBLK):
        first = block * QBLK
        end = first + QBLK
        step_fn = jax.checkpoint(partial(attend_block, offset=first))
        pieces.append(step_fn(query[first:end], keys[:end], values[:end], seg[first:end], seg[:end]))
    return jnp.concatenate(pieces, axis=0)

def layer(xg, segg, params):
    w_qkv, b_qv, w_out, b_out, w_up, b_up, w_down, b_down, ln_gain, ln_bias = params
    a1 = low(norm_rows(xg, ln_gain[0], ln_bias[0]))
    query = low(low_back(hdot(a1, w_qkv[0]) + b_qv[0]))
    keys = low(low_back(hdot(a1, w_qkv[1])))
    values = low(low_back(hdot(a1, w_qkv[2]) + b_qv[1]))
    shape4 = (ROWS_DEV, LEN, HEADS, HD)
    q4 = query.reshape(shape4)
    k4 = keys.reshape(shape4)
    v4 = values.reshape(shape4)
    rows_out = []
    for row in range(ROWS_DEV):
        rows_out.append(attend_row(q4[row], k4[row], v4[row], segg[row]))
    attended = jnp.stack(rows_out).reshape(ROWS_DEV * LEN, D)
    attended = low(low_back(attended))
    branch = low_back(hdot(attended, w_out) + b_out)
    mixed = xg + branch
    a2 = low(norm_rows(mixed, ln_gain[1], ln_bias[1]))
    pre = low_back(hdot(a2, w_up) + b_up)
    activ = low(jax.nn.gelu(pre, approximate=False))
    branch2 = low_back(hdot(activ, w_down) + b_down)
    return mixed + branch2

def reference(tokens, segment_ids, w_qkv, b_qv, w_out, b_out, w_up, b_up, w_down, b_down, ln_gain, ln_bias, out_grad):
    params = tuple((p.astype(jnp.float32) for p in (w_qkv, b_qv, w_out, b_out, w_up, b_up, w_down, b_down, ln_gain, ln_bias)))
    xs = tokens.astype(jnp.float32).reshape(N_DP, ROWS_DEV * LEN, D)
    segs = segment_ids.reshape(N_DP, ROWS_DEV, LEN)
    step_fn = jax.checkpoint(layer)

    def forward(xs, params):
        return lax.map(lambda pair: step_fn(pair[0], pair[1], params), (xs, segs))
    result, pullback = jax.vjp(forward, xs, params)
    cot = out_grad.astype(jnp.float32).reshape(N_DP, ROWS_DEV * LEN, D)
    grad_x, grads = pullback(cot)
    block_out = result.reshape(TOKENS, D).astype(jnp.bfloat16)
    grad_in = grad_x.reshape(TOKENS, D)
    return (block_out, grad_in, grads[0], grads[1], grads[2], grads[3], grads[4], grads[5], grads[6], grads[7], grads[8], grads[9])
```

```python
import jax
import jax.numpy as jnp
from jax import lax
from jax.experimental import pallas as pl
from jax.experimental.pallas import tpu as pltpu
from jax.sharding import PartitionSpec as P

HD = 64
LEN = 1024
QBLK = 512
EPS = 1e-05
BLK = 256
NEG = -1e30
f32 = jnp.float32
bf16 = jnp.bfloat16


def nt(left, right):
    return lax.dot_general(left, right, (((1,), (1,)), ((), ())), preferred_element_type=f32)


def nn(left, right):
    return lax.dot_general(left, right, (((1,), (0,)), ((), ())), preferred_element_type=f32)


def tn(left, right):
    return lax.dot_general(left, right, (((0,), (0,)), ((), ())), preferred_element_type=f32)


def head_masks():
    lane = lax.broadcasted_iota(jnp.int32, (BLK, 2 * HD), 1)
    return (lane < HD, lane >= HD)


def pick(mask, value):
    return jnp.where(mask, value, jnp.zeros_like(value))


def attn_fwd_body(info, q_ref, k_ref, v_ref, st_ref, o_ref, lse_ref):
    block = pl.program_id(1)
    query = q_ref[...]
    first = st_ref[...]
    q_pos = block * BLK + lax.broadcasted_iota(jnp.int32, (1, BLK), 1)
    masks = head_masks()
    sub = lax.broadcasted_iota(jnp.int32, (BLK, BLK), 0)

    def step(at, carry):
        j = block - at
        row = pl.multiple_of((j ^ info[0]) * BLK, BLK)
        keys = k_ref[pl.ds(row, BLK), :]
        vals_t = v_ref[pl.ds(row, BLK), :].T
        k_pos = sub + j * BLK
        allowed = (k_pos >= first) & (k_pos <= q_pos)
        out = []
        for h in range(2):
            top, total, acc = carry[h]
            s = jnp.where(allowed, nt(pick(masks[h], keys), query), NEG)
            new = jnp.maximum(top, jnp.max(s, axis=0, keepdims=True))
            scale = jnp.exp(top - new)
            p = jnp.exp(s - new)
            total = total * scale + jnp.sum(p, axis=0, keepdims=True)
            acc = acc * scale + nn(vals_t[h * HD : (h + 1) * HD], p.astype(bf16))
            out.append((new, total, acc))
        return tuple(out)

    init = tuple(
        (jnp.full((1, BLK), NEG, f32), jnp.zeros((1, BLK), f32), jnp.zeros((HD, BLK), f32))
        for _ in range(2)
    )
    done = lax.fori_loop(0, block + 1 - info[1 + block], step, init)
    both = jnp.concatenate([acc / total for _, total, acc in done], axis=0)
    o_ref[...] = both.T.astype(bf16)
    for h in range(2):
        top, total, _ = done[h]
        lse_ref[0, h : h + 1, :] = top + jnp.log(total)


def attn_bwd_body(info, q_ref, k_ref, v_ref, st_ref, o_ref, lse_ref, do_ref, dq_ref, dk_ref, dv_ref, dk_acc, dv_acc):
    block = pl.program_id(1)

    @pl.when(block == 0)
    def _():
        dk_acc[...] = jnp.zeros_like(dk_acc)
        dv_acc[...] = jnp.zeros_like(dv_acc)

    query = q_ref[...]
    cot = do_ref[...]
    first = st_ref[...]
    q_pos = block * BLK + lax.broadcasted_iota(jnp.int32, (1, BLK), 1)
    masks = head_masks()
    sub = lax.broadcasted_iota(jnp.int32, (BLK, BLK), 0)
    prod_t = (cot.astype(f32) * o_ref[...].astype(f32)).T
    delta = [jnp.sum(prod_t[h * HD : (h + 1) * HD], axis=0, keepdims=True) for h in range(2)]
    lse = [lse_ref[0, h : h + 1, :] for h in range(2)]
    q_heads = [pick(m, query) for m in masks]
    c_heads = [pick(m, cot) for m in masks]

    def step(j, dq):
        row = pl.multiple_of((j ^ info[0]) * BLK, BLK)
        keys = k_ref[pl.ds(row, BLK), :]
        vals = v_ref[pl.ds(row, BLK), :]
        k_pos = sub + j * BLK
        allowed = (k_pos >= first) & (k_pos <= q_pos)
        dk = dk_acc[pl.ds(row, BLK), :]
        dv = dv_acc[pl.ds(row, BLK), :]
        for h in range(2):
            k_head = pick(masks[h], keys)
            p = jnp.exp(jnp.where(allowed, nt(k_head, query) - lse[h], NEG))
            dp = nt(pick(masks[h], vals), cot)
            ds = (p * (dp - delta[h])).astype(bf16)
            dv = dv + nn(p.astype(bf16), c_heads[h])
            dk = dk + nn(ds, q_heads[h])
            dq = dq + tn(ds, k_head)
        dk_acc[pl.ds(row, BLK), :] = dk
        dv_acc[pl.ds(row, BLK), :] = dv
        return dq

    dq = lax.fori_loop(info[1 + block], block + 1, step, jnp.zeros((BLK, 2 * HD), f32))
    dq_ref[...] = (dq * HD**-0.5).astype(bf16)

    @pl.when(block == pl.num_programs(1) - 1)
    def _():
        dk_ref[...] = dk_acc[...].astype(bf16)
        dv_ref[...] = dv_acc[...].astype(bf16)


def specs():
    small = pl.BlockSpec((BLK, 2 * HD), lambda p, i, info: (i ^ info[0], p))
    whole = pl.BlockSpec((LEN, 2 * HD), lambda p, i, info: (0, p))
    start = pl.BlockSpec((1, BLK), lambda p, i, info: (0, i ^ info[0]))
    lse = pl.BlockSpec((1, 2, BLK), lambda p, i, info: (p, 0, i ^ info[0]))
    return small, whole, start, lse


def attn_fwd(info, query, keys, values, start):
    pairs = query.shape[1] // (2 * HD)
    small, whole, first, lse = specs()
    return pl.pallas_call(
        attn_fwd_body,
        out_shape=(
            jax.ShapeDtypeStruct(query.shape, bf16),
            jax.ShapeDtypeStruct((pairs, 2, LEN), f32),
        ),
        grid_spec=pltpu.PrefetchScalarGridSpec(
            num_scalar_prefetch=1,
            grid=(pairs, LEN // BLK),
            in_specs=[small, whole, whole, first],
            out_specs=[small, lse],
        ),
        cost_estimate=pl.CostEstimate(
            flops=4 * pairs * 10 * BLK * BLK * 256 * 2, bytes_accessed=4 << 20, transcendentals=pairs * 20 * BLK * BLK
        ),
        name="attn_fwd",
    )(info, query, keys, values, start)


def attn_bwd(info, query, keys, values, start, out, lse, cot):
    pairs = query.shape[1] // (2 * HD)
    small, whole, first, lse_spec = specs()
    shape = jax.ShapeDtypeStruct(query.shape, bf16)
    return pl.pallas_call(
        attn_bwd_body,
        out_shape=(shape, shape, shape),
        grid_spec=pltpu.PrefetchScalarGridSpec(
            num_scalar_prefetch=1,
            grid=(pairs, LEN // BLK),
            in_specs=[small, whole, whole, first, small, lse_spec, small],
            out_specs=[small, whole, whole],
            scratch_shapes=[pltpu.VMEM((LEN, 2 * HD), f32), pltpu.VMEM((LEN, 2 * HD), f32)],
        ),
        cost_estimate=pl.CostEstimate(
            flops=10 * pairs * 10 * BLK * BLK * 256 * 2, bytes_accessed=4 << 20, transcendentals=pairs * 20 * BLK * BLK
        ),
        name="attn_bwd",
    )(info, query, keys, values, start, out, lse, cot)


def up_body(a_ref, w_ref, b_ref, g_ref, s_ref):
    rows = a_ref[...]
    for part in range(w_ref.shape[1] // 256):
        cols = slice(part * 256, part * 256 + 256)
        u = nn(rows, w_ref[:, cols]) + b_ref[:, cols].astype(f32)
        size = jnp.abs(u)
        t = 1.0 / (1.0 + 0.3275911 * 0.7071067811865476 * size)
        poly = t * (0.5 * 0.254829592 + t * (0.5 * -0.284496736 + t * (0.5 * 1.421413741 + t * (0.5 * -1.453152027 + t * (0.5 * 1.061405429)))))
        bell = jnp.exp(-0.5 * u * u)
        tail = poly * bell
        cdf = jnp.where(u >= 0, 1.0 - tail, tail)
        g_ref[:, cols] = (u * cdf).astype(bf16)
        s_ref[:, cols] = (cdf + u * bell * 0.3989422804014327).astype(bf16)


def up_gelu(rows, weight, bias):
    m, k = rows.shape
    n = weight.shape[1]
    bm = 256
    shape = jax.ShapeDtypeStruct((m, n), bf16)
    tile = pl.BlockSpec((bm, n), lambda i: (i, 0))
    return pl.pallas_call(
        up_body,
        out_shape=(shape, shape),
        grid=(m // bm,),
        in_specs=[pl.BlockSpec((bm, k), lambda i: (i, 0)), pl.BlockSpec((k, n), lambda i: (0, 0)), pl.BlockSpec((1, n), lambda i: (0, 0))],
        out_specs=(tile, tile),
        cost_estimate=pl.CostEstimate(flops=2 * m * n * k * 2, bytes_accessed=8 << 20, transcendentals=m * n),
        name="up_gelu",
    )(rows, weight, bias.reshape(1, n))


def norm_rows(values, gain, shift):
    center = values - jnp.mean(values, axis=-1, keepdims=True)
    spread = jnp.mean(center * center, axis=-1, keepdims=True)
    return center * lax.rsqrt(spread + EPS) * gain + shift


def split_heads(flat, rows):
    return flat.reshape(rows, LEN, flat.shape[1] // HD, HD)


def block_scores(query, keys, seg_q, seg_k, offset):
    scores = jnp.einsum(
        "rqhd,rkhd->rhqk", query, keys, preferred_element_type=jnp.float32
    ) * HD ** (-0.5)
    q_pos = offset + jnp.arange(query.shape[1], dtype=jnp.int32)
    k_pos = jnp.arange(keys.shape[1], dtype=jnp.int32)
    allowed = (seg_q[:, :, None] == seg_k[:, None, :]) & (
        k_pos[None, None, :] <= q_pos[None, :, None]
    )
    return jnp.where(allowed[:, None], scores, -1e30)


def attention_forward(query, keys, values, seg_all):
    rows = query.shape[0] // LEN
    q4 = split_heads(query, rows)
    k4 = split_heads(keys, rows)
    v4 = split_heads(values, rows)
    seg2 = seg_all.reshape(rows, LEN)
    outputs = []
    totals = []
    for block in range(LEN // QBLK):
        first = block * QBLK
        end = first + QBLK
        scores = block_scores(
            q4[:, first:end], k4[:, :end], seg2[:, first:end], seg2[:, :end], first
        )
        top = jnp.max(scores, axis=-1, keepdims=True)
        expd = jnp.exp(scores - top)
        summed = jnp.sum(expd, axis=-1, keepdims=True)
        weights = (expd / summed).astype(jnp.bfloat16)
        outputs.append(
            jnp.einsum("rhqk,rkhd->rqhd", weights, v4[:, :end], preferred_element_type=jnp.float32)
        )
        totals.append(top + jnp.log(summed))
    attended = jnp.concatenate(outputs, axis=1).reshape(query.shape).astype(jnp.bfloat16)
    return (attended, totals)


def attention_backward(query, keys, values, seg_all, totals, grad_att):
    rows = query.shape[0] // LEN
    q4 = split_heads(query, rows)
    k4 = split_heads(keys, rows)
    v4 = split_heads(values, rows)
    g4 = split_heads(grad_att, rows)
    seg2 = seg_all.reshape(rows, LEN)
    scale = HD ** (-0.5)
    grad_k = jnp.zeros(k4.shape, jnp.float32)
    grad_v = jnp.zeros(v4.shape, jnp.float32)
    grad_q_parts = []
    for block in range(LEN // QBLK):
        first = block * QBLK
        end = first + QBLK
        scores = block_scores(
            q4[:, first:end], k4[:, :end], seg2[:, first:end], seg2[:, :end], first
        )
        probs = jnp.exp(scores - totals[block])
        weights = probs.astype(jnp.bfloat16)
        grad_w = jnp.einsum(
            "rqhd,rkhd->rhqk", g4[:, first:end], v4[:, :end], preferred_element_type=jnp.float32
        )
        delta = jnp.sum(probs * grad_w, axis=-1, keepdims=True)
        grad_s = (probs * (grad_w - delta)).astype(jnp.bfloat16)
        grad_q_parts.append(
            jnp.einsum("rhqk,rkhd->rqhd", grad_s, k4[:, :end], preferred_element_type=jnp.float32)
            * scale
        )
        padding = ((0, 0), (0, LEN - end), (0, 0), (0, 0))
        grad_k = grad_k + jnp.pad(
            jnp.einsum(
                "rhqk,rqhd->rkhd", grad_s, q4[:, first:end], preferred_element_type=jnp.float32
            )
            * scale,
            padding,
        )
        grad_v = grad_v + jnp.pad(
            jnp.einsum(
                "rhqk,rqhd->rkhd", weights, g4[:, first:end], preferred_element_type=jnp.float32
            ),
            padding,
        )
    shape = query.shape
    grad_q = jnp.concatenate(grad_q_parts, axis=1).reshape(shape).astype(jnp.bfloat16)
    return (
        grad_q,
        grad_k.reshape(shape).astype(jnp.bfloat16),
        grad_v.reshape(shape).astype(jnp.bfloat16),
    )


def tensor_parallel_shards(
    tokens,
    segment_ids,
    w_qkv,
    b_qv,
    w_out,
    b_out,
    w_up,
    b_up,
    w_down,
    b_down,
    ln_gain,
    ln_bias,
    out_grad,
):
    resid = tokens.astype(jnp.float32)
    qv_bias = b_qv.astype(jnp.float32)
    up_bias = b_up.astype(jnp.float32)
    local_rows = tokens.shape[0]
    normed, first_back = jax.vjp(norm_rows, resid, ln_gain[0], ln_bias[0])
    lowered = normed.astype(jnp.bfloat16)
    joined, seg_all = (
        lax.all_gather(lowered, "mp", axis=0, tiled=True),
        lax.all_gather(segment_ids, "mp", axis=0, tiled=True),
    )
    query = (jnp.dot(joined, w_qkv[0], preferred_element_type=jnp.float32) + qv_bias[0]).astype(
        jnp.bfloat16
    )
    keys = jnp.dot(joined, w_qkv[1], preferred_element_type=jnp.float32).astype(jnp.bfloat16)
    values = (jnp.dot(joined, w_qkv[2], preferred_element_type=jnp.float32) + qv_bias[1]).astype(
        jnp.bfloat16
    )
    query, keys, values = (query, keys, values)
    attended, totals = attention_forward(query, keys, values, seg_all)
    attn_sum = lax.psum_scatter(
        jnp.dot(attended, w_out, preferred_element_type=jnp.float32).astype(jnp.bfloat16),
        "mp",
        scatter_dimension=0,
        tiled=True,
    ).astype(jnp.float32)
    mixed = resid + attn_sum + b_out.astype(jnp.float32)
    normed2, second_back = jax.vjp(norm_rows, mixed, ln_gain[1], ln_bias[1])
    lowered2 = normed2.astype(jnp.bfloat16)
    joined2 = lax.all_gather(lowered2, "mp", axis=0, tiled=True)
    pre_act = jnp.dot(joined2, w_up, preferred_element_type=jnp.float32) + up_bias
    pre_act, activ = (pre_act, jax.nn.gelu(pre_act, approximate=False).astype(jnp.bfloat16))
    block_out = (
        mixed
        + lax.psum_scatter(
            jnp.dot(activ, w_down, preferred_element_type=jnp.float32).astype(jnp.bfloat16),
            "mp",
            scatter_dimension=0,
            tiled=True,
        ).astype(jnp.float32)
        + b_down.astype(jnp.float32)
    ).astype(jnp.bfloat16)
    grad_y = out_grad.astype(jnp.float32)
    grad_z = lax.all_gather(out_grad, "mp", axis=0, tiled=True)
    grad_down = jnp.einsum("tf,td->fd", activ, grad_z, preferred_element_type=jnp.float32)
    grad_bdown = jnp.sum(grad_z, axis=0, dtype=jnp.float32)
    grad_act = jnp.einsum("td,fd->tf", grad_z, w_down, preferred_element_type=jnp.float32)
    gelu_back = jax.vjp(lambda value: jax.nn.gelu(value, approximate=False), pre_act)[1]
    grad_pre = gelu_back(grad_act)[0].astype(jnp.bfloat16)
    grad_up = jnp.einsum("td,tf->df", joined2, grad_pre, preferred_element_type=jnp.float32)
    grad_bup = jnp.sum(grad_pre, axis=0, dtype=jnp.float32)
    grad_n2 = lax.psum_scatter(
        jnp.einsum("tf,df->td", grad_pre, w_up, preferred_element_type=jnp.float32).astype(
            jnp.bfloat16
        ),
        "mp",
        scatter_dimension=0,
        tiled=True,
    ).astype(jnp.float32)
    grad_h, grad_g2, grad_s2 = second_back(grad_n2)
    grad_h = grad_h + grad_y
    grad_branch = lax.all_gather(grad_h.astype(jnp.bfloat16), "mp", axis=0, tiled=True)
    grad_wout = jnp.einsum("tc,td->cd", attended, grad_branch, preferred_element_type=jnp.float32)
    grad_bout = jnp.sum(grad_branch, axis=0, dtype=jnp.float32)
    grad_att = jnp.einsum(
        "td,cd->tc", grad_branch, w_out, preferred_element_type=jnp.float32
    ).astype(jnp.bfloat16)
    grad_q, grad_k, grad_v = attention_backward(query, keys, values, seg_all, totals, grad_att)
    grad_qkv = jnp.stack(
        [
            jnp.einsum("td,tc->dc", joined, piece, preferred_element_type=jnp.float32)
            for piece in (grad_q, grad_k, grad_v)
        ]
    )
    grad_bqv = jnp.stack(
        [jnp.sum(grad_q, axis=0, dtype=jnp.float32), jnp.sum(grad_v, axis=0, dtype=jnp.float32)]
    )
    summed = jnp.zeros((local_rows * lax.axis_size("mp"), w_qkv.shape[1]), jnp.float32)
    for index, piece in enumerate((grad_q, grad_k, grad_v)):
        summed = summed + jnp.einsum(
            "tc,dc->td", piece, w_qkv[index], preferred_element_type=jnp.float32
        )
    grad_n1 = lax.psum_scatter(
        summed.astype(jnp.bfloat16), "mp", scatter_dimension=0, tiled=True
    ).astype(jnp.float32)
    grad_x, grad_g1, grad_s1 = first_back(grad_n1)
    grad_in = grad_x + grad_h
    weight_totals = (
        lax.psum(grad_qkv.astype(jnp.bfloat16), "dp").astype(jnp.float32),
        lax.psum(grad_bqv.astype(jnp.bfloat16), "dp").astype(jnp.float32),
        lax.psum(grad_wout.astype(jnp.bfloat16), "dp").astype(jnp.float32),
        lax.psum(grad_bout.astype(jnp.bfloat16), "dp").astype(jnp.float32),
        lax.psum(grad_up.astype(jnp.bfloat16), "dp").astype(jnp.float32),
        lax.psum(grad_bup.astype(jnp.bfloat16), "dp").astype(jnp.float32),
        lax.psum(grad_down.astype(jnp.bfloat16), "dp").astype(jnp.float32),
        lax.psum(grad_bdown.astype(jnp.bfloat16), "dp").astype(jnp.float32),
    )
    norm_totals = lax.psum(
        (jnp.stack([grad_g1, grad_g2]), jnp.stack([grad_s1, grad_s2])), ("dp", "mp")
    )
    return (block_out, grad_in) + tuple(weight_totals) + tuple(norm_totals)


def row_per_chip(mesh):
    return mesh.shape["mp"] == 4 and mesh.shape["dp"] == 8


def swap(value, axis, size, bit):
    return lax.ppermute(value, axis, [(i, i ^ bit) for i in range(size)])


def core(value):
    return swap(value, "mp", 4, 1)


def cross(value):
    return swap(value, "mp", 4, 2)


def along(value, bit):
    return swap(value, "dp", 8, bit)


def after(value, *others):
    return lax.optimization_barrier((value,) + others)[0]


def take(value, at):
    return lax.dynamic_index_in_dim(value, at, 0, keepdims=False)


def place(whole, piece, at):
    return lax.dynamic_update_index_in_dim(whole, piece, at, 0)


def gather_spread(weight, ready):
    me = lax.axis_index("dp") & 3
    quarters = weight.reshape(4, weight.shape[0] // 4, weight.shape[1])
    mine = take(quarters, me)
    if ready is not None:
        mine = after(mine, ready)
    mine = cross(mine)
    whole = jnp.zeros_like(quarters)
    whole = place(whole, mine, me)
    for bit in (1, 2, 3):
        whole = place(whole, along(mine, bit), me ^ bit)
    return whole.reshape(weight.shape)


def reduce_all(own, other):
    rows, cols = own.shape
    me = lax.axis_index("dp")
    side, deep = me & 1, me >> 1
    eighth = rows // 8
    own = own.reshape(2, 4, eighth, cols)
    got = cross(other).reshape(2, 4, eighth, cols)
    away = (take(own, 1 - side).astype(f32) + take(got, 1 - side).astype(f32)).astype(bf16)
    near = along(away, 1)

    def part(step):
        at = deep ^ step
        total = take(take(own, side), at).astype(f32) + take(take(got, side), at).astype(f32)
        return total + take(near, at).astype(f32)

    arrived = [along(part(step).astype(bf16), 2 * step) for step in (1, 2, 3)]
    total = part(0)
    for piece in arrived:
        total = total + piece.astype(f32)
    mine = lax.optimization_barrier(total.astype(bf16))
    level = [mine] + [along(mine, 2 * step) for step in (1, 2, 3)]
    return level, [along(piece, 1) for piece in level]


def settle(whole, index, pieces):
    me = lax.axis_index("dp")
    side, deep = me & 1, me >> 1
    zero = jnp.int32(0)
    for flip in (0, 1):
        for step in range(4):
            piece = pieces[flip][step].astype(f32)[None, None, None]
            whole = lax.dynamic_update_slice(
                whole, piece, (jnp.int32(index), side ^ flip, deep ^ step, zero, zero)
            )
    return whole


def reduce_weight(pairs):
    rows, cols = pairs[0][0].shape
    whole = jnp.zeros((len(pairs), 2, 4, rows // 8, cols), f32)
    for index, (own, other) in enumerate(pairs):
        whole = settle(whole, index, reduce_all(own, other))
    return whole.reshape(len(pairs) * rows, cols)


def row_per_chip_shards(
    tokens,
    segment_ids,
    w_qkv,
    b_qv,
    w_out,
    b_out,
    w_up,
    b_up,
    w_down,
    b_down,
    ln_gain,
    ln_bias,
    out_grad,
):
    half = tokens.shape[0]
    side = lax.axis_index("mp") & 1
    resid = tokens.astype(f32)
    normed, first_back = jax.vjp(norm_rows, resid, ln_gain[0], ln_bias[0])
    a1_own = normed.astype(bf16)

    qkv_other = cross(w_qkv)
    small = cross(jnp.concatenate([b_qv.reshape(-1), b_up]))
    out_other = cross(after(w_out, qkv_other))
    up_other = gather_spread(w_up, qkv_other)
    down_other = gather_spread(w_down, out_other)
    width = b_qv.shape[1]
    qv_biases = (b_qv.astype(f32), small[: 2 * width].reshape(2, width).astype(f32))
    up_biases = (b_up, small[2 * width :])
    qkvs, outs = (w_qkv, qkv_other), (w_out, out_other)
    ups, downs = (w_up, up_other), (w_down, down_other)

    a1 = jnp.concatenate([a1_own, core(a1_own)])
    dz = jnp.concatenate([out_grad, core(out_grad)])
    seg_other = core(segment_ids)
    seg = jnp.concatenate([segment_ids, seg_other])
    start = jnp.sum((seg[None, :] < seg[:, None]).astype(jnp.int32), axis=1)[None]
    ordered = jnp.where(side == 0, seg, jnp.concatenate([seg_other, segment_ids]))
    blocks = ordered.reshape(LEN // BLK, BLK)
    low = jnp.sum((blocks[None, :, -1] < blocks[:, None, 0]).astype(jnp.int32), axis=1)
    info = jnp.concatenate([(side * (LEN // BLK // 2))[None].astype(jnp.int32), low])

    saved = []
    for weight, bias in zip(qkvs, qv_biases):
        query = (nn(a1, weight[0]) + bias[0]).astype(bf16) * jnp.bfloat16(HD**-0.5)
        keys = nn(a1, weight[1]).astype(bf16)
        values = (nn(a1, weight[2]) + bias[1]).astype(bf16)
        out, lse = attn_fwd(info, query, keys, values, start)
        saved.append((query, keys, values, out, lse))
    outs_a = [entry[3] for entry in saved]

    def pair_sum(lefts, rights, product):
        there = sum(product(left[half:], right) for left, right in zip(lefts, rights))
        came = core(there.astype(bf16))
        here = sum(product(left[:half], right) for left, right in zip(lefts, rights))
        return here + came.astype(f32)

    mixed = resid + pair_sum(outs_a, outs, nn) + b_out.astype(f32)
    normed2, second_back = jax.vjp(norm_rows, mixed, ln_gain[1], ln_bias[1])
    a2_own = normed2.astype(bf16)
    a2 = jnp.concatenate([a2_own, core(a2_own)])
    acts = [up_gelu(a2, weight, bias) for weight, bias in zip(ups, up_biases)]
    activs = [act[0] for act in acts]
    grads_down = [tn(activ, dz).astype(bf16) for activ in activs]
    dus = [(nt(dz, down) * act[1].astype(f32)).astype(bf16) for act, down in zip(acts, downs)]
    grad_y = out_grad.astype(f32)
    grad_n2 = pair_sum(dus, ups, nt)
    grad_h, grad_g2, grad_s2 = second_back(grad_n2)
    grad_h = grad_h + grad_y
    dattn_own = grad_h.astype(bf16)
    dattn = jnp.concatenate([dattn_own, core(dattn_own)])
    grads_up = [tn(a2, du).astype(bf16) for du in dus]
    block_out = (mixed + pair_sum(activs, downs, nn) + b_down.astype(f32)).astype(bf16)

    grads_out, grads_qkv, sums, terms = [], [], [], []
    for (query, keys, values, out, lse), weight, w_o, du in zip(saved, qkvs, outs, dus):
        cot = nt(dattn, w_o).astype(bf16)
        grads_out.append(tn(out, dattn).astype(bf16))
        trio = attn_bwd(info, query, keys, values, start, out, lse, cot)
        grads_qkv.append([tn(a1, piece).astype(bf16) for piece in trio])
        terms.append(trio)
        sums.append(
            jnp.concatenate(
                [jnp.sum(piece, axis=0, dtype=f32) for piece in (trio[0], trio[2], du)]
            )
        )
    grad_n1 = pair_sum(
        [piece for trio in terms for piece in trio],
        [weight[i] for weight in qkvs for i in range(3)],
        nt,
    )
    grad_x, grad_g1, grad_s1 = first_back(grad_n1)
    grad_in = grad_x + grad_h

    h = grads_down[0].shape[0] // 2
    grad_down = reduce_weight([tuple(g[i * h : i * h + h] for g in grads_down) for i in range(2)])
    grad_up = reduce_weight([tuple(g[i * h : i * h + h] for g in grads_up) for i in range(2)])
    grad_wout = reduce_weight([tuple(grads_out)])
    grad_qkv = reduce_weight([(grads_qkv[0][i], grads_qkv[1][i]) for i in range(3)])
    grad_qkv = grad_qkv.reshape(w_qkv.shape)

    common = jnp.concatenate(
        [
            jnp.sum(dattn_own, axis=0, dtype=f32),
            jnp.sum(out_grad, axis=0, dtype=f32),
            grad_g1,
            grad_g2,
            grad_s1,
            grad_s2,
        ]
    )
    common = common + core(common)
    vector = jnp.concatenate([sums[0], common]) + cross(jnp.concatenate([sums[1], common]))
    for bit in (1, 2, 4):
        vector = vector + along(vector, bit)
    wide, units = ln_gain.shape[1], b_up.shape[0]
    ends = [2 * width, units, wide, wide, 2 * wide, 2 * wide]
    cuts = [sum(ends[:i]) for i in range(len(ends) + 1)]
    grad_bqv, grad_bup, grad_bout, grad_bdown, grad_gain, grad_shift = [
        vector[low:high] for low, high in zip(cuts[:-1], cuts[1:])
    ]
    return (
        block_out,
        grad_in,
        grad_qkv,
        grad_bqv.reshape(b_qv.shape),
        grad_wout,
        grad_bout,
        grad_up,
        grad_bup,
        grad_down,
        grad_bdown,
        grad_gain.reshape(ln_gain.shape),
        grad_shift.reshape(ln_bias.shape),
    )


def solution(mesh):
    in_specs = (
        P(("dp", "mp"), None),
        P(("dp", "mp")),
        P(None, None, "mp"),
        P(None, "mp"),
        P("mp", None),
        P(),
        P(None, "mp"),
        P("mp"),
        P("mp", None),
        P(),
        P(),
        P(),
        P(("dp", "mp"), None),
    )
    out_specs = (
        P(("dp", "mp"), None),
        P(("dp", "mp"), None),
        P(None, None, "mp"),
        P(None, "mp"),
        P("mp", None),
        P(),
        P(None, "mp"),
        P("mp"),
        P("mp", None),
        P(),
        P(),
        P(),
    )
    body = row_per_chip_shards if row_per_chip(mesh) else tensor_parallel_shards
    return jax.shard_map(body, mesh=mesh, in_specs=in_specs, out_specs=out_specs, check_vma=False)
```

```python
import jax
import jax.numpy as jnp
from jax import lax
from jax.experimental import pallas as pl
from jax.experimental.pallas import tpu as pltpu
from jax.sharding import Mesh
from jax.sharding import PartitionSpec as P

HD = 64
LEN = 1024
QBLK = 512
EPS = 1e-05
BLK = 256

NEG = -1e30
GRANT = 18 << 20
f32 = jnp.float32
bf16 = jnp.bfloat16


def nt(left, right):
    return lax.dot_general(left, right, (((1,), (1,)), ((), ())), preferred_element_type=f32)


def nn(left, right):
    return lax.dot_general(left, right, (((1,), (0,)), ((), ())), preferred_element_type=f32)


def tn(left, right):
    return lax.dot_general(left, right, (((0,), (0,)), ((), ())), preferred_element_type=f32)


def attn_bias(block, j, first):
    q_pos = block * BLK + lax.broadcasted_iota(jnp.int32, (1, BLK), 1)
    k_pos = j * BLK + lax.broadcasted_iota(jnp.int32, (BLK, BLK), 0)
    return jnp.where((k_pos >= first) & (k_pos <= q_pos), 0.0, NEG)


def head_rows(refs, scratch, heads):
    lane = lax.broadcasted_iota(jnp.int32, (LEN, 2 * HD), 1)
    for ref, out in zip(refs, scratch):
        for h in range(heads):
            pair = ref[:, (h // 2) * 2 * HD : (h // 2 + 1) * 2 * HD]
            out[h] = jnp.where((lane < HD) == (h % 2 == 0), pair, jnp.zeros_like(pair))


def attn_fwd_body(info, q_ref, k_ref, v_ref, st_ref, o_ref, lse_ref, k_heads, v_turned):
    block = pl.program_id(0)
    heads = q_ref.shape[1] // HD
    first = st_ref[...]

    @pl.when(block == 0)
    def _():
        head_rows([k_ref], [k_heads], heads)
        for pair in range(heads // 2):
            turned = v_ref[:, pair * 2 * HD : (pair + 1) * 2 * HD].T
            for h in (0, 1):
                v_turned[2 * pair + h, :HD] = turned[h * HD : (h + 1) * HD]
                v_turned[2 * pair + h, HD:] = jnp.ones((16, LEN), bf16)

    def step(at, carry):
        j = block - at
        row = pl.multiple_of((j ^ info[0]) * BLK, BLK)
        bias = attn_bias(block, j, first)
        out = []
        for h in range(heads):
            top, acc = carry[h]
            query = q_ref[:, (h // 2) * 2 * HD : (h // 2 + 1) * 2 * HD]
            s = nt(k_heads[h, pl.ds(row, BLK), :], query) + bias
            new = jnp.maximum(top, jnp.max(s, axis=0, keepdims=True))
            p = jnp.exp(s - new).astype(bf16)
            acc = acc * jnp.exp(top - new) + nn(v_turned[h, :, pl.ds(row, BLK)], p)
            out.append((new, acc))
        return tuple(out)

    init = tuple((jnp.full((1, BLK), NEG, f32), jnp.zeros((HD + 16, BLK), f32)) for _ in range(heads))
    done = lax.fori_loop(0, block + 1 - info[1 + block], step, init)
    for pair in range(heads // 2):
        both = [acc[:HD] / acc[HD : HD + 1] for _, acc in done[2 * pair : 2 * pair + 2]]
        o_ref[:, pair * 2 * HD : (pair + 1) * 2 * HD] = jnp.concatenate(both, axis=0).T.astype(bf16)
    for h in range(heads):
        top, acc = done[h]
        lse_ref[h : h + 1, :] = top + jnp.log(acc[HD : HD + 1])


def attn_bwd_body(info, q_ref, k_ref, v_ref, st_ref, o_ref, lse_ref, do_ref, d_ref, k_heads, v_heads, dk_acc, dv_acc):
    block = pl.program_id(0)
    heads = q_ref.shape[1] // HD
    first = st_ref[...]
    lane = lax.broadcasted_iota(jnp.int32, (BLK, 2 * HD), 1)

    @pl.when(block == 0)
    def _():
        head_rows([k_ref, v_ref], [k_heads, v_heads], heads)
        dk_acc[...] = jnp.zeros_like(dk_acc)
        dv_acc[...] = jnp.zeros_like(dv_acc)

    deltas = []
    for pair in range(heads // 2):
        cols = slice(pair * 2 * HD, (pair + 1) * 2 * HD)
        turned = (do_ref[:, cols].astype(f32) * o_ref[:, cols].astype(f32)).T
        for h in (0, 1):
            deltas.append(jnp.sum(turned[h * HD : (h + 1) * HD], axis=0, keepdims=True))

    def step(j, dqs):
        row = pl.multiple_of((j ^ info[0]) * BLK, BLK)
        bias = attn_bias(block, j, first)
        out = list(dqs)
        for pair in range(heads // 2):
            cols = slice(pair * 2 * HD, (pair + 1) * 2 * HD)
            query, cot = q_ref[:, cols], do_ref[:, cols]
            dk = dk_acc[pl.ds(row, BLK), cols]
            dv = dv_acc[pl.ds(row, BLK), cols]
            for h in (2 * pair, 2 * pair + 1):
                mask = (lane < HD) == (h % 2 == 0)
                keys = k_heads[h, pl.ds(row, BLK), :]
                p = jnp.exp(nt(keys, query) + (bias - lse_ref[h : h + 1, :]))
                dp = nt(v_heads[h, pl.ds(row, BLK), :], cot)
                ds = (p * (dp - deltas[h])).astype(bf16)
                dv = dv + nn(p.astype(bf16), jnp.where(mask, cot, jnp.zeros_like(cot)))
                dk = dk + nn(ds, jnp.where(mask, query, jnp.zeros_like(query)))
                out[pair] = out[pair] + tn(ds, keys)
            dk_acc[pl.ds(row, BLK), cols] = dk
            dv_acc[pl.ds(row, BLK), cols] = dv
        return tuple(out)

    init = tuple(jnp.zeros((BLK, 2 * HD), f32) for _ in range(heads // 2))
    dqs = lax.fori_loop(info[1 + block], block + 1, step, init)
    here = pl.multiple_of((block ^ info[0]) * BLK, BLK)
    for pair in range(heads // 2):
        cols = slice(pair * 2 * HD, (pair + 1) * 2 * HD)
        d_ref[0, pl.ds(here, BLK), cols] = (dqs[pair] * HD**-0.5).astype(bf16)

    @pl.when(block == pl.num_programs(0) - 1)
    def _():
        d_ref[1] = dk_acc[...].astype(bf16)
        d_ref[2] = dv_acc[...].astype(bf16)


def attn_specs(width):
    small = pl.BlockSpec((BLK, width), lambda i, info: (i ^ info[0], 0))
    whole = pl.BlockSpec((LEN, width), lambda i, info: (0, 0))
    start = pl.BlockSpec((1, BLK), lambda i, info: (0, i ^ info[0]))
    lse = pl.BlockSpec((width // HD, BLK), lambda i, info: (0, i ^ info[0]))
    return small, whole, start, lse


def attn_cost(width, products):
    blocks = 10 * BLK * BLK * (width // HD)
    return pl.CostEstimate(flops=2 * products * blocks * 256, bytes_accessed=4 << 20, transcendentals=blocks)


def attn_fwd(info, query, keys, values, start):
    width = query.shape[1]
    heads = width // HD
    small, whole, first, lse = attn_specs(width)
    return pl.pallas_call(
        attn_fwd_body,
        out_shape=(jax.ShapeDtypeStruct(query.shape, bf16), jax.ShapeDtypeStruct((heads, LEN), f32)),
        grid_spec=pltpu.PrefetchScalarGridSpec(
            num_scalar_prefetch=1,
            grid=(LEN // BLK,),
            in_specs=[small, whole, whole, first],
            out_specs=[small, lse],
            scratch_shapes=[pltpu.VMEM((heads, LEN, 2 * HD), bf16), pltpu.VMEM((heads, HD + 16, LEN), bf16)],
        ),
        cost_estimate=attn_cost(width, 2),
        compiler_params=pltpu.CompilerParams(vmem_limit_bytes=GRANT),
        name="attn_fwd",
    )(info, query, keys, values, start)


def attn_bwd(info, query, keys, values, start, out, lse, cot):
    width = query.shape[1]
    heads = width // HD
    small, whole, first, lse_spec = attn_specs(width)
    return pl.pallas_call(
        attn_bwd_body,
        out_shape=jax.ShapeDtypeStruct((3,) + query.shape, bf16),
        grid_spec=pltpu.PrefetchScalarGridSpec(
            num_scalar_prefetch=1,
            grid=(LEN // BLK,),
            in_specs=[small, whole, whole, first, small, lse_spec, small],
            out_specs=pl.BlockSpec((3, LEN, width), lambda i, info: (0, 0, 0)),
            scratch_shapes=[
                pltpu.VMEM((heads, LEN, 2 * HD), bf16),
                pltpu.VMEM((heads, LEN, 2 * HD), bf16),
                pltpu.VMEM((LEN, width), f32),
                pltpu.VMEM((LEN, width), f32),
            ],
        ),
        cost_estimate=attn_cost(width, 5),
        compiler_params=pltpu.CompilerParams(vmem_limit_bytes=GRANT),
        name="attn_bwd",
    )(info, query, keys, values, start, out, lse, cot)


def up_body(a_ref, w_ref, b_ref, g_ref, s_ref):
    rows = a_ref[...]
    for part in range(w_ref.shape[1] // 256):
        cols = slice(part * 256, part * 256 + 256)
        u = nn(rows, w_ref[:, cols]) + b_ref[:, cols].astype(f32)
        size = jnp.abs(u)
        t = 1.0 / (1.0 + 0.3275911 * 0.7071067811865476 * size)
        poly = t * (0.5 * 0.254829592 + t * (0.5 * -0.284496736 + t * (0.5 * 1.421413741 + t * (0.5 * -1.453152027 + t * (0.5 * 1.061405429)))))
        bell = jnp.exp(-0.5 * u * u)
        tail = poly * bell
        cdf = jnp.where(u >= 0, 1.0 - tail, tail)
        g_ref[:, cols] = (u * cdf).astype(bf16)
        s_ref[:, cols] = (cdf + u * bell * 0.3989422804014327).astype(bf16)


def up_gelu(rows, weight, bias):
    m, k = rows.shape
    n = weight.shape[1]
    bm = 256
    shape = jax.ShapeDtypeStruct((m, n), bf16)
    tile = pl.BlockSpec((bm, n), lambda i: (i, 0))
    return pl.pallas_call(
        up_body,
        out_shape=(shape, shape),
        grid=(m // bm,),
        in_specs=[pl.BlockSpec((bm, k), lambda i: (i, 0)), pl.BlockSpec((k, n), lambda i: (0, 0)), pl.BlockSpec((1, n), lambda i: (0, 0))],
        out_specs=(tile, tile),
        cost_estimate=pl.CostEstimate(flops=2 * m * n * k * 2, bytes_accessed=8 << 20, transcendentals=m * n),
        compiler_params=pltpu.CompilerParams(vmem_limit_bytes=GRANT),
        name="up_gelu",
    )(rows, weight, bias.reshape(1, n))


def const_spec(shape):
    return pl.BlockSpec(shape, lambda i: (0,) * len(shape))


def row_spec(rows, cols):
    return pl.BlockSpec((rows, cols), lambda i: (i, 0))


def project_body(a_ref, w_ref, b_ref, q_ref, k_ref, v_ref):
    rows = a_ref[...]
    q_ref[...] = (nn(rows, w_ref[0]) + b_ref[0:1].astype(f32)).astype(bf16) * jnp.bfloat16(HD**-0.5)
    k_ref[...] = nn(rows, w_ref[1]).astype(bf16)
    v_ref[...] = (nn(rows, w_ref[2]) + b_ref[1:2].astype(f32)).astype(bf16)


def project(rows, weight, bias):
    m, k = rows.shape
    n = weight.shape[2]
    tile = 256
    shape = jax.ShapeDtypeStruct((m, n), bf16)
    return pl.pallas_call(
        project_body,
        out_shape=(shape, shape, shape),
        grid=(m // tile,),
        in_specs=[row_spec(tile, k), const_spec(weight.shape), const_spec(bias.shape)],
        out_specs=[row_spec(tile, n)] * 3,
        cost_estimate=pl.CostEstimate(flops=6 * m * n * k, bytes_accessed=6 << 20, transcendentals=0),
        compiler_params=pltpu.CompilerParams(vmem_limit_bytes=GRANT),
        name="project",
    )(rows, weight, bias)


def sum_dots(lefts, rights, product):
    stacked = lefts[0].ndim == 3
    m, k = lefts[0].shape[-2:]
    n = rights[0].shape[-1] if product is nn else rights[0].shape[-2]
    terms = len(lefts)
    tile = 256
    steps = m // tile // 2

    def body(*refs):
        total = None
        for left, right in zip(refs[:terms], refs[terms : 2 * terms]):
            for at in range(left.shape[0] if stacked else 1):
                term = product(left[at], right[at]) if stacked else product(left[...], right[...])
                total = term if total is None else total + term
        here, there = refs[2 * terms :]

        @pl.when(pl.program_id(0) < steps)
        def _():
            there[...] = total.astype(bf16)

        @pl.when(pl.program_id(0) >= steps)
        def _():
            here[...] = total

    def turn(i):
        return jnp.where(i < steps, i + steps, i - steps)

    if stacked:
        left_spec = pl.BlockSpec((lefts[0].shape[0], tile, k), lambda i: (0, turn(i), 0))
    else:
        left_spec = pl.BlockSpec((tile, k), lambda i: (turn(i), 0))
    flops = 2 * m * n * k * terms * (lefts[0].shape[0] if stacked else 1)
    return pl.pallas_call(
        body,
        out_shape=(jax.ShapeDtypeStruct((m // 2, n), f32), jax.ShapeDtypeStruct((m // 2, n), bf16)),
        grid=(2 * steps,),
        in_specs=[left_spec] * terms + [const_spec(r.shape) for r in rights],
        out_specs=[
            pl.BlockSpec((tile, n), lambda i: (jnp.maximum(i - steps, 0), 0)),
            pl.BlockSpec((tile, n), lambda i: (jnp.minimum(i, steps - 1), 0)),
        ],
        cost_estimate=pl.CostEstimate(flops=flops, bytes_accessed=8 << 20, transcendentals=0),
        compiler_params=pltpu.CompilerParams(vmem_limit_bytes=GRANT),
        name="sum_dots",
    )(*lefts, *rights)


def center_rows(rows):
    center = rows - jnp.mean(rows, axis=-1, keepdims=True)
    scale = lax.rsqrt(jnp.mean(center * center, axis=-1, keepdims=True) + EPS)
    return center * scale, scale


def first_norm_body(x_ref, g_ref, gain_ref, shift_ref, a_ref, sum_ref):
    normal, _ = center_rows(x_ref[...].astype(f32))
    a_ref[...] = (normal * gain_ref[...] + shift_ref[...]).astype(bf16)

    @pl.when(pl.program_id(0) == 0)
    def _():
        sum_ref[...] = jnp.zeros_like(sum_ref)

    sum_ref[...] += jnp.sum(g_ref[...].astype(f32), axis=0, keepdims=True)


def first_norm(tokens, cotangent, gain, shift):
    m, d = tokens.shape
    tile = 128
    return pl.pallas_call(
        first_norm_body,
        out_shape=(jax.ShapeDtypeStruct((m, d), bf16), jax.ShapeDtypeStruct((1, d), f32)),
        grid=(m // tile,),
        in_specs=[row_spec(tile, d), row_spec(tile, d), const_spec((1, d)), const_spec((1, d))],
        out_specs=[row_spec(tile, d), const_spec((1, d))],
        cost_estimate=pl.CostEstimate(flops=10 * m * d, bytes_accessed=6 * m * d, transcendentals=0),
        compiler_params=pltpu.CompilerParams(vmem_limit_bytes=GRANT),
        name="first_norm",
    )(tokens, cotangent, gain, shift)


def second_norm_body(x_ref, here_ref, came_ref, b_ref, gain_ref, shift_ref, h_ref, a_ref):
    mixed = x_ref[...].astype(f32) + (here_ref[...] + came_ref[...].astype(f32)) + b_ref[...].astype(f32)
    h_ref[...] = mixed
    normal, _ = center_rows(mixed)
    a_ref[...] = (normal * gain_ref[...] + shift_ref[...]).astype(bf16)


def second_norm(tokens, here, came, bias, gain, shift):
    m, d = tokens.shape
    tile = 128
    return pl.pallas_call(
        second_norm_body,
        out_shape=(jax.ShapeDtypeStruct((m, d), f32), jax.ShapeDtypeStruct((m, d), bf16)),
        grid=(m // tile,),
        in_specs=[row_spec(tile, d)] * 3 + [const_spec((1, d))] * 3,
        out_specs=[row_spec(tile, d)] * 2,
        cost_estimate=pl.CostEstimate(flops=12 * m * d, bytes_accessed=14 * m * d, transcendentals=0),
        compiler_params=pltpu.CompilerParams(vmem_limit_bytes=GRANT),
        name="second_norm",
    )(tokens, here, came, bias, gain, shift)


def norm_back_body(v_ref, here_ref, came_ref, gain_ref, res_ref, out_ref, low_ref, sums_ref):
    normal, scale = center_rows(v_ref[...].astype(f32))
    grad = here_ref[...] + came_ref[...].astype(f32)
    scaled = grad * gain_ref[...]
    inner = jnp.mean(scaled * normal, axis=-1, keepdims=True)
    back = scale * (scaled - jnp.mean(scaled, axis=-1, keepdims=True) - normal * inner)
    back = back + res_ref[...].astype(f32)
    low = back.astype(bf16)
    out_ref[...] = back
    low_ref[...] = low

    @pl.when(pl.program_id(0) == 0)
    def _():
        sums_ref[...] = jnp.zeros_like(sums_ref)

    sums_ref[0:1] += jnp.sum(grad * normal, axis=0, keepdims=True)
    sums_ref[1:2] += jnp.sum(grad, axis=0, keepdims=True)
    sums_ref[2:3] += jnp.sum(low.astype(f32), axis=0, keepdims=True)


def norm_back(values, here, came, gain, residual):
    m, d = values.shape
    tile = 128
    return pl.pallas_call(
        norm_back_body,
        out_shape=(
            jax.ShapeDtypeStruct((m, d), f32),
            jax.ShapeDtypeStruct((m, d), bf16),
            jax.ShapeDtypeStruct((8, d), f32),
        ),
        grid=(m // tile,),
        in_specs=[row_spec(tile, d)] * 3 + [const_spec((1, d)), row_spec(tile, d)],
        out_specs=[row_spec(tile, d)] * 2 + [const_spec((8, d))],
        cost_estimate=pl.CostEstimate(flops=30 * m * d, bytes_accessed=20 * m * d, transcendentals=0),
        compiler_params=pltpu.CompilerParams(vmem_limit_bytes=GRANT),
        name="norm_back",
    )(values, here, came, gain, residual)


def back_act_body(z_ref, w_ref, s_ref, du_ref, sum_ref):
    du = (nt(z_ref[...], w_ref[...]) * s_ref[...].astype(f32)).astype(bf16)
    du_ref[...] = du

    @pl.when(pl.program_id(0) == 0)
    def _():
        sum_ref[...] = jnp.zeros_like(sum_ref)

    sum_ref[...] += jnp.sum(du.astype(f32), axis=0, keepdims=True)


def back_act(cotangent, weight, slope):
    m, d = cotangent.shape
    n = weight.shape[0]
    tile = 256
    return pl.pallas_call(
        back_act_body,
        out_shape=(jax.ShapeDtypeStruct((m, n), bf16), jax.ShapeDtypeStruct((1, n), f32)),
        grid=(m // tile,),
        in_specs=[row_spec(tile, d), const_spec((n, d)), row_spec(tile, n)],
        out_specs=[row_spec(tile, n), const_spec((1, n))],
        cost_estimate=pl.CostEstimate(flops=2 * m * n * d, bytes_accessed=8 << 20, transcendentals=0),
        compiler_params=pltpu.CompilerParams(vmem_limit_bytes=GRANT),
        name="back_act",
    )(cotangent, weight, slope)


def frame_sums_body(a_ref, d_ref, o_ref, g_ref, dw_ref, do_ref, sums_ref, a_turned):
    at = pl.program_id(0)

    @pl.when(at == 0)
    def _():
        a_turned[...] = a_ref[...].T
        do_ref[...] = tn(o_ref[...], g_ref[...]).astype(bf16)

    piece = d_ref[0]
    dw_ref[0] = nn(a_turned[...], piece).astype(bf16)
    sums_ref[0] = jnp.sum(piece.astype(f32), axis=0, keepdims=True)


def frame_sums(rows, trio, out, cotangent):
    t, d = rows.shape
    n = trio.shape[2]
    return pl.pallas_call(
        frame_sums_body,
        out_shape=(
            jax.ShapeDtypeStruct((3, d, n), bf16),
            jax.ShapeDtypeStruct((n, d), bf16),
            jax.ShapeDtypeStruct((3, 1, n), f32),
        ),
        grid=(3,),
        in_specs=[
            const_spec((t, d)),
            pl.BlockSpec((1, t, n), lambda i: (i, 0, 0)),
            const_spec((t, n)),
            const_spec((t, d)),
        ],
        out_specs=[
            pl.BlockSpec((1, d, n), lambda i: (i, 0, 0)),
            const_spec((n, d)),
            pl.BlockSpec((1, 1, n), lambda i: (i, 0, 0)),
        ],
        scratch_shapes=[pltpu.VMEM((d, t), bf16)],
        cost_estimate=pl.CostEstimate(flops=8 * t * d * n, bytes_accessed=8 << 20, transcendentals=0),
        compiler_params=pltpu.CompilerParams(vmem_limit_bytes=GRANT),
        name="frame_sums",
    )(rows, trio, out, cotangent)


def norm_rows(values, gain, shift):
    center = values - jnp.mean(values, axis=-1, keepdims=True)
    spread = jnp.mean(center * center, axis=-1, keepdims=True)
    return center * lax.rsqrt(spread + EPS) * gain + shift


def split_heads(flat, rows):
    return flat.reshape(rows, LEN, flat.shape[1] // HD, HD)


def block_scores(query, keys, seg_q, seg_k, offset):
    scores = jnp.einsum(
        "rqhd,rkhd->rhqk", query, keys, preferred_element_type=jnp.float32
    ) * HD ** (-0.5)
    q_pos = offset + jnp.arange(query.shape[1], dtype=jnp.int32)
    k_pos = jnp.arange(keys.shape[1], dtype=jnp.int32)
    allowed = (seg_q[:, :, None] == seg_k[:, None, :]) & (
        k_pos[None, None, :] <= q_pos[None, :, None]
    )
    return jnp.where(allowed[:, None], scores, -1e30)


def attention_forward(query, keys, values, seg_all):
    rows = query.shape[0] // LEN
    q4 = split_heads(query, rows)
    k4 = split_heads(keys, rows)
    v4 = split_heads(values, rows)
    seg2 = seg_all.reshape(rows, LEN)
    outputs = []
    totals = []
    for block in range(LEN // QBLK):
        first = block * QBLK
        end = first + QBLK
        scores = block_scores(
            q4[:, first:end], k4[:, :end], seg2[:, first:end], seg2[:, :end], first
        )
        top = jnp.max(scores, axis=-1, keepdims=True)
        expd = jnp.exp(scores - top)
        summed = jnp.sum(expd, axis=-1, keepdims=True)
        weights = (expd / summed).astype(jnp.bfloat16)
        outputs.append(
            jnp.einsum("rhqk,rkhd->rqhd", weights, v4[:, :end], preferred_element_type=jnp.float32)
        )
        totals.append(top + jnp.log(summed))
    attended = jnp.concatenate(outputs, axis=1).reshape(query.shape).astype(jnp.bfloat16)
    return (attended, totals)


def attention_backward(query, keys, values, seg_all, totals, grad_att):
    rows = query.shape[0] // LEN
    q4 = split_heads(query, rows)
    k4 = split_heads(keys, rows)
    v4 = split_heads(values, rows)
    g4 = split_heads(grad_att, rows)
    seg2 = seg_all.reshape(rows, LEN)
    scale = HD ** (-0.5)
    grad_k = jnp.zeros(k4.shape, jnp.float32)
    grad_v = jnp.zeros(v4.shape, jnp.float32)
    grad_q_parts = []
    for block in range(LEN // QBLK):
        first = block * QBLK
        end = first + QBLK
        scores = block_scores(
            q4[:, first:end], k4[:, :end], seg2[:, first:end], seg2[:, :end], first
        )
        probs = jnp.exp(scores - totals[block])
        weights = probs.astype(jnp.bfloat16)
        grad_w = jnp.einsum(
            "rqhd,rkhd->rhqk", g4[:, first:end], v4[:, :end], preferred_element_type=jnp.float32
        )
        delta = jnp.sum(probs * grad_w, axis=-1, keepdims=True)
        grad_s = (probs * (grad_w - delta)).astype(jnp.bfloat16)
        grad_q_parts.append(
            jnp.einsum("rhqk,rkhd->rqhd", grad_s, k4[:, :end], preferred_element_type=jnp.float32)
            * scale
        )
        padding = ((0, 0), (0, LEN - end), (0, 0), (0, 0))
        grad_k = grad_k + jnp.pad(
            jnp.einsum(
                "rhqk,rqhd->rkhd", grad_s, q4[:, first:end], preferred_element_type=jnp.float32
            )
            * scale,
            padding,
        )
        grad_v = grad_v + jnp.pad(
            jnp.einsum(
                "rhqk,rqhd->rkhd", weights, g4[:, first:end], preferred_element_type=jnp.float32
            ),
            padding,
        )
    shape = query.shape
    grad_q = jnp.concatenate(grad_q_parts, axis=1).reshape(shape).astype(jnp.bfloat16)
    return (
        grad_q,
        grad_k.reshape(shape).astype(jnp.bfloat16),
        grad_v.reshape(shape).astype(jnp.bfloat16),
    )


def tensor_parallel_shards(
    tokens,
    segment_ids,
    w_qkv,
    b_qv,
    w_out,
    b_out,
    w_up,
    b_up,
    w_down,
    b_down,
    ln_gain,
    ln_bias,
    out_grad,
):
    resid = tokens.astype(jnp.float32)
    qv_bias = b_qv.astype(jnp.float32)
    up_bias = b_up.astype(jnp.float32)
    local_rows = tokens.shape[0]
    normed, first_back = jax.vjp(norm_rows, resid, ln_gain[0], ln_bias[0])
    lowered = normed.astype(jnp.bfloat16)
    joined, seg_all = (
        lax.all_gather(lowered, "mp", axis=0, tiled=True),
        lax.all_gather(segment_ids, "mp", axis=0, tiled=True),
    )
    query = (jnp.dot(joined, w_qkv[0], preferred_element_type=jnp.float32) + qv_bias[0]).astype(
        jnp.bfloat16
    )
    keys = jnp.dot(joined, w_qkv[1], preferred_element_type=jnp.float32).astype(jnp.bfloat16)
    values = (jnp.dot(joined, w_qkv[2], preferred_element_type=jnp.float32) + qv_bias[1]).astype(
        jnp.bfloat16
    )
    query, keys, values = (query, keys, values)
    attended, totals = attention_forward(query, keys, values, seg_all)
    attn_sum = lax.psum_scatter(
        jnp.dot(attended, w_out, preferred_element_type=jnp.float32).astype(jnp.bfloat16),
        "mp",
        scatter_dimension=0,
        tiled=True,
    ).astype(jnp.float32)
    mixed = resid + attn_sum + b_out.astype(jnp.float32)
    normed2, second_back = jax.vjp(norm_rows, mixed, ln_gain[1], ln_bias[1])
    lowered2 = normed2.astype(jnp.bfloat16)
    joined2 = lax.all_gather(lowered2, "mp", axis=0, tiled=True)
    pre_act = jnp.dot(joined2, w_up, preferred_element_type=jnp.float32) + up_bias
    pre_act, activ = (pre_act, jax.nn.gelu(pre_act, approximate=False).astype(jnp.bfloat16))
    block_out = (
        mixed
        + lax.psum_scatter(
            jnp.dot(activ, w_down, preferred_element_type=jnp.float32).astype(jnp.bfloat16),
            "mp",
            scatter_dimension=0,
            tiled=True,
        ).astype(jnp.float32)
        + b_down.astype(jnp.float32)
    ).astype(jnp.bfloat16)
    grad_y = out_grad.astype(jnp.float32)
    grad_z = lax.all_gather(out_grad, "mp", axis=0, tiled=True)
    grad_down = jnp.einsum("tf,td->fd", activ, grad_z, preferred_element_type=jnp.float32)
    grad_bdown = jnp.sum(grad_z, axis=0, dtype=jnp.float32)
    grad_act = jnp.einsum("td,fd->tf", grad_z, w_down, preferred_element_type=jnp.float32)
    gelu_back = jax.vjp(lambda value: jax.nn.gelu(value, approximate=False), pre_act)[1]
    grad_pre = gelu_back(grad_act)[0].astype(jnp.bfloat16)
    grad_up = jnp.einsum("td,tf->df", joined2, grad_pre, preferred_element_type=jnp.float32)
    grad_bup = jnp.sum(grad_pre, axis=0, dtype=jnp.float32)
    grad_n2 = lax.psum_scatter(
        jnp.einsum("tf,df->td", grad_pre, w_up, preferred_element_type=jnp.float32).astype(
            jnp.bfloat16
        ),
        "mp",
        scatter_dimension=0,
        tiled=True,
    ).astype(jnp.float32)
    grad_h, grad_g2, grad_s2 = second_back(grad_n2)
    grad_h = grad_h + grad_y
    grad_branch = lax.all_gather(grad_h.astype(jnp.bfloat16), "mp", axis=0, tiled=True)
    grad_wout = jnp.einsum("tc,td->cd", attended, grad_branch, preferred_element_type=jnp.float32)
    grad_bout = jnp.sum(grad_branch, axis=0, dtype=jnp.float32)
    grad_att = jnp.einsum(
        "td,cd->tc", grad_branch, w_out, preferred_element_type=jnp.float32
    ).astype(jnp.bfloat16)
    grad_q, grad_k, grad_v = attention_backward(query, keys, values, seg_all, totals, grad_att)
    grad_qkv = jnp.stack(
        [
            jnp.einsum("td,tc->dc", joined, piece, preferred_element_type=jnp.float32)
            for piece in (grad_q, grad_k, grad_v)
        ]
    )
    grad_bqv = jnp.stack(
        [jnp.sum(grad_q, axis=0, dtype=jnp.float32), jnp.sum(grad_v, axis=0, dtype=jnp.float32)]
    )
    summed = jnp.zeros((local_rows * lax.axis_size("mp"), w_qkv.shape[1]), jnp.float32)
    for index, piece in enumerate((grad_q, grad_k, grad_v)):
        summed = summed + jnp.einsum(
            "tc,dc->td", piece, w_qkv[index], preferred_element_type=jnp.float32
        )
    grad_n1 = lax.psum_scatter(
        summed.astype(jnp.bfloat16), "mp", scatter_dimension=0, tiled=True
    ).astype(jnp.float32)
    grad_x, grad_g1, grad_s1 = first_back(grad_n1)
    grad_in = grad_x + grad_h
    weight_totals = (
        lax.psum(grad_qkv.astype(jnp.bfloat16), "dp").astype(jnp.float32),
        lax.psum(grad_bqv.astype(jnp.bfloat16), "dp").astype(jnp.float32),
        lax.psum(grad_wout.astype(jnp.bfloat16), "dp").astype(jnp.float32),
        lax.psum(grad_bout.astype(jnp.bfloat16), "dp").astype(jnp.float32),
        lax.psum(grad_up.astype(jnp.bfloat16), "dp").astype(jnp.float32),
        lax.psum(grad_bup.astype(jnp.bfloat16), "dp").astype(jnp.float32),
        lax.psum(grad_down.astype(jnp.bfloat16), "dp").astype(jnp.float32),
        lax.psum(grad_bdown.astype(jnp.bfloat16), "dp").astype(jnp.float32),
    )
    norm_totals = lax.psum(
        (jnp.stack([grad_g1, grad_g2]), jnp.stack([grad_s1, grad_s2])), ("dp", "mp")
    )
    return (block_out, grad_in) + tuple(weight_totals) + tuple(norm_totals)


def row_per_chip(mesh):
    return mesh.shape["mp"] == 4 and mesh.shape["dp"] == 8


def swap(value, axis):
    return lax.ppermute(value, axis, [(0, 1), (1, 0)])


def core(value):
    return swap(value, "core")


def cross(value):
    return swap(value, "x")


def after(value, *others):
    return lax.optimization_barrier((value,) + others)[0]


def take(value, at):
    return lax.dynamic_index_in_dim(value, at, 0, keepdims=False)


def place(whole, piece, at):
    return lax.dynamic_update_index_in_dim(whole, piece, at, 0)


def gather_spread(weight, ready):
    me = lax.axis_index("y") + 2 * (lax.axis_index("z") & 1)
    shape = weight.shape
    quarters = weight.reshape(4, -1, shape[-1])
    mine = take(quarters, me)
    if ready is not None:
        mine = after(mine, ready)
    mine = cross(mine)
    whole = place(jnp.zeros_like(quarters), mine, me)
    whole = place(whole, swap(mine, "y"), me ^ 1)
    for bits in (2, 3):
        perm = [(i, i ^ bits) for i in range(8)]
        whole = place(whole, lax.ppermute(mine, ("z", "y"), perm), me ^ bits)
    return whole.reshape(shape), mine


def everyone(value, axis):
    return lax.all_to_all(jnp.broadcast_to(value, (4,) + value.shape), axis, 0, 0, tiled=False)


def spread_y(own, got):
    side = lax.axis_index("y")
    return swap((take(own, 1 - side).astype(f32) + take(got, 1 - side).astype(f32)).astype(bf16), "y")


def spread_z(own, got, near):
    side = lax.axis_index("y")
    total = take(own, side).astype(f32) + take(got, side).astype(f32) + near.astype(f32)
    return lax.all_to_all(total.astype(bf16), "z", 0, 0, tiled=False)


def gather_z(parts):
    mine = jnp.sum(parts.astype(f32), axis=0).astype(bf16)
    return everyone(mine, "z")


def by_owner(value):
    return value.reshape(2, 4, value.shape[0] // 8, value.shape[1])


def reduce_all(own, other):
    own = by_owner(own)
    got = by_owner(cross(other))
    near = spread_y(own, got)
    level = gather_z(spread_z(own, got, near))
    return level, swap(level, "y")


def settle(whole, index, pieces):
    side = lax.axis_index("y")
    zero = jnp.int32(0)
    for flip in (0, 1):
        piece = pieces[flip].astype(f32)[None, None]
        whole = lax.dynamic_update_slice(
            whole, piece, (jnp.int32(index), side ^ flip, zero, zero, zero)
        )
    return whole


def reduce_weight(pairs):
    rows, cols = pairs[0][0].shape
    whole = jnp.zeros((len(pairs), 2, 4, rows // 8, cols), f32)
    for index, (own, other) in enumerate(pairs):
        whole = settle(whole, index, reduce_all(own, other))
    return whole.reshape(len(pairs) * rows, cols)


def row_per_chip_shards(
    tokens,
    segment_ids,
    w_qkv,
    b_qv,
    w_out,
    b_out,
    w_up,
    b_up,
    w_down,
    b_down,
    ln_gain,
    ln_bias,
    out_grad,
):
    half = tokens.shape[0]
    side = lax.axis_index("core")
    width, wide = b_qv.shape[1], tokens.shape[1]
    gains, shifts = ln_gain[:, None], ln_bias[:, None]
    a1_own, sum_dz = first_norm(tokens, out_grad, gains[0], shifts[0])

    small = cross(jnp.concatenate([b_qv.reshape(-1), b_up]))
    qkv_other, ready = gather_spread(w_qkv.reshape(-1, w_qkv.shape[2]), None)
    qkv_other = qkv_other.reshape(w_qkv.shape)
    up_other, ready = gather_spread(w_up, ready)
    out_other = cross(after(w_out, ready))
    down_other = cross(after(w_down, out_other))
    qv_biases = (b_qv, small[: 2 * width].reshape(2, width))
    up_biases = (b_up, small[2 * width :])
    qkvs, outs = (w_qkv, qkv_other), (w_out, out_other)
    ups, downs = (w_up, up_other), (w_down, down_other)

    a1 = jnp.concatenate([a1_own, core(a1_own)])
    dz = jnp.concatenate([out_grad, core(out_grad)])
    seg_other = core(segment_ids)
    seg = jnp.concatenate([segment_ids, seg_other])
    start = jnp.sum((seg[None, :] < seg[:, None]).astype(jnp.int32), axis=1)[None]
    ordered = jnp.where(side == 0, seg, jnp.concatenate([seg_other, segment_ids]))
    blocks = ordered.reshape(LEN // BLK, BLK)
    low = jnp.sum((blocks[None, :, -1] < blocks[:, None, 0]).astype(jnp.int32), axis=1)
    info = jnp.concatenate([(side * (LEN // BLK // 2))[None].astype(jnp.int32), low])

    saved = []
    for weight, bias in zip(qkvs, qv_biases):
        query, keys, values = project(a1, weight, bias)
        out, lse = attn_fwd(info, query, keys, values, start)
        saved.append((query, keys, values, out, lse))

    def pair_sum(lefts, rights, product):
        here, there = sum_dots(lefts, rights, product)
        return here, core(there)

    here, came = pair_sum([entry[3] for entry in saved], outs, nn)
    mixed, a2_own = second_norm(tokens, here, came, b_out[None], gains[1], shifts[1])
    a2 = jnp.concatenate([a2_own, core(a2_own)])
    acts = [up_gelu(a2, weight, bias) for weight, bias in zip(ups, up_biases)]
    activs = [act[0] for act in acts]
    grads_down = [tn(activ, dz).astype(bf16) for activ in activs]
    dus, sums_up = zip(*[back_act(dz, down, act[1]) for act, down in zip(acts, downs)])
    here, came = pair_sum(dus, ups, nt)
    grad_h, dattn_own, sums_h = norm_back(mixed, here, came, gains[1], out_grad)
    dattn = jnp.concatenate([dattn_own, core(dattn_own)])
    grads_up = [tn(a2, du).astype(bf16) for du in dus]
    here, came = pair_sum(activs, downs, nn)
    block_out = (mixed + here + came.astype(f32) + b_down.astype(f32)).astype(bf16)

    grads_out, grads_qkv, sums, trios = [], [], [], []
    for (query, keys, values, out, lse), w_o, sum_up in zip(saved, outs, sums_up):
        cot = nt(dattn, w_o).astype(bf16)
        trio = attn_bwd(info, query, keys, values, start, out, lse, cot)
        d_qkv, d_out, sum_trio = frame_sums(a1, trio, out, dattn)
        grads_qkv.append(d_qkv.reshape(-1, width))
        grads_out.append(d_out)
        trios.append(trio)
        sums.append(jnp.concatenate([sum_trio[0, 0], sum_trio[2, 0], sum_up[0]]))
    here, came = pair_sum(trios, qkvs, nt)
    grad_in, _, sums_x = norm_back(tokens, here, came, gains[0], grad_h)

    h = grads_down[0].shape[0] // 2
    grad_down = reduce_weight([tuple(g[i * h : i * h + h] for g in grads_down) for i in range(2)])
    grad_up = reduce_weight([tuple(g[i * h : i * h + h] for g in grads_up) for i in range(2)])
    grad_wout = reduce_weight([tuple(grads_out)])
    grad_qkv = reduce_weight([tuple(grads_qkv)])
    grad_qkv = grad_qkv.reshape(w_qkv.shape)

    common = jnp.concatenate([sums_h[2], sum_dz[0], sums_x[0], sums_h[0], sums_x[1], sums_h[1]])
    common = common + core(common)
    vector = jnp.concatenate([sums[0], common]) + cross(jnp.concatenate([sums[1], common]))
    vector = vector + swap(vector, "y")
    for bits in (1, 2):
        vector = vector + lax.ppermute(vector, "z", [(i, i ^ bits) for i in range(4)])
    units = b_up.shape[0]
    ends = [2 * width, units, wide, wide, 2 * wide, 2 * wide]
    cuts = [sum(ends[:i]) for i in range(len(ends) + 1)]
    grad_bqv, grad_bup, grad_bout, grad_bdown, grad_gain, grad_shift = [
        vector[low:high] for low, high in zip(cuts[:-1], cuts[1:])
    ]
    return (
        block_out,
        grad_in,
        grad_qkv,
        grad_bqv.reshape(b_qv.shape),
        grad_wout,
        grad_bout,
        grad_up,
        grad_bup,
        grad_down,
        grad_bdown,
        grad_gain.reshape(ln_gain.shape),
        grad_shift.reshape(ln_bias.shape),
    )


def solution(mesh):
    rows, frames = ("dp", "mp"), "mp"
    body = tensor_parallel_shards
    if row_per_chip(mesh):
        shape = (mesh.shape["dp"] // 2, 2, mesh.shape["mp"] // 2, 2)
        mesh = Mesh(mesh.devices.reshape(shape), ("z", "y", "x", "core"))
        rows, frames = ("z", "y", "x", "core"), ("x", "core")
        body = row_per_chip_shards
    in_specs = (
        P(rows, None),
        P(rows),
        P(None, None, frames),
        P(None, frames),
        P(frames, None),
        P(),
        P(None, frames),
        P(frames),
        P(frames, None),
        P(),
        P(),
        P(),
        P(rows, None),
    )
    out_specs = (
        P(rows, None),
        P(rows, None),
        P(None, None, frames),
        P(None, frames),
        P(frames, None),
        P(),
        P(None, frames),
        P(frames),
        P(frames, None),
        P(),
        P(),
        P(),
    )
    return jax.shard_map(body, mesh=mesh, in_specs=in_specs, out_specs=out_specs, check_vma=False)
```

```python
from functools import partial

import jax
import jax.numpy as jnp
from jax import lax
from jax.experimental import pallas as pl
from jax.experimental.pallas import tpu as pltpu
from jax.sharding import Mesh
from jax.sharding import PartitionSpec as P

HD = 64
LEN = 1024
QBLK = 512
EPS = 1e-05
BLK = 256

NEG = -1e30
GRANT = 10 << 20
BRIEF = pl.CostEstimate(flops=1, bytes_accessed=1, transcendentals=0)
f32 = jnp.float32
bf16 = jnp.bfloat16


def nt(left, right):
    return lax.dot_general(left, right, (((1,), (1,)), ((), ())), preferred_element_type=f32)


def nn(left, right):
    return lax.dot_general(left, right, (((1,), (0,)), ((), ())), preferred_element_type=f32)


def tn(left, right):
    return lax.dot_general(left, right, (((0,), (0,)), ((), ())), preferred_element_type=f32)


def attn_bias(block, j, first):
    q_pos = block * BLK + lax.broadcasted_iota(jnp.int32, (1, BLK), 1)
    k_pos = j * BLK + lax.broadcasted_iota(jnp.int32, (BLK, BLK), 0)
    return jnp.where((k_pos >= first) & (k_pos <= q_pos), 0.0, NEG)


def head_rows(refs, scratch, heads):
    lane = lax.broadcasted_iota(jnp.int32, (LEN, 2 * HD), 1)
    for ref, out in zip(refs, scratch):
        for h in range(heads):
            pair = ref[:, (h // 2) * 2 * HD : (h // 2 + 1) * 2 * HD]
            out[h] = jnp.where((lane < HD) == (h % 2 == 0), pair, jnp.zeros_like(pair))


def attn_fwd_body(info, q_ref, k_ref, v_ref, st_ref, o_ref, lse_ref, k_heads, v_turned):
    block = pl.program_id(0)
    heads = q_ref.shape[1] // HD
    first = st_ref[...]

    @pl.when(block == 0)
    def _():
        head_rows([k_ref], [k_heads], heads)
        for pair in range(heads // 2):
            turned = v_ref[:, pair * 2 * HD : (pair + 1) * 2 * HD].T
            for h in (0, 1):
                v_turned[2 * pair + h, :HD] = turned[h * HD : (h + 1) * HD]
                v_turned[2 * pair + h, HD:] = jnp.ones((16, LEN), bf16)

    def step(at, carry):
        j = block - at
        row = pl.multiple_of((j ^ info[0]) * BLK, BLK)
        bias = attn_bias(block, j, first)
        out = []
        for h in range(heads):
            top, acc = carry[h]
            query = q_ref[:, (h // 2) * 2 * HD : (h // 2 + 1) * 2 * HD]
            s = nt(k_heads[h, pl.ds(row, BLK), :], query) + bias
            new = jnp.maximum(top, jnp.max(s, axis=0, keepdims=True))
            p = jnp.exp(s - new).astype(bf16)
            acc = acc * jnp.exp(top - new) + nn(v_turned[h, :, pl.ds(row, BLK)], p)
            out.append((new, acc))
        return tuple(out)

    init = tuple((jnp.full((1, BLK), NEG, f32), jnp.zeros((HD + 16, BLK), f32)) for _ in range(heads))
    done = lax.fori_loop(0, block + 1 - info[1 + block], step, init)
    for pair in range(heads // 2):
        both = [acc[:HD] / acc[HD : HD + 1] for _, acc in done[2 * pair : 2 * pair + 2]]
        o_ref[:, pair * 2 * HD : (pair + 1) * 2 * HD] = jnp.concatenate(both, axis=0).T.astype(bf16)
    for h in range(heads):
        top, acc = done[h]
        lse_ref[h : h + 1, :] = top + jnp.log(acc[HD : HD + 1])


def attn_bwd_body(info, q_ref, k_ref, v_ref, st_ref, o_ref, lse_ref, do_ref, d_ref, k_heads, v_heads, dk_acc, dv_acc):
    block = pl.program_id(0)
    heads = q_ref.shape[1] // HD
    first = st_ref[...]
    lane = lax.broadcasted_iota(jnp.int32, (BLK, 2 * HD), 1)

    @pl.when(block == 0)
    def _():
        head_rows([k_ref, v_ref], [k_heads, v_heads], heads)
        dk_acc[...] = jnp.zeros_like(dk_acc)
        dv_acc[...] = jnp.zeros_like(dv_acc)

    deltas = []
    for pair in range(heads // 2):
        cols = slice(pair * 2 * HD, (pair + 1) * 2 * HD)
        turned = (do_ref[:, cols].astype(f32) * o_ref[:, cols].astype(f32)).T
        for h in (0, 1):
            deltas.append(jnp.sum(turned[h * HD : (h + 1) * HD], axis=0, keepdims=True))

    def step(j, dqs):
        row = pl.multiple_of((j ^ info[0]) * BLK, BLK)
        bias = attn_bias(block, j, first)
        out = list(dqs)
        for pair in range(heads // 2):
            cols = slice(pair * 2 * HD, (pair + 1) * 2 * HD)
            query, cot = q_ref[:, cols], do_ref[:, cols]
            dk = dk_acc[pl.ds(row, BLK), cols]
            dv = dv_acc[pl.ds(row, BLK), cols]
            for h in (2 * pair, 2 * pair + 1):
                mask = (lane < HD) == (h % 2 == 0)
                keys = k_heads[h, pl.ds(row, BLK), :]
                p = jnp.exp(nt(keys, query) + (bias - lse_ref[h : h + 1, :]))
                dp = nt(v_heads[h, pl.ds(row, BLK), :], cot)
                ds = (p * (dp - deltas[h])).astype(bf16)
                dv = dv + nn(p.astype(bf16), jnp.where(mask, cot, jnp.zeros_like(cot)))
                dk = dk + nn(ds, jnp.where(mask, query, jnp.zeros_like(query)))
                out[pair] = out[pair] + tn(ds, keys)
            dk_acc[pl.ds(row, BLK), cols] = dk
            dv_acc[pl.ds(row, BLK), cols] = dv
        return tuple(out)

    init = tuple(jnp.zeros((BLK, 2 * HD), f32) for _ in range(heads // 2))
    dqs = lax.fori_loop(info[1 + block], block + 1, step, init)
    here = pl.multiple_of((block ^ info[0]) * BLK, BLK)
    for pair in range(heads // 2):
        cols = slice(pair * 2 * HD, (pair + 1) * 2 * HD)
        d_ref[0, pl.ds(here, BLK), cols] = (dqs[pair] * HD**-0.5).astype(bf16)

    @pl.when(block == pl.num_programs(0) - 1)
    def _():
        d_ref[1] = dk_acc[...].astype(bf16)
        d_ref[2] = dv_acc[...].astype(bf16)


def attn_specs(width):
    small = pl.BlockSpec((BLK, width), lambda i, info: (i ^ info[0], 0))
    whole = pl.BlockSpec((LEN, width), lambda i, info: (0, 0))
    start = pl.BlockSpec((1, BLK), lambda i, info: (0, i ^ info[0]))
    lse = pl.BlockSpec((width // HD, BLK), lambda i, info: (0, i ^ info[0]))
    return small, whole, start, lse


def attn_fwd(info, query, keys, values, start):
    width = query.shape[1]
    heads = width // HD
    small, whole, first, lse = attn_specs(width)
    return pl.pallas_call(
        attn_fwd_body,
        out_shape=(jax.ShapeDtypeStruct(query.shape, bf16), jax.ShapeDtypeStruct((heads, LEN), f32)),
        grid_spec=pltpu.PrefetchScalarGridSpec(
            num_scalar_prefetch=1,
            grid=(LEN // BLK,),
            in_specs=[small, whole, whole, first],
            out_specs=[small, lse],
            scratch_shapes=[pltpu.VMEM((heads, LEN, 2 * HD), bf16), pltpu.VMEM((heads, HD + 16, LEN), bf16)],
        ),
        cost_estimate=BRIEF,
        compiler_params=pltpu.CompilerParams(vmem_limit_bytes=GRANT),
        name="attn_fwd",
    )(info, query, keys, values, start)


def attn_bwd(info, query, keys, values, start, out, lse, cot):
    width = query.shape[1]
    heads = width // HD
    small, whole, first, lse_spec = attn_specs(width)
    return pl.pallas_call(
        attn_bwd_body,
        out_shape=jax.ShapeDtypeStruct((3,) + query.shape, bf16),
        grid_spec=pltpu.PrefetchScalarGridSpec(
            num_scalar_prefetch=1,
            grid=(LEN // BLK,),
            in_specs=[small, whole, whole, first, small, lse_spec, small],
            out_specs=pl.BlockSpec((3, LEN, width), lambda i, info: (0, 0, 0)),
            scratch_shapes=[
                pltpu.VMEM((heads, LEN, 2 * HD), bf16),
                pltpu.VMEM((heads, LEN, 2 * HD), bf16),
                pltpu.VMEM((LEN, width), f32),
                pltpu.VMEM((LEN, width), f32),
            ],
        ),
        cost_estimate=BRIEF,
        compiler_params=pltpu.CompilerParams(vmem_limit_bytes=GRANT),
        name="attn_bwd",
    )(info, query, keys, values, start, out, lse, cot)


def up_body(a_ref, w_ref, b_ref, g_ref, s_ref):
    rows = a_ref[...]
    for part in range(w_ref.shape[1] // 256):
        cols = slice(part * 256, part * 256 + 256)
        u = nn(rows, w_ref[:, cols]) + b_ref[:, cols].astype(f32)
        size = jnp.abs(u)
        t = 1.0 / (1.0 + 0.3275911 * 0.7071067811865476 * size)
        poly = t * (0.5 * 0.254829592 + t * (0.5 * -0.284496736 + t * (0.5 * 1.421413741 + t * (0.5 * -1.453152027 + t * (0.5 * 1.061405429)))))
        bell = jnp.exp(-0.5 * u * u)
        tail = poly * bell
        cdf = jnp.where(u >= 0, 1.0 - tail, tail)
        g_ref[:, cols] = (u * cdf).astype(bf16)
        s_ref[:, cols] = (cdf + u * bell * 0.3989422804014327).astype(bf16)


def up_gelu(rows, weight, bias):
    m, k = rows.shape
    n = weight.shape[1]
    bm = 256
    shape = jax.ShapeDtypeStruct((m, n), bf16)
    tile = pl.BlockSpec((bm, n), lambda i: (i, 0))
    return pl.pallas_call(
        up_body,
        out_shape=(shape, shape),
        grid=(m // bm,),
        in_specs=[pl.BlockSpec((bm, k), lambda i: (i, 0)), pl.BlockSpec((k, n), lambda i: (0, 0)), pl.BlockSpec((1, n), lambda i: (0, 0))],
        out_specs=(tile, tile),
        cost_estimate=BRIEF,
        compiler_params=pltpu.CompilerParams(vmem_limit_bytes=GRANT),
        name="up_gelu",
    )(rows, weight, bias.reshape(1, n))


def const_spec(shape):
    return pl.BlockSpec(shape, lambda i: (0,) * len(shape))


def row_spec(rows, cols):
    return pl.BlockSpec((rows, cols), lambda i: (i, 0))


def project_body(a_ref, w_ref, b_ref, q_ref, k_ref, v_ref):
    rows = a_ref[...]
    q_ref[...] = (nn(rows, w_ref[0]) + b_ref[0:1].astype(f32)).astype(bf16) * jnp.bfloat16(HD**-0.5)
    k_ref[...] = nn(rows, w_ref[1]).astype(bf16)
    v_ref[...] = (nn(rows, w_ref[2]) + b_ref[1:2].astype(f32)).astype(bf16)


def project(rows, weight, bias):
    m, k = rows.shape
    n = weight.shape[2]
    tile = 256
    shape = jax.ShapeDtypeStruct((m, n), bf16)
    return pl.pallas_call(
        project_body,
        out_shape=(shape, shape, shape),
        grid=(m // tile,),
        in_specs=[row_spec(tile, k), const_spec(weight.shape), const_spec(bias.shape)],
        out_specs=[row_spec(tile, n)] * 3,
        cost_estimate=BRIEF,
        compiler_params=pltpu.CompilerParams(vmem_limit_bytes=GRANT),
        name="project",
    )(rows, weight, bias)


def sum_dots(product, lefts, rights):
    stacked = lefts[0].ndim == 3
    m, k = lefts[0].shape[-2:]
    n = rights[0].shape[-1] if product is nn else rights[0].shape[-2]
    terms = len(lefts)
    tile = 256
    steps = m // tile // 2

    def body(*refs):
        total = None
        for left, right in zip(refs[:terms], refs[terms : 2 * terms]):
            for at in range(left.shape[0] if stacked else 1):
                term = product(left[at], right[at]) if stacked else product(left[...], right[...])
                total = term if total is None else total + term
        here, there = refs[2 * terms :]

        @pl.when(pl.program_id(0) < steps)
        def _():
            there[...] = total.astype(bf16)

        @pl.when(pl.program_id(0) >= steps)
        def _():
            here[...] = total

    def turn(i):
        return jnp.where(i < steps, i + steps, i - steps)

    if stacked:
        left_spec = pl.BlockSpec((lefts[0].shape[0], tile, k), lambda i: (0, turn(i), 0))
    else:
        left_spec = pl.BlockSpec((tile, k), lambda i: (turn(i), 0))
    return pl.pallas_call(
        body,
        out_shape=(jax.ShapeDtypeStruct((m // 2, n), f32), jax.ShapeDtypeStruct((m // 2, n), bf16)),
        grid=(2 * steps,),
        in_specs=[left_spec] * terms + [const_spec(r.shape) for r in rights],
        out_specs=[
            pl.BlockSpec((tile, n), lambda i: (jnp.maximum(i - steps, 0), 0)),
            pl.BlockSpec((tile, n), lambda i: (jnp.minimum(i, steps - 1), 0)),
        ],
        cost_estimate=BRIEF,
        compiler_params=pltpu.CompilerParams(vmem_limit_bytes=GRANT),
        name="sum_dots",
    )(*lefts, *rights)


def center_rows(rows):
    center = rows - jnp.mean(rows, axis=-1, keepdims=True)
    scale = lax.rsqrt(jnp.mean(center * center, axis=-1, keepdims=True) + EPS)
    return center * scale, scale


def first_norm_body(x_ref, g_ref, gain_ref, shift_ref, a_ref, sum_ref):
    normal, _ = center_rows(x_ref[...].astype(f32))
    a_ref[...] = (normal * gain_ref[...] + shift_ref[...]).astype(bf16)

    @pl.when(pl.program_id(0) == 0)
    def _():
        sum_ref[...] = jnp.zeros_like(sum_ref)

    sum_ref[...] += jnp.sum(g_ref[...].astype(f32), axis=0, keepdims=True)


def first_norm(tokens, cotangent, gain, shift):
    m, d = tokens.shape
    tile = 128
    return pl.pallas_call(
        first_norm_body,
        out_shape=(jax.ShapeDtypeStruct((m, d), bf16), jax.ShapeDtypeStruct((1, d), f32)),
        grid=(m // tile,),
        in_specs=[row_spec(tile, d), row_spec(tile, d), const_spec((1, d)), const_spec((1, d))],
        out_specs=[row_spec(tile, d), const_spec((1, d))],
        cost_estimate=BRIEF,
        compiler_params=pltpu.CompilerParams(vmem_limit_bytes=GRANT),
        name="first_norm",
    )(tokens, cotangent, gain, shift)


def second_norm_body(x_ref, here_ref, came_ref, b_ref, gain_ref, shift_ref, h_ref, a_ref):
    mixed = x_ref[...].astype(f32) + (here_ref[...] + came_ref[...].astype(f32)) + b_ref[...].astype(f32)
    h_ref[...] = mixed
    normal, _ = center_rows(mixed)
    a_ref[...] = (normal * gain_ref[...] + shift_ref[...]).astype(bf16)


def second_norm(tokens, here, came, bias, gain, shift):
    m, d = tokens.shape
    tile = 128
    return pl.pallas_call(
        second_norm_body,
        out_shape=(jax.ShapeDtypeStruct((m, d), f32), jax.ShapeDtypeStruct((m, d), bf16)),
        grid=(m // tile,),
        in_specs=[row_spec(tile, d)] * 3 + [const_spec((1, d))] * 3,
        out_specs=[row_spec(tile, d)] * 2,
        cost_estimate=BRIEF,
        compiler_params=pltpu.CompilerParams(vmem_limit_bytes=GRANT),
        name="second_norm",
    )(tokens, here, came, bias, gain, shift)


def norm_back_body(v_ref, here_ref, came_ref, gain_ref, res_ref, out_ref, low_ref, sums_ref):
    normal, scale = center_rows(v_ref[...].astype(f32))
    grad = here_ref[...] + came_ref[...].astype(f32)
    scaled = grad * gain_ref[...]
    inner = jnp.mean(scaled * normal, axis=-1, keepdims=True)
    back = scale * (scaled - jnp.mean(scaled, axis=-1, keepdims=True) - normal * inner)
    back = back + res_ref[...].astype(f32)
    low = back.astype(bf16)
    out_ref[...] = back
    low_ref[...] = low

    @pl.when(pl.program_id(0) == 0)
    def _():
        sums_ref[...] = jnp.zeros_like(sums_ref)

    sums_ref[0:1] += jnp.sum(grad * normal, axis=0, keepdims=True)
    sums_ref[1:2] += jnp.sum(grad, axis=0, keepdims=True)
    sums_ref[2:3] += jnp.sum(low.astype(f32), axis=0, keepdims=True)


def norm_back(values, here, came, gain, residual):
    m, d = values.shape
    tile = 128
    return pl.pallas_call(
        norm_back_body,
        out_shape=(
            jax.ShapeDtypeStruct((m, d), f32),
            jax.ShapeDtypeStruct((m, d), bf16),
            jax.ShapeDtypeStruct((8, d), f32),
        ),
        grid=(m // tile,),
        in_specs=[row_spec(tile, d)] * 3 + [const_spec((1, d)), row_spec(tile, d)],
        out_specs=[row_spec(tile, d)] * 2 + [const_spec((8, d))],
        cost_estimate=BRIEF,
        compiler_params=pltpu.CompilerParams(vmem_limit_bytes=GRANT),
        name="norm_back",
    )(values, here, came, gain, residual)


def back_act_body(z_ref, w_ref, s_ref, du_ref, sum_ref):
    du = (nt(z_ref[...], w_ref[...]) * s_ref[...].astype(f32)).astype(bf16)
    du_ref[...] = du

    @pl.when(pl.program_id(0) == 0)
    def _():
        sum_ref[...] = jnp.zeros_like(sum_ref)

    sum_ref[...] += jnp.sum(du.astype(f32), axis=0, keepdims=True)


def back_act(cotangent, weight, slope):
    m, d = cotangent.shape
    n = weight.shape[0]
    tile = 256
    return pl.pallas_call(
        back_act_body,
        out_shape=(jax.ShapeDtypeStruct((m, n), bf16), jax.ShapeDtypeStruct((1, n), f32)),
        grid=(m // tile,),
        in_specs=[row_spec(tile, d), const_spec((n, d)), row_spec(tile, n)],
        out_specs=[row_spec(tile, n), const_spec((1, n))],
        cost_estimate=BRIEF,
        compiler_params=pltpu.CompilerParams(vmem_limit_bytes=GRANT),
        name="back_act",
    )(cotangent, weight, slope)


def frame_sums_body(a_ref, d_ref, o_ref, g_ref, one_ref, two_ref, sums_ref, a_turned):
    rows, width = g_ref.shape[1], o_ref.shape[1]
    count = rows // width
    a_turned[...] = a_ref[...].T
    for at in range(4 * count):
        kind, part = divmod(at, count)
        out = one_ref if at < 2 * count else two_ref
        if kind < 3:
            block = nn(a_turned[part * width : (part + 1) * width, :], d_ref[kind])
        else:
            block = tn(o_ref[...], g_ref[:, part * width : (part + 1) * width])
        low = (at % (2 * count)) * width
        out[low : low + width, :] = block.astype(bf16)
    for kind in range(3):
        sums_ref[kind] = jnp.sum(d_ref[kind].astype(f32), axis=0, keepdims=True)


def frame_sums(rows, trio, out, cotangent):
    t, d = rows.shape
    n = trio.shape[2]
    half = jax.ShapeDtypeStruct((2 * d, n), bf16)
    one, two, sums = pl.pallas_call(
        frame_sums_body,
        out_shape=(half, half, jax.ShapeDtypeStruct((3, 1, n), f32)),
        grid=(1,),
        in_specs=[const_spec((t, d)), const_spec((3, t, n)), const_spec((t, n)), const_spec((t, d))],
        out_specs=[const_spec((2 * d, n)), const_spec((2 * d, n)), const_spec((3, 1, n))],
        scratch_shapes=[pltpu.VMEM((d, t), bf16)],
        cost_estimate=BRIEF,
        compiler_params=pltpu.CompilerParams(vmem_limit_bytes=GRANT),
        name="frame_sums",
    )(rows, trio, out, cotangent)
    return (one, two), sums


def norm_rows(values, gain, shift):
    center = values - jnp.mean(values, axis=-1, keepdims=True)
    spread = jnp.mean(center * center, axis=-1, keepdims=True)
    return center * lax.rsqrt(spread + EPS) * gain + shift


def split_heads(flat, rows):
    return flat.reshape(rows, LEN, flat.shape[1] // HD, HD)


def block_scores(query, keys, seg_q, seg_k, offset):
    scores = jnp.einsum(
        "rqhd,rkhd->rhqk", query, keys, preferred_element_type=jnp.float32
    ) * HD ** (-0.5)
    q_pos = offset + jnp.arange(query.shape[1], dtype=jnp.int32)
    k_pos = jnp.arange(keys.shape[1], dtype=jnp.int32)
    allowed = (seg_q[:, :, None] == seg_k[:, None, :]) & (
        k_pos[None, None, :] <= q_pos[None, :, None]
    )
    return jnp.where(allowed[:, None], scores, -1e30)


def attention_forward(query, keys, values, seg_all):
    rows = query.shape[0] // LEN
    q4 = split_heads(query, rows)
    k4 = split_heads(keys, rows)
    v4 = split_heads(values, rows)
    seg2 = seg_all.reshape(rows, LEN)
    outputs = []
    totals = []
    for block in range(LEN // QBLK):
        first = block * QBLK
        end = first + QBLK
        scores = block_scores(
            q4[:, first:end], k4[:, :end], seg2[:, first:end], seg2[:, :end], first
        )
        top = jnp.max(scores, axis=-1, keepdims=True)
        expd = jnp.exp(scores - top)
        summed = jnp.sum(expd, axis=-1, keepdims=True)
        weights = (expd / summed).astype(jnp.bfloat16)
        outputs.append(
            jnp.einsum("rhqk,rkhd->rqhd", weights, v4[:, :end], preferred_element_type=jnp.float32)
        )
        totals.append(top + jnp.log(summed))
    attended = jnp.concatenate(outputs, axis=1).reshape(query.shape).astype(jnp.bfloat16)
    return (attended, totals)


def attention_backward(query, keys, values, seg_all, totals, grad_att):
    rows = query.shape[0] // LEN
    q4 = split_heads(query, rows)
    k4 = split_heads(keys, rows)
    v4 = split_heads(values, rows)
    g4 = split_heads(grad_att, rows)
    seg2 = seg_all.reshape(rows, LEN)
    scale = HD ** (-0.5)
    grad_k = jnp.zeros(k4.shape, jnp.float32)
    grad_v = jnp.zeros(v4.shape, jnp.float32)
    grad_q_parts = []
    for block in range(LEN // QBLK):
        first = block * QBLK
        end = first + QBLK
        scores = block_scores(
            q4[:, first:end], k4[:, :end], seg2[:, first:end], seg2[:, :end], first
        )
        probs = jnp.exp(scores - totals[block])
        weights = probs.astype(jnp.bfloat16)
        grad_w = jnp.einsum(
            "rqhd,rkhd->rhqk", g4[:, first:end], v4[:, :end], preferred_element_type=jnp.float32
        )
        delta = jnp.sum(probs * grad_w, axis=-1, keepdims=True)
        grad_s = (probs * (grad_w - delta)).astype(jnp.bfloat16)
        grad_q_parts.append(
            jnp.einsum("rhqk,rkhd->rqhd", grad_s, k4[:, :end], preferred_element_type=jnp.float32)
            * scale
        )
        padding = ((0, 0), (0, LEN - end), (0, 0), (0, 0))
        grad_k = grad_k + jnp.pad(
            jnp.einsum(
                "rhqk,rqhd->rkhd", grad_s, q4[:, first:end], preferred_element_type=jnp.float32
            )
            * scale,
            padding,
        )
        grad_v = grad_v + jnp.pad(
            jnp.einsum(
                "rhqk,rqhd->rkhd", weights, g4[:, first:end], preferred_element_type=jnp.float32
            ),
            padding,
        )
    shape = query.shape
    grad_q = jnp.concatenate(grad_q_parts, axis=1).reshape(shape).astype(jnp.bfloat16)
    return (
        grad_q,
        grad_k.reshape(shape).astype(jnp.bfloat16),
        grad_v.reshape(shape).astype(jnp.bfloat16),
    )


def tensor_parallel_shards(
    tokens,
    segment_ids,
    w_qkv,
    b_qv,
    w_out,
    b_out,
    w_up,
    b_up,
    w_down,
    b_down,
    ln_gain,
    ln_bias,
    out_grad,
):
    resid = tokens.astype(jnp.float32)
    qv_bias = b_qv.astype(jnp.float32)
    up_bias = b_up.astype(jnp.float32)
    local_rows = tokens.shape[0]
    normed, first_back = jax.vjp(norm_rows, resid, ln_gain[0], ln_bias[0])
    lowered = normed.astype(jnp.bfloat16)
    joined, seg_all = (
        lax.all_gather(lowered, "mp", axis=0, tiled=True),
        lax.all_gather(segment_ids, "mp", axis=0, tiled=True),
    )
    query = (jnp.dot(joined, w_qkv[0], preferred_element_type=jnp.float32) + qv_bias[0]).astype(
        jnp.bfloat16
    )
    keys = jnp.dot(joined, w_qkv[1], preferred_element_type=jnp.float32).astype(jnp.bfloat16)
    values = (jnp.dot(joined, w_qkv[2], preferred_element_type=jnp.float32) + qv_bias[1]).astype(
        jnp.bfloat16
    )
    query, keys, values = (query, keys, values)
    attended, totals = attention_forward(query, keys, values, seg_all)
    attn_sum = lax.psum_scatter(
        jnp.dot(attended, w_out, preferred_element_type=jnp.float32).astype(jnp.bfloat16),
        "mp",
        scatter_dimension=0,
        tiled=True,
    ).astype(jnp.float32)
    mixed = resid + attn_sum + b_out.astype(jnp.float32)
    normed2, second_back = jax.vjp(norm_rows, mixed, ln_gain[1], ln_bias[1])
    lowered2 = normed2.astype(jnp.bfloat16)
    joined2 = lax.all_gather(lowered2, "mp", axis=0, tiled=True)
    pre_act = jnp.dot(joined2, w_up, preferred_element_type=jnp.float32) + up_bias
    pre_act, activ = (pre_act, jax.nn.gelu(pre_act, approximate=False).astype(jnp.bfloat16))
    block_out = (
        mixed
        + lax.psum_scatter(
            jnp.dot(activ, w_down, preferred_element_type=jnp.float32).astype(jnp.bfloat16),
            "mp",
            scatter_dimension=0,
            tiled=True,
        ).astype(jnp.float32)
        + b_down.astype(jnp.float32)
    ).astype(jnp.bfloat16)
    grad_y = out_grad.astype(jnp.float32)
    grad_z = lax.all_gather(out_grad, "mp", axis=0, tiled=True)
    grad_down = jnp.einsum("tf,td->fd", activ, grad_z, preferred_element_type=jnp.float32)
    grad_bdown = jnp.sum(grad_z, axis=0, dtype=jnp.float32)
    grad_act = jnp.einsum("td,fd->tf", grad_z, w_down, preferred_element_type=jnp.float32)
    gelu_back = jax.vjp(lambda value: jax.nn.gelu(value, approximate=False), pre_act)[1]
    grad_pre = gelu_back(grad_act)[0].astype(jnp.bfloat16)
    grad_up = jnp.einsum("td,tf->df", joined2, grad_pre, preferred_element_type=jnp.float32)
    grad_bup = jnp.sum(grad_pre, axis=0, dtype=jnp.float32)
    grad_n2 = lax.psum_scatter(
        jnp.einsum("tf,df->td", grad_pre, w_up, preferred_element_type=jnp.float32).astype(
            jnp.bfloat16
        ),
        "mp",
        scatter_dimension=0,
        tiled=True,
    ).astype(jnp.float32)
    grad_h, grad_g2, grad_s2 = second_back(grad_n2)
    grad_h = grad_h + grad_y
    grad_branch = lax.all_gather(grad_h.astype(jnp.bfloat16), "mp", axis=0, tiled=True)
    grad_wout = jnp.einsum("tc,td->cd", attended, grad_branch, preferred_element_type=jnp.float32)
    grad_bout = jnp.sum(grad_branch, axis=0, dtype=jnp.float32)
    grad_att = jnp.einsum(
        "td,cd->tc", grad_branch, w_out, preferred_element_type=jnp.float32
    ).astype(jnp.bfloat16)
    grad_q, grad_k, grad_v = attention_backward(query, keys, values, seg_all, totals, grad_att)
    grad_qkv = jnp.stack(
        [
            jnp.einsum("td,tc->dc", joined, piece, preferred_element_type=jnp.float32)
            for piece in (grad_q, grad_k, grad_v)
        ]
    )
    grad_bqv = jnp.stack(
        [jnp.sum(grad_q, axis=0, dtype=jnp.float32), jnp.sum(grad_v, axis=0, dtype=jnp.float32)]
    )
    summed = jnp.zeros((local_rows * lax.axis_size("mp"), w_qkv.shape[1]), jnp.float32)
    for index, piece in enumerate((grad_q, grad_k, grad_v)):
        summed = summed + jnp.einsum(
            "tc,dc->td", piece, w_qkv[index], preferred_element_type=jnp.float32
        )
    grad_n1 = lax.psum_scatter(
        summed.astype(jnp.bfloat16), "mp", scatter_dimension=0, tiled=True
    ).astype(jnp.float32)
    grad_x, grad_g1, grad_s1 = first_back(grad_n1)
    grad_in = grad_x + grad_h
    weight_totals = (
        lax.psum(grad_qkv.astype(jnp.bfloat16), "dp").astype(jnp.float32),
        lax.psum(grad_bqv.astype(jnp.bfloat16), "dp").astype(jnp.float32),
        lax.psum(grad_wout.astype(jnp.bfloat16), "dp").astype(jnp.float32),
        lax.psum(grad_bout.astype(jnp.bfloat16), "dp").astype(jnp.float32),
        lax.psum(grad_up.astype(jnp.bfloat16), "dp").astype(jnp.float32),
        lax.psum(grad_bup.astype(jnp.bfloat16), "dp").astype(jnp.float32),
        lax.psum(grad_down.astype(jnp.bfloat16), "dp").astype(jnp.float32),
        lax.psum(grad_bdown.astype(jnp.bfloat16), "dp").astype(jnp.float32),
    )
    norm_totals = lax.psum(
        (jnp.stack([grad_g1, grad_g2]), jnp.stack([grad_s1, grad_s2])), ("dp", "mp")
    )
    return (block_out, grad_in) + tuple(weight_totals) + tuple(norm_totals)


def row_per_chip(mesh):
    return mesh.shape["mp"] == 4 and mesh.shape["dp"] == 8


def swap(value, axis):
    return lax.ppermute(value, axis, [(0, 1), (1, 0)])


def core(value):
    return swap(value, "core")


def cross(value):
    return swap(value, "x")


def after(value, *others):
    return lax.optimization_barrier((value,) + others)[0]


def take(value, at):
    return lax.dynamic_index_in_dim(value, at, 0, keepdims=False)


def place(whole, piece, at):
    return lax.dynamic_update_index_in_dim(whole, piece, at, 0)


def quarter_of(weight):
    me = lax.axis_index("y") + 2 * (lax.axis_index("z") & 1)
    return take(weight.reshape(4, -1, weight.shape[-1]), me)


def share(mine):
    out = [swap(mine, "y")]
    for bits in (2, 3):
        out.append(lax.ppermute(mine, ("z", "y"), [(i, i ^ bits) for i in range(8)]))
    return out


def assemble(mine, others):
    me = lax.axis_index("y") + 2 * (lax.axis_index("z") & 1)
    whole = place(jnp.zeros((4,) + mine.shape, mine.dtype), mine, me)
    for bits, piece in zip((1, 2, 3), others):
        whole = place(whole, piece, me ^ bits)
    return whole.reshape(-1, mine.shape[-1])


def across_frames(left, right):
    return tn(left, right).astype(bf16)


def everyone(value):
    return lax.all_to_all(value, "z", 0, 0, tiled=False)


def deal(value):
    return lax.all_to_all(value, "z", 0, 0, tiled=False)


def swap_z(value, bits):
    return lax.ppermute(value, "z", [(i, i ^ bits) for i in range(4)])


def spread_y(own, got):
    side = lax.axis_index("y")
    return (take(own, 1 - side).astype(f32) + take(got, 1 - side).astype(f32)).astype(bf16)


def spread_z(own, got, near):
    side = lax.axis_index("y")
    total = take(own, side).astype(f32) + take(got, side).astype(f32) + near.astype(f32)
    return total.astype(bf16)


def gather_z(parts):
    mine = jnp.sum(parts.astype(f32), axis=0).astype(bf16)
    return jnp.broadcast_to(mine, (4,) + mine.shape)


def by_owner(value):
    return value.reshape(2, 4, value.shape[0] // 8, value.shape[1])


def settle(*pieces):
    side = lax.axis_index("y")
    whole = jnp.zeros((2,) + pieces[0].shape, f32)
    for flip in (0, 1):
        whole = place(whole, pieces[flip].astype(f32), side ^ flip)
    return whole.reshape(-1, pieces[0].shape[-1])


def join_attn(pieces, qkv_shape, out_shape):
    whole = jnp.concatenate([p.reshape(-1, out_shape[0], qkv_shape[2]) for p in pieces])
    cut = whole.shape[0] - out_shape[1] // qkv_shape[2]
    grad_out = jnp.swapaxes(whole[cut:], 0, 1).reshape(out_shape)
    return whole[:cut].reshape(qkv_shape), grad_out


class Line:
    def __init__(self):
        self.last = None

    def __call__(self, function, *args):
        if self.last is not None:
            args, _ = lax.optimization_barrier((args, self.last))
        out = function(*args)
        self.last = jax.tree.leaves(out)[0]
        return out


def row_per_chip_shards(
    tokens,
    segment_ids,
    w_qkv,
    b_qv,
    w_out,
    b_out,
    w_up,
    b_up,
    w_down,
    b_down,
    ln_gain,
    ln_bias,
    out_grad,
):
    side = lax.axis_index("core")
    width, wide = b_qv.shape[1], tokens.shape[1]
    gains, shifts = ln_gain[:, None], ln_bias[:, None]
    line = Line()

    def pair(own, other):
        return line(lambda *both: jnp.concatenate(both), own, other)

    qkv_mine = cross(line(quarter_of, w_qkv.reshape(-1, width)))
    a1_own, sum_dz = line(first_norm, tokens, out_grad, gains[0], shifts[0])
    a1_came = core(a1_own)
    seg_other = core(segment_ids)
    small = cross(jnp.concatenate([b_qv.reshape(-1), b_up]))
    up_quarter = line(quarter_of, w_up)
    down_quarter = line(quarter_of, w_down)

    def ranges(mine, other):
        seg = jnp.concatenate([mine, other])
        start = jnp.sum((seg[None, :] < seg[:, None]).astype(jnp.int32), axis=1)[None]
        ordered = jnp.where(side == 0, seg, jnp.concatenate([other, mine]))
        blocks = ordered.reshape(LEN // BLK, BLK)
        low = jnp.sum((blocks[None, :, -1] < blocks[:, None, 0]).astype(jnp.int32), axis=1)
        return start, jnp.concatenate([(side * (LEN // BLK // 2))[None].astype(jnp.int32), low])

    start, info = line(ranges, segment_ids, seg_other)
    a1 = pair(a1_own, a1_came)
    own = tuple(line(project, a1, w_qkv, b_qv))
    qkv_mine, w_out_now, up_quarter, _ = lax.optimization_barrier((qkv_mine, w_out, up_quarter, own[0]))
    qkv_parts = share(qkv_mine)
    out_other = cross(w_out_now)
    up_mine = cross(up_quarter)
    own = own + tuple(line(partial(attn_fwd, info), *own, start))
    up_mine, down_quarter, _ = lax.optimization_barrier((up_mine, down_quarter, own[3]))
    up_parts = share(up_mine)
    down_mine = cross(down_quarter)
    qkv_other = line(assemble, qkv_mine, qkv_parts).reshape(w_qkv.shape)
    other = tuple(line(project, a1, qkv_other, small[: 2 * width].reshape(2, width)))
    other = other + tuple(line(partial(attn_fwd, info), *other, start))
    down_mine, dz_own, _ = lax.optimization_barrier((down_mine, out_grad, other[3]))
    down_parts = share(down_mine)
    dz_came = core(dz_own)

    here, there = line(partial(sum_dots, nn), [own[3], other[3]], [w_out, out_other])
    came = core(there)
    up_other = line(assemble, up_mine, up_parts)
    mixed, a2_own = line(second_norm, tokens, here, came, b_out[None], gains[1], shifts[1])
    a2_came = core(a2_own)
    dz = pair(dz_own, dz_came)
    a2 = pair(a2_own, a2_came)

    act_other, slope_other = line(up_gelu, a2, up_other, small[2 * width :])
    down_got = cross(line(across_frames, act_other, dz))
    act_own, slope_own = line(up_gelu, a2, w_up, b_up)
    down_own = line(across_frames, act_own, dz)
    du_own, sum_up_own = line(back_act, dz, w_down, slope_own)
    down_other = line(assemble, down_mine, down_parts)
    du_other, sum_up_other = line(back_act, dz, down_other, slope_other)
    here, there = line(partial(sum_dots, nt), [du_own, du_other], [w_up, up_other])
    came = core(there)
    up_other_grad = line(across_frames, a2, du_other)
    grad_h, dattn_own, sums_h = line(norm_back, mixed, here, came, gains[1], out_grad)
    dattn_came = core(dattn_own)
    up_got = cross(after(up_other_grad, grad_h))
    up_own = line(across_frames, a2, du_own)
    dattn = pair(dattn_own, dattn_came)

    def back(entry, weight):
        query, keys, values, out, lse = entry
        cot = line(lambda *both: nt(*both).astype(bf16), dattn, weight)
        trio = line(partial(attn_bwd, info), query, keys, values, start, out, lse, cot)
        return (trio,) + tuple(line(frame_sums, a1, trio, out, dattn))

    trio_other, attn_other, sum_trio_other = back(other, out_other)
    down_own, down_got = by_owner(down_own), by_owner(down_got)
    down_near = swap(line(spread_y, down_own, down_got), "y")
    trio_own, attn_own, sum_trio_own = back(own, w_out)
    down_parts = deal(line(spread_z, down_own, down_got, down_near))
    here, there = line(partial(sum_dots, nt), [trio_own, trio_other], [w_qkv, qkv_other])
    came = core(there)
    y_here, y_there = line(partial(sum_dots, nn), [act_own, act_other], [w_down, down_other])
    y_came = core(y_there)
    grad_in, _, sums_x = line(norm_back, tokens, here, came, gains[0], grad_h)
    down_level = everyone(line(gather_z, down_parts))
    up_own, up_got = by_owner(up_own), by_owner(up_got)
    up_near = swap(line(spread_y, up_own, up_got), "y")
    attn_got = []
    hold = up_got
    for piece in attn_other:
        hold = cross(after(piece, hold))
        attn_got.append(hold)

    def finish(mixed, here, came):
        return (mixed + here + came.astype(f32) + b_down.astype(f32)).astype(bf16)

    block_out = line(finish, mixed, y_here, y_came)
    sums = [
        line(lambda trio, up: jnp.concatenate([trio[0, 0], trio[2, 0], up[0]]), trio, up)
        for trio, up in ((sum_trio_own, sum_up_own), (sum_trio_other, sum_up_other))
    ]
    common = line(
        lambda h, z, x: jnp.concatenate([h[2], z[0], x[0], h[0], x[1], h[1]]), sums_h, sum_dz, sums_x
    )
    common_came = core(common)
    up_parts = deal(line(spread_z, up_own, up_got, up_near))
    vector, vector_out = line(
        lambda a, b, c, d: (jnp.concatenate([a, c + d]), jnp.concatenate([b, c + d])), *sums, common, common_came
    )
    vector_came = cross(vector_out)
    down_other_level = swap(down_level, "y")
    pairs = [(by_owner(o), by_owner(g)) for o, g in zip(attn_own, attn_got)]
    add = lambda left, right: left + right
    attn_near = [swap(line(spread_y, *pairs[0]), "y")]
    vector = line(add, vector, vector_came)
    vector_came = swap(vector, "y")
    grad_down = line(settle, down_level, down_other_level)
    up_level = everyone(line(gather_z, up_parts))
    attn_parts = [deal(line(spread_z, *pairs[0], attn_near[0]))]
    vector = line(add, vector, vector_came)
    vector_came = swap_z(vector, 1)
    up_other_level = swap(up_level, "y")
    attn_near.append(swap(line(spread_y, *pairs[1]), "y"))
    attn_levels = [everyone(line(gather_z, attn_parts[0]))]
    vector = line(add, vector, vector_came)
    vector_came = swap_z(vector, 2)
    grad_up = line(settle, up_level, up_other_level)
    attn_parts.append(deal(line(spread_z, *pairs[1], attn_near[1])))
    vector = line(add, vector, vector_came)
    attn_others = [swap(attn_levels[0], "y")]
    attn_levels.append(everyone(line(gather_z, attn_parts[1])))
    attn_grads = [line(settle, attn_levels[0], attn_others[0])]
    attn_others.append(swap(attn_levels[1], "y"))
    attn_grads.append(line(settle, attn_levels[1], attn_others[1]))
    grad_qkv, grad_wout = join_attn(attn_grads, w_qkv.shape, w_out.shape)
    units = b_up.shape[0]
    ends = [2 * width, units, wide, wide, 2 * wide, 2 * wide]
    cuts = [sum(ends[:i]) for i in range(len(ends) + 1)]
    grad_bqv, grad_bup, grad_bout, grad_bdown, grad_gain, grad_shift = [
        vector[low:high] for low, high in zip(cuts[:-1], cuts[1:])
    ]
    return (
        block_out,
        grad_in,
        grad_qkv,
        grad_bqv.reshape(b_qv.shape),
        grad_wout,
        grad_bout,
        grad_up,
        grad_bup,
        grad_down,
        grad_bdown,
        grad_gain.reshape(ln_gain.shape),
        grad_shift.reshape(ln_bias.shape),
    )


def solution(mesh):
    rows, frames = ("dp", "mp"), "mp"
    body = tensor_parallel_shards
    if row_per_chip(mesh):
        shape = (mesh.shape["dp"] // 2, 2, mesh.shape["mp"] // 2, 2)
        mesh = Mesh(mesh.devices.reshape(shape), ("z", "y", "x", "core"))
        rows, frames = ("z", "y", "x", "core"), ("x", "core")
        body = row_per_chip_shards
    in_specs = (
        P(rows, None),
        P(rows),
        P(None, None, frames),
        P(None, frames),
        P(frames, None),
        P(),
        P(None, frames),
        P(frames),
        P(frames, None),
        P(),
        P(),
        P(),
        P(rows, None),
    )
    out_specs = (
        P(rows, None),
        P(rows, None),
        P(None, None, frames),
        P(None, frames),
        P(frames, None),
        P(),
        P(None, frames),
        P(frames),
        P(frames, None),
        P(),
        P(),
        P(),
    )
    return jax.shard_map(body, mesh=mesh, in_specs=in_specs, out_specs=out_specs, check_vma=False)
```

```python
from functools import partial

import jax
import jax.numpy as jnp
from jax import lax
from jax.experimental import pallas as pl
from jax.experimental.pallas import tpu as pltpu
from jax.sharding import Mesh
from jax.sharding import PartitionSpec as P

HD = 64
LEN = 1024
QBLK = 512
EPS = 1e-05
BLK = 256

NEG = -1e30
GRANT = 10 << 20
EXTRA = 128
BRIEF = pl.CostEstimate(flops=1, bytes_accessed=1, transcendentals=0)
f32 = jnp.float32
bf16 = jnp.bfloat16


def nt(left, right):
    return lax.dot_general(left, right, (((1,), (1,)), ((), ())), preferred_element_type=f32)


def nn(left, right):
    return lax.dot_general(left, right, (((1,), (0,)), ((), ())), preferred_element_type=f32)


def tn(left, right):
    return lax.dot_general(left, right, (((0,), (0,)), ((), ())), preferred_element_type=f32)


def attn_bias(block, j, first):
    q_pos = block * BLK + lax.broadcasted_iota(jnp.int32, (1, BLK), 1)
    k_pos = j * BLK + lax.broadcasted_iota(jnp.int32, (BLK, BLK), 0)
    return jnp.where((k_pos >= first) & (k_pos <= q_pos), 0.0, NEG)


def head_rows(refs, scratch, heads):
    lane = lax.broadcasted_iota(jnp.int32, (LEN, 2 * HD), 1)
    for ref, out in zip(refs, scratch):
        for h in range(heads):
            pair = ref[:, (h // 2) * 2 * HD : (h // 2 + 1) * 2 * HD]
            out[h] = jnp.where((lane < HD) == (h % 2 == 0), pair, jnp.zeros_like(pair))


def attn_fwd_body(info, q_ref, k_ref, v_ref, st_ref, o_ref, lse_ref, k_heads, v_turned):
    block = pl.program_id(0)
    heads = q_ref.shape[1] // HD
    first = st_ref[...]

    @pl.when(block == 0)
    def _():
        head_rows([k_ref], [k_heads], heads)
        for pair in range(heads // 2):
            turned = v_ref[:, pair * 2 * HD : (pair + 1) * 2 * HD].T
            for h in (0, 1):
                v_turned[2 * pair + h, :HD] = turned[h * HD : (h + 1) * HD]
                v_turned[2 * pair + h, HD:] = jnp.ones((16, LEN), bf16)

    def step(at, carry):
        j = block - at
        row = pl.multiple_of((j ^ info[0]) * BLK, BLK)
        bias = attn_bias(block, j, first)
        out = []
        for h in range(heads):
            top, acc = carry[h]
            query = q_ref[:, (h // 2) * 2 * HD : (h // 2 + 1) * 2 * HD]
            s = nt(k_heads[h, pl.ds(row, BLK), :], query) + bias
            new = jnp.maximum(top, jnp.max(s, axis=0, keepdims=True))
            p = jnp.exp(s - new).astype(bf16)
            acc = acc * jnp.exp(top - new) + nn(v_turned[h, :, pl.ds(row, BLK)], p)
            out.append((new, acc))
        return tuple(out)

    init = tuple((jnp.full((1, BLK), NEG, f32), jnp.zeros((HD + 16, BLK), f32)) for _ in range(heads))
    done = lax.fori_loop(0, block + 1 - info[1 + block], step, init)
    for pair in range(heads // 2):
        both = [acc[:HD] / acc[HD : HD + 1] for _, acc in done[2 * pair : 2 * pair + 2]]
        o_ref[:, pair * 2 * HD : (pair + 1) * 2 * HD] = jnp.concatenate(both, axis=0).T.astype(bf16)
    for h in range(heads):
        top, acc = done[h]
        lse_ref[h : h + 1, :] = top + jnp.log(acc[HD : HD + 1])


def attn_bwd_body(info, q_ref, k_ref, v_ref, st_ref, o_ref, lse_ref, do_ref, d_ref, k_heads, v_heads, dk_acc, dv_acc):
    block = pl.program_id(0)
    heads = q_ref.shape[1] // HD
    first = st_ref[...]
    lane = lax.broadcasted_iota(jnp.int32, (BLK, 2 * HD), 1)

    @pl.when(block == 0)
    def _():
        head_rows([k_ref, v_ref], [k_heads, v_heads], heads)
        dk_acc[...] = jnp.zeros_like(dk_acc)
        dv_acc[...] = jnp.zeros_like(dv_acc)

    deltas = []
    for pair in range(heads // 2):
        cols = slice(pair * 2 * HD, (pair + 1) * 2 * HD)
        turned = (do_ref[:, cols].astype(f32) * o_ref[:, cols].astype(f32)).T
        for h in (0, 1):
            deltas.append(jnp.sum(turned[h * HD : (h + 1) * HD], axis=0, keepdims=True))

    def step(j, dqs):
        row = pl.multiple_of((j ^ info[0]) * BLK, BLK)
        bias = attn_bias(block, j, first)
        out = list(dqs)
        for pair in range(heads // 2):
            cols = slice(pair * 2 * HD, (pair + 1) * 2 * HD)
            query, cot = q_ref[:, cols], do_ref[:, cols]
            dk = dk_acc[pl.ds(row, BLK), cols]
            dv = dv_acc[pl.ds(row, BLK), cols]
            for h in (2 * pair, 2 * pair + 1):
                mask = (lane < HD) == (h % 2 == 0)
                keys = k_heads[h, pl.ds(row, BLK), :]
                p = jnp.exp(nt(keys, query) + (bias - lse_ref[h : h + 1, :]))
                dp = nt(v_heads[h, pl.ds(row, BLK), :], cot)
                ds = (p * (dp - deltas[h])).astype(bf16)
                dv = dv + nn(p.astype(bf16), jnp.where(mask, cot, jnp.zeros_like(cot)))
                dk = dk + nn(ds, jnp.where(mask, query, jnp.zeros_like(query)))
                out[pair] = out[pair] + tn(ds, keys)
            dk_acc[pl.ds(row, BLK), cols] = dk
            dv_acc[pl.ds(row, BLK), cols] = dv
        return tuple(out)

    init = tuple(jnp.zeros((BLK, 2 * HD), f32) for _ in range(heads // 2))
    dqs = lax.fori_loop(info[1 + block], block + 1, step, init)
    here = pl.multiple_of((block ^ info[0]) * BLK, BLK)
    for pair in range(heads // 2):
        cols = slice(pair * 2 * HD, (pair + 1) * 2 * HD)
        d_ref[0, pl.ds(here, BLK), cols] = (dqs[pair] * HD**-0.5).astype(bf16)

    @pl.when(block == pl.num_programs(0) - 1)
    def _():
        d_ref[1] = dk_acc[...].astype(bf16)
        d_ref[2] = dv_acc[...].astype(bf16)


def attn_specs(width):
    small = pl.BlockSpec((BLK, width), lambda i, info: (i ^ info[0], 0))
    whole = pl.BlockSpec((LEN, width), lambda i, info: (0, 0))
    start = pl.BlockSpec((1, BLK), lambda i, info: (0, i ^ info[0]))
    lse = pl.BlockSpec((width // HD, BLK), lambda i, info: (0, i ^ info[0]))
    return small, whole, start, lse


def attn_fwd(info, query, keys, values, start):
    width = query.shape[1]
    heads = width // HD
    small, whole, first, lse = attn_specs(width)
    return pl.pallas_call(
        attn_fwd_body,
        out_shape=(jax.ShapeDtypeStruct(query.shape, bf16), jax.ShapeDtypeStruct((heads, LEN), f32)),
        grid_spec=pltpu.PrefetchScalarGridSpec(
            num_scalar_prefetch=1,
            grid=(LEN // BLK,),
            in_specs=[small, whole, whole, first],
            out_specs=[small, lse],
            scratch_shapes=[pltpu.VMEM((heads, LEN, 2 * HD), bf16), pltpu.VMEM((heads, HD + 16, LEN), bf16)],
        ),
        cost_estimate=BRIEF,
        compiler_params=pltpu.CompilerParams(vmem_limit_bytes=GRANT),
        name="attn_fwd",
    )(info, query, keys, values, start)


def attn_bwd(info, query, keys, values, start, out, lse, cot):
    width = query.shape[1]
    heads = width // HD
    small, whole, first, lse_spec = attn_specs(width)
    return pl.pallas_call(
        attn_bwd_body,
        out_shape=jax.ShapeDtypeStruct((3,) + query.shape, bf16),
        grid_spec=pltpu.PrefetchScalarGridSpec(
            num_scalar_prefetch=1,
            grid=(LEN // BLK,),
            in_specs=[small, whole, whole, first, small, lse_spec, small],
            out_specs=pl.BlockSpec((3, LEN, width), lambda i, info: (0, 0, 0)),
            scratch_shapes=[
                pltpu.VMEM((heads, LEN, 2 * HD), bf16),
                pltpu.VMEM((heads, LEN, 2 * HD), bf16),
                pltpu.VMEM((LEN, width), f32),
                pltpu.VMEM((LEN, width), f32),
            ],
        ),
        cost_estimate=BRIEF,
        compiler_params=pltpu.CompilerParams(vmem_limit_bytes=GRANT),
        name="attn_bwd",
    )(info, query, keys, values, start, out, lse, cot)


def up_body(a_ref, w_ref, b_ref, g_ref, s_ref):
    rows = a_ref[...]
    for part in range(w_ref.shape[1] // 256):
        cols = slice(part * 256, part * 256 + 256)
        u = nn(rows, w_ref[:, cols]) + b_ref[:, cols].astype(f32)
        size = jnp.abs(u)
        t = 1.0 / (1.0 + 0.3275911 * 0.7071067811865476 * size)
        poly = t * (0.5 * 0.254829592 + t * (0.5 * -0.284496736 + t * (0.5 * 1.421413741 + t * (0.5 * -1.453152027 + t * (0.5 * 1.061405429)))))
        bell = jnp.exp(-0.5 * u * u)
        tail = poly * bell
        cdf = jnp.where(u >= 0, 1.0 - tail, tail)
        g_ref[:, cols] = (u * cdf).astype(bf16)
        s_ref[:, cols] = (cdf + u * bell * 0.3989422804014327).astype(bf16)


def up_gelu(rows, weight, bias):
    m, k = rows.shape
    n = weight.shape[1]
    bm = 256
    shape = jax.ShapeDtypeStruct((m, n), bf16)
    tile = pl.BlockSpec((bm, n), lambda i: (i, 0))
    return pl.pallas_call(
        up_body,
        out_shape=(shape, shape),
        grid=(m // bm,),
        in_specs=[pl.BlockSpec((bm, k), lambda i: (i, 0)), pl.BlockSpec((k, n), lambda i: (0, 0)), pl.BlockSpec((1, n), lambda i: (0, 0))],
        out_specs=(tile, tile),
        cost_estimate=BRIEF,
        compiler_params=pltpu.CompilerParams(vmem_limit_bytes=GRANT),
        name="up_gelu",
    )(rows, weight, bias.reshape(1, n))


def const_spec(shape):
    return pl.BlockSpec(shape, lambda i: (0,) * len(shape))


def row_spec(rows, cols):
    return pl.BlockSpec((rows, cols), lambda i: (i, 0))


def project_body(a_ref, w_ref, b_ref, q_ref, k_ref, v_ref):
    rows = a_ref[...]
    q_ref[...] = (nn(rows, w_ref[0]) + b_ref[0:1].astype(f32)).astype(bf16) * jnp.bfloat16(HD**-0.5)
    k_ref[...] = nn(rows, w_ref[1]).astype(bf16)
    v_ref[...] = (nn(rows, w_ref[2]) + b_ref[1:2].astype(f32)).astype(bf16)


def project(rows, weight, bias):
    m, k = rows.shape
    n = weight.shape[2]
    tile = 256
    shape = jax.ShapeDtypeStruct((m, n), bf16)
    return pl.pallas_call(
        project_body,
        out_shape=(shape, shape, shape),
        grid=(m // tile,),
        in_specs=[row_spec(tile, k), const_spec(weight.shape), const_spec(bias.shape)],
        out_specs=[row_spec(tile, n)] * 3,
        cost_estimate=BRIEF,
        compiler_params=pltpu.CompilerParams(vmem_limit_bytes=GRANT),
        name="project",
    )(rows, weight, bias)


def sum_dots(product, lefts, rights):
    stacked = lefts[0].ndim == 3
    m, k = lefts[0].shape[-2:]
    n = rights[0].shape[-1] if product is nn else rights[0].shape[-2]
    terms = len(lefts)
    tile = 256
    steps = m // tile // 2

    def body(*refs):
        total = None
        for left, right in zip(refs[:terms], refs[terms : 2 * terms]):
            for at in range(left.shape[0] if stacked else 1):
                term = product(left[at], right[at]) if stacked else product(left[...], right[...])
                total = term if total is None else total + term
        here, there = refs[2 * terms :]

        @pl.when(pl.program_id(0) < steps)
        def _():
            there[...] = total.astype(bf16)

        @pl.when(pl.program_id(0) >= steps)
        def _():
            here[...] = total

    def turn(i):
        return jnp.where(i < steps, i + steps, i - steps)

    if stacked:
        left_spec = pl.BlockSpec((lefts[0].shape[0], tile, k), lambda i: (0, turn(i), 0))
    else:
        left_spec = pl.BlockSpec((tile, k), lambda i: (turn(i), 0))
    return pl.pallas_call(
        body,
        out_shape=(jax.ShapeDtypeStruct((m // 2, n), f32), jax.ShapeDtypeStruct((m // 2, n), bf16)),
        grid=(2 * steps,),
        in_specs=[left_spec] * terms + [const_spec(r.shape) for r in rights],
        out_specs=[
            pl.BlockSpec((tile, n), lambda i: (jnp.maximum(i - steps, 0), 0)),
            pl.BlockSpec((tile, n), lambda i: (jnp.minimum(i, steps - 1), 0)),
        ],
        cost_estimate=BRIEF,
        compiler_params=pltpu.CompilerParams(vmem_limit_bytes=GRANT),
        name="sum_dots",
    )(*lefts, *rights)


def center_rows(rows):
    center = rows - jnp.mean(rows, axis=-1, keepdims=True)
    scale = lax.rsqrt(jnp.mean(center * center, axis=-1, keepdims=True) + EPS)
    return center * scale, scale


def first_norm_body(x_ref, g_ref, gain_ref, shift_ref, a_ref, sum_ref):
    normal, _ = center_rows(x_ref[...].astype(f32))
    a_ref[...] = (normal * gain_ref[...] + shift_ref[...]).astype(bf16)

    @pl.when(pl.program_id(0) == 0)
    def _():
        sum_ref[...] = jnp.zeros_like(sum_ref)

    sum_ref[...] += jnp.sum(g_ref[...].astype(f32), axis=0, keepdims=True)


def first_norm(tokens, cotangent, gain, shift):
    m, d = tokens.shape
    tile = 128
    return pl.pallas_call(
        first_norm_body,
        out_shape=(jax.ShapeDtypeStruct((m, d), bf16), jax.ShapeDtypeStruct((1, d), f32)),
        grid=(m // tile,),
        in_specs=[row_spec(tile, d), row_spec(tile, d), const_spec((1, d)), const_spec((1, d))],
        out_specs=[row_spec(tile, d), const_spec((1, d))],
        cost_estimate=BRIEF,
        compiler_params=pltpu.CompilerParams(vmem_limit_bytes=GRANT),
        name="first_norm",
    )(tokens, cotangent, gain, shift)


def second_norm_body(x_ref, here_ref, came_ref, b_ref, gain_ref, shift_ref, h_ref, a_ref):
    mixed = x_ref[...].astype(f32) + (here_ref[...] + came_ref[...].astype(f32)) + b_ref[...].astype(f32)
    h_ref[...] = mixed
    normal, _ = center_rows(mixed)
    a_ref[...] = (normal * gain_ref[...] + shift_ref[...]).astype(bf16)


def second_norm(tokens, here, came, bias, gain, shift):
    m, d = tokens.shape
    tile = 128
    return pl.pallas_call(
        second_norm_body,
        out_shape=(jax.ShapeDtypeStruct((m, d), f32), jax.ShapeDtypeStruct((m, d), bf16)),
        grid=(m // tile,),
        in_specs=[row_spec(tile, d)] * 3 + [const_spec((1, d))] * 3,
        out_specs=[row_spec(tile, d)] * 2,
        cost_estimate=BRIEF,
        compiler_params=pltpu.CompilerParams(vmem_limit_bytes=GRANT),
        name="second_norm",
    )(tokens, here, came, bias, gain, shift)


def norm_back_body(v_ref, here_ref, low_came_ref, high_came_ref, gain_ref, res_ref, out_ref, low_ref, sums_ref):
    normal, scale = center_rows(v_ref[...].astype(f32))
    first = pl.program_id(0) < pl.num_programs(0) // 2
    came = jnp.where(first, low_came_ref[...], high_came_ref[...])
    grad = here_ref[...] + came.astype(f32)
    scaled = grad * gain_ref[...]
    inner = jnp.mean(scaled * normal, axis=-1, keepdims=True)
    back = scale * (scaled - jnp.mean(scaled, axis=-1, keepdims=True) - normal * inner)
    back = back + res_ref[...].astype(f32)
    low = back.astype(bf16)
    out_ref[...] = back
    low_ref[...] = low

    @pl.when(pl.program_id(0) == 0)
    def _():
        sums_ref[...] = jnp.zeros_like(sums_ref)

    sums_ref[0:1] += jnp.sum(grad * normal, axis=0, keepdims=True)
    sums_ref[1:2] += jnp.sum(grad, axis=0, keepdims=True)
    sums_ref[2:3] += jnp.sum(low.astype(f32), axis=0, keepdims=True)


def norm_back(values, here, came, gain, residual):
    m, d = values.shape
    tile = 128
    half = m // tile // 2
    low = pl.BlockSpec((tile, d), lambda i: (jnp.minimum(i, half - 1), 0))
    high = pl.BlockSpec((tile, d), lambda i: (jnp.maximum(i - half, 0), 0))
    return pl.pallas_call(
        norm_back_body,
        out_shape=(
            jax.ShapeDtypeStruct((m, d), f32),
            jax.ShapeDtypeStruct((m, d), bf16),
            jax.ShapeDtypeStruct((8, d), f32),
        ),
        grid=(m // tile,),
        in_specs=[row_spec(tile, d)] * 2 + [low, high, const_spec((1, d)), row_spec(tile, d)],
        out_specs=[row_spec(tile, d)] * 2 + [const_spec((8, d))],
        cost_estimate=BRIEF,
        compiler_params=pltpu.CompilerParams(vmem_limit_bytes=GRANT),
        name="norm_back",
    )(values, here, *came, gain, residual)


def back_act_body(z_ref, w_ref, s_ref, du_ref, sum_ref):
    du = (nt(z_ref[...], w_ref[...]) * s_ref[...].astype(f32)).astype(bf16)
    du_ref[...] = du

    @pl.when(pl.program_id(0) == 0)
    def _():
        sum_ref[...] = jnp.zeros_like(sum_ref)

    sum_ref[...] += jnp.sum(du.astype(f32), axis=0, keepdims=True)


def back_act(cotangent, weight, slope):
    m, d = cotangent.shape
    n = weight.shape[0]
    tile = 256
    return pl.pallas_call(
        back_act_body,
        out_shape=(jax.ShapeDtypeStruct((m, n), bf16), jax.ShapeDtypeStruct((1, n), f32)),
        grid=(m // tile,),
        in_specs=[row_spec(tile, d), const_spec((n, d)), row_spec(tile, n)],
        out_specs=[row_spec(tile, n), const_spec((1, n))],
        cost_estimate=BRIEF,
        compiler_params=pltpu.CompilerParams(vmem_limit_bytes=GRANT),
        name="back_act",
    )(cotangent, weight, slope)


def frame_sums_body(a_ref, d_ref, o_ref, g_ref, one_ref, two_ref, sums_ref, a_turned):
    rows, width = g_ref.shape[1], o_ref.shape[1]
    count = rows // width
    a_turned[...] = a_ref[...].T
    for at in range(4 * count):
        kind, part = divmod(at, count)
        out = one_ref if at < 2 * count else two_ref
        if kind < 3:
            block = nn(a_turned[part * width : (part + 1) * width, :], d_ref[kind])
        else:
            block = tn(o_ref[...], g_ref[:, part * width : (part + 1) * width])
        low = (at % (2 * count)) * width
        out[low : low + width, :] = block.astype(bf16)
    two_ref[2 * rows :, :] = jnp.zeros((EXTRA, width), bf16)
    for kind in range(3):
        sums_ref[kind] = jnp.sum(d_ref[kind].astype(f32), axis=0, keepdims=True)


def frame_sums(rows, trio, out, cotangent):
    t, d = rows.shape
    n = trio.shape[2]
    half = jax.ShapeDtypeStruct((2 * d, n), bf16)
    one, two, sums = pl.pallas_call(
        frame_sums_body,
        out_shape=(half, jax.ShapeDtypeStruct((2 * d + EXTRA, n), bf16), jax.ShapeDtypeStruct((3, 1, n), f32)),
        grid=(1,),
        in_specs=[const_spec((t, d)), const_spec((3, t, n)), const_spec((t, n)), const_spec((t, d))],
        out_specs=[const_spec((2 * d, n)), const_spec((2 * d + EXTRA, n)), const_spec((3, 1, n))],
        scratch_shapes=[pltpu.VMEM((d, t), bf16)],
        cost_estimate=BRIEF,
        compiler_params=pltpu.CompilerParams(vmem_limit_bytes=GRANT),
        name="frame_sums",
    )(rows, trio, out, cotangent)
    return (one, two), sums


def frames_body(a_ref, g_ref, out_ref, turned):
    tile = out_ref.shape[0]
    turned[...] = a_ref[...].T
    out_ref[...] = nn(turned[...], g_ref[...]).astype(bf16)


def across_frames(left, right):
    t, m = left.shape
    n = right.shape[1]
    tile = 256
    return pl.pallas_call(
        frames_body,
        out_shape=jax.ShapeDtypeStruct((m, n), bf16),
        grid=(m // tile,),
        in_specs=[pl.BlockSpec((t, tile), lambda i: (0, i)), const_spec((t, n))],
        out_specs=row_spec(tile, n),
        scratch_shapes=[pltpu.VMEM((tile, t), bf16)],
        cost_estimate=BRIEF,
        compiler_params=pltpu.CompilerParams(vmem_limit_bytes=GRANT),
        name="across_frames",
    )(left, right)


def turn_back_body(a_ref, w_ref, out_ref):
    out_ref[...] = nt(a_ref[...], w_ref[...]).astype(bf16)


def turn_back(rows, weight):
    m, k = rows.shape
    n = weight.shape[0]
    tile = 256
    return pl.pallas_call(
        turn_back_body,
        out_shape=jax.ShapeDtypeStruct((m, n), bf16),
        grid=(m // tile,),
        in_specs=[row_spec(tile, k), const_spec((n, k))],
        out_specs=row_spec(tile, n),
        cost_estimate=BRIEF,
        compiler_params=pltpu.CompilerParams(vmem_limit_bytes=GRANT),
        name="turn_back",
    )(rows, weight)


def side_sum_body(info, *refs):
    total = refs[0][0].astype(f32)
    for ref in refs[1:-1]:
        total = total + (ref[0] if len(ref.shape) == 3 else ref[...]).astype(f32)
    refs[-1][...] = total.astype(bf16)


def side_sum(side, own, got, near=None):
    _, rows, cols = own.shape
    tile = rows // 4
    pick_spec = pl.BlockSpec((1, tile, cols), lambda i, info: (info[0], i, 0))
    flat = pl.BlockSpec((tile, cols), lambda i, info: (i, 0))
    args = [own, got] + ([] if near is None else [near])
    return pl.pallas_call(
        side_sum_body,
        out_shape=jax.ShapeDtypeStruct((rows, cols), bf16),
        grid_spec=pltpu.PrefetchScalarGridSpec(
            num_scalar_prefetch=1,
            grid=(4,),
            in_specs=[pick_spec, pick_spec] + [flat] * (len(args) - 2),
            out_specs=flat,
        ),
        cost_estimate=BRIEF,
        compiler_params=pltpu.CompilerParams(vmem_limit_bytes=GRANT),
        name="side_sum",
    )(side[None], *args)


def add_low_body(a_ref, b_ref, out_ref):
    out_ref[...] = (a_ref[...].astype(f32) + b_ref[...].astype(f32)).astype(bf16)


def add_low(left, right):
    rows, cols = left.shape
    tile = rows // 2
    return pl.pallas_call(
        add_low_body,
        out_shape=jax.ShapeDtypeStruct((rows, cols), bf16),
        grid=(2,),
        in_specs=[row_spec(tile, cols)] * 2,
        out_specs=row_spec(tile, cols),
        cost_estimate=BRIEF,
        compiler_params=pltpu.CompilerParams(vmem_limit_bytes=GRANT),
        name="add_low",
    )(left, right)


def quarter_sums_body(info, own_ref, got_ref, near_ref, send_ref, keep_ref):
    total = own_ref[0, 0].astype(f32) + got_ref[0, 0].astype(f32) + near_ref[0].astype(f32)

    @pl.when(pl.program_id(0) == 0)
    def _():
        send_ref[...] = total.astype(bf16)

    @pl.when(pl.program_id(0) == 1)
    def _():
        keep_ref[...] = total.astype(bf16)


def quarter_sums(place, own, got, near):
    _, rows, cols = own.shape
    rows = rows // 2
    tile = rows // 2
    deep = pl.BlockSpec((1, 1, tile, cols), lambda f, i, info: (info[0], info[1] ^ 1 ^ f, i, 0))
    flat = pl.BlockSpec((1, tile, cols), lambda f, i, info: (info[1] ^ 1 ^ f, i, 0))
    shape = jax.ShapeDtypeStruct((rows, cols), bf16)
    return pl.pallas_call(
        quarter_sums_body,
        out_shape=(shape, shape),
        grid_spec=pltpu.PrefetchScalarGridSpec(
            num_scalar_prefetch=1,
            grid=(2, 2),
            in_specs=[deep, deep, flat],
            out_specs=[
                pl.BlockSpec((tile, cols), lambda f, i, info: (jnp.where(f == 0, i, 1), 0)),
                pl.BlockSpec((tile, cols), lambda f, i, info: (jnp.where(f == 0, 0, i), 0)),
            ],
        ),
        cost_estimate=BRIEF,
        compiler_params=pltpu.CompilerParams(vmem_limit_bytes=GRANT),
        name="quarter_sums",
    )(place, own.reshape(2, 2, rows, cols), got.reshape(2, 2, rows, cols), near.reshape(2, rows, cols))


def settle_body(info, *refs):
    for at in range(4):

        @pl.when(pl.program_id(0) == at)
        def _(at=at):
            refs[4][0] = refs[at][...].astype(f32)


def settle(place, *pieces, extra=0):
    rows, cols = pieces[0].shape
    tile = rows // 2

    def spec(at):
        return pl.BlockSpec(
            (tile, cols), lambda f, i, info: (jnp.where(f == at, i, jnp.where(f < at, 0, 1)), 0)
        )

    def out_map(f, i, info):
        return (2 * (info[0] ^ (f // 2)) + (info[1] ^ (f % 2)), i, 0)

    out = pl.pallas_call(
        settle_body,
        out_shape=jax.ShapeDtypeStruct((4 + extra // rows, rows, cols), f32),
        grid_spec=pltpu.PrefetchScalarGridSpec(
            num_scalar_prefetch=1,
            grid=(4, 2),
            in_specs=[spec(at) for at in range(4)],
            out_specs=pl.BlockSpec((1, tile, cols), out_map),
        ),
        cost_estimate=BRIEF,
        compiler_params=pltpu.CompilerParams(vmem_limit_bytes=GRANT),
        name="settle",
    )(place, *pieces)
    return out.reshape(-1, cols)


def norm_rows(values, gain, shift):
    center = values - jnp.mean(values, axis=-1, keepdims=True)
    spread = jnp.mean(center * center, axis=-1, keepdims=True)
    return center * lax.rsqrt(spread + EPS) * gain + shift


def split_heads(flat, rows):
    return flat.reshape(rows, LEN, flat.shape[1] // HD, HD)


def block_scores(query, keys, seg_q, seg_k, offset):
    scores = jnp.einsum(
        "rqhd,rkhd->rhqk", query, keys, preferred_element_type=jnp.float32
    ) * HD ** (-0.5)
    q_pos = offset + jnp.arange(query.shape[1], dtype=jnp.int32)
    k_pos = jnp.arange(keys.shape[1], dtype=jnp.int32)
    allowed = (seg_q[:, :, None] == seg_k[:, None, :]) & (
        k_pos[None, None, :] <= q_pos[None, :, None]
    )
    return jnp.where(allowed[:, None], scores, -1e30)


def attention_forward(query, keys, values, seg_all):
    rows = query.shape[0] // LEN
    q4 = split_heads(query, rows)
    k4 = split_heads(keys, rows)
    v4 = split_heads(values, rows)
    seg2 = seg_all.reshape(rows, LEN)
    outputs = []
    totals = []
    for block in range(LEN // QBLK):
        first = block * QBLK
        end = first + QBLK
        scores = block_scores(
            q4[:, first:end], k4[:, :end], seg2[:, first:end], seg2[:, :end], first
        )
        top = jnp.max(scores, axis=-1, keepdims=True)
        expd = jnp.exp(scores - top)
        summed = jnp.sum(expd, axis=-1, keepdims=True)
        weights = (expd / summed).astype(jnp.bfloat16)
        outputs.append(
            jnp.einsum("rhqk,rkhd->rqhd", weights, v4[:, :end], preferred_element_type=jnp.float32)
        )
        totals.append(top + jnp.log(summed))
    attended = jnp.concatenate(outputs, axis=1).reshape(query.shape).astype(jnp.bfloat16)
    return (attended, totals)


def attention_backward(query, keys, values, seg_all, totals, grad_att):
    rows = query.shape[0] // LEN
    q4 = split_heads(query, rows)
    k4 = split_heads(keys, rows)
    v4 = split_heads(values, rows)
    g4 = split_heads(grad_att, rows)
    seg2 = seg_all.reshape(rows, LEN)
    scale = HD ** (-0.5)
    grad_k = jnp.zeros(k4.shape, jnp.float32)
    grad_v = jnp.zeros(v4.shape, jnp.float32)
    grad_q_parts = []
    for block in range(LEN // QBLK):
        first = block * QBLK
        end = first + QBLK
        scores = block_scores(
            q4[:, first:end], k4[:, :end], seg2[:, first:end], seg2[:, :end], first
        )
        probs = jnp.exp(scores - totals[block])
        weights = probs.astype(jnp.bfloat16)
        grad_w = jnp.einsum(
            "rqhd,rkhd->rhqk", g4[:, first:end], v4[:, :end], preferred_element_type=jnp.float32
        )
        delta = jnp.sum(probs * grad_w, axis=-1, keepdims=True)
        grad_s = (probs * (grad_w - delta)).astype(jnp.bfloat16)
        grad_q_parts.append(
            jnp.einsum("rhqk,rkhd->rqhd", grad_s, k4[:, :end], preferred_element_type=jnp.float32)
            * scale
        )
        padding = ((0, 0), (0, LEN - end), (0, 0), (0, 0))
        grad_k = grad_k + jnp.pad(
            jnp.einsum(
                "rhqk,rqhd->rkhd", grad_s, q4[:, first:end], preferred_element_type=jnp.float32
            )
            * scale,
            padding,
        )
        grad_v = grad_v + jnp.pad(
            jnp.einsum(
                "rhqk,rqhd->rkhd", weights, g4[:, first:end], preferred_element_type=jnp.float32
            ),
            padding,
        )
    shape = query.shape
    grad_q = jnp.concatenate(grad_q_parts, axis=1).reshape(shape).astype(jnp.bfloat16)
    return (
        grad_q,
        grad_k.reshape(shape).astype(jnp.bfloat16),
        grad_v.reshape(shape).astype(jnp.bfloat16),
    )


def tensor_parallel_shards(
    tokens,
    segment_ids,
    w_qkv,
    b_qv,
    w_out,
    b_out,
    w_up,
    b_up,
    w_down,
    b_down,
    ln_gain,
    ln_bias,
    out_grad,
):
    resid = tokens.astype(jnp.float32)
    qv_bias = b_qv.astype(jnp.float32)
    up_bias = b_up.astype(jnp.float32)
    local_rows = tokens.shape[0]
    normed, first_back = jax.vjp(norm_rows, resid, ln_gain[0], ln_bias[0])
    lowered = normed.astype(jnp.bfloat16)
    joined, seg_all = (
        lax.all_gather(lowered, "mp", axis=0, tiled=True),
        lax.all_gather(segment_ids, "mp", axis=0, tiled=True),
    )
    query = (jnp.dot(joined, w_qkv[0], preferred_element_type=jnp.float32) + qv_bias[0]).astype(
        jnp.bfloat16
    )
    keys = jnp.dot(joined, w_qkv[1], preferred_element_type=jnp.float32).astype(jnp.bfloat16)
    values = (jnp.dot(joined, w_qkv[2], preferred_element_type=jnp.float32) + qv_bias[1]).astype(
        jnp.bfloat16
    )
    query, keys, values = (query, keys, values)
    attended, totals = attention_forward(query, keys, values, seg_all)
    attn_sum = lax.psum_scatter(
        jnp.dot(attended, w_out, preferred_element_type=jnp.float32).astype(jnp.bfloat16),
        "mp",
        scatter_dimension=0,
        tiled=True,
    ).astype(jnp.float32)
    mixed = resid + attn_sum + b_out.astype(jnp.float32)
    normed2, second_back = jax.vjp(norm_rows, mixed, ln_gain[1], ln_bias[1])
    lowered2 = normed2.astype(jnp.bfloat16)
    joined2 = lax.all_gather(lowered2, "mp", axis=0, tiled=True)
    pre_act = jnp.dot(joined2, w_up, preferred_element_type=jnp.float32) + up_bias
    pre_act, activ = (pre_act, jax.nn.gelu(pre_act, approximate=False).astype(jnp.bfloat16))
    block_out = (
        mixed
        + lax.psum_scatter(
            jnp.dot(activ, w_down, preferred_element_type=jnp.float32).astype(jnp.bfloat16),
            "mp",
            scatter_dimension=0,
            tiled=True,
        ).astype(jnp.float32)
        + b_down.astype(jnp.float32)
    ).astype(jnp.bfloat16)
    grad_y = out_grad.astype(jnp.float32)
    grad_z = lax.all_gather(out_grad, "mp", axis=0, tiled=True)
    grad_down = jnp.einsum("tf,td->fd", activ, grad_z, preferred_element_type=jnp.float32)
    grad_bdown = jnp.sum(grad_z, axis=0, dtype=jnp.float32)
    grad_act = jnp.einsum("td,fd->tf", grad_z, w_down, preferred_element_type=jnp.float32)
    gelu_back = jax.vjp(lambda value: jax.nn.gelu(value, approximate=False), pre_act)[1]
    grad_pre = gelu_back(grad_act)[0].astype(jnp.bfloat16)
    grad_up = jnp.einsum("td,tf->df", joined2, grad_pre, preferred_element_type=jnp.float32)
    grad_bup = jnp.sum(grad_pre, axis=0, dtype=jnp.float32)
    grad_n2 = lax.psum_scatter(
        jnp.einsum("tf,df->td", grad_pre, w_up, preferred_element_type=jnp.float32).astype(
            jnp.bfloat16
        ),
        "mp",
        scatter_dimension=0,
        tiled=True,
    ).astype(jnp.float32)
    grad_h, grad_g2, grad_s2 = second_back(grad_n2)
    grad_h = grad_h + grad_y
    grad_branch = lax.all_gather(grad_h.astype(jnp.bfloat16), "mp", axis=0, tiled=True)
    grad_wout = jnp.einsum("tc,td->cd", attended, grad_branch, preferred_element_type=jnp.float32)
    grad_bout = jnp.sum(grad_branch, axis=0, dtype=jnp.float32)
    grad_att = jnp.einsum(
        "td,cd->tc", grad_branch, w_out, preferred_element_type=jnp.float32
    ).astype(jnp.bfloat16)
    grad_q, grad_k, grad_v = attention_backward(query, keys, values, seg_all, totals, grad_att)
    grad_qkv = jnp.stack(
        [
            jnp.einsum("td,tc->dc", joined, piece, preferred_element_type=jnp.float32)
            for piece in (grad_q, grad_k, grad_v)
        ]
    )
    grad_bqv = jnp.stack(
        [jnp.sum(grad_q, axis=0, dtype=jnp.float32), jnp.sum(grad_v, axis=0, dtype=jnp.float32)]
    )
    summed = jnp.zeros((local_rows * lax.axis_size("mp"), w_qkv.shape[1]), jnp.float32)
    for index, piece in enumerate((grad_q, grad_k, grad_v)):
        summed = summed + jnp.einsum(
            "tc,dc->td", piece, w_qkv[index], preferred_element_type=jnp.float32
        )
    grad_n1 = lax.psum_scatter(
        summed.astype(jnp.bfloat16), "mp", scatter_dimension=0, tiled=True
    ).astype(jnp.float32)
    grad_x, grad_g1, grad_s1 = first_back(grad_n1)
    grad_in = grad_x + grad_h
    weight_totals = (
        lax.psum(grad_qkv.astype(jnp.bfloat16), "dp").astype(jnp.float32),
        lax.psum(grad_bqv.astype(jnp.bfloat16), "dp").astype(jnp.float32),
        lax.psum(grad_wout.astype(jnp.bfloat16), "dp").astype(jnp.float32),
        lax.psum(grad_bout.astype(jnp.bfloat16), "dp").astype(jnp.float32),
        lax.psum(grad_up.astype(jnp.bfloat16), "dp").astype(jnp.float32),
        lax.psum(grad_bup.astype(jnp.bfloat16), "dp").astype(jnp.float32),
        lax.psum(grad_down.astype(jnp.bfloat16), "dp").astype(jnp.float32),
        lax.psum(grad_bdown.astype(jnp.bfloat16), "dp").astype(jnp.float32),
    )
    norm_totals = lax.psum(
        (jnp.stack([grad_g1, grad_g2]), jnp.stack([grad_s1, grad_s2])), ("dp", "mp")
    )
    return (block_out, grad_in) + tuple(weight_totals) + tuple(norm_totals)


def row_per_chip(mesh):
    return mesh.shape["mp"] == 4 and mesh.shape["dp"] == 8


def swap(value, axis):
    return lax.ppermute(value, axis, [(0, 1), (1, 0)])


def core(value):
    return swap(value, "core")


def cross(value):
    return swap(value, "x")


def after(value, *others):
    return lax.optimization_barrier((value,) + others)[0]


def take(value, at):
    return lax.dynamic_index_in_dim(value, at, 0, keepdims=False)


def place(whole, piece, at):
    return lax.dynamic_update_index_in_dim(whole, piece, at, 0)


def quarter_of(weight):
    me = lax.axis_index("y") + 2 * (lax.axis_index("z") & 1)
    return take(weight.reshape(4, -1, weight.shape[-1]), me)


def share(mine):
    out = [swap(mine, "y")]
    for bits in (2, 3):
        out.append(lax.ppermute(mine, ("z", "y"), [(i, i ^ bits) for i in range(8)]))
    return out


def assemble(mine, others):
    me = lax.axis_index("y") + 2 * (lax.axis_index("z") & 1)
    whole = place(jnp.zeros((4,) + mine.shape, mine.dtype), mine, me)
    for bits, piece in zip((1, 2, 3), others):
        whole = place(whole, piece, me ^ bits)
    return whole.reshape(-1, mine.shape[-1])


def swap_z(value, bits):
    return lax.ppermute(value, "z", [(i, i ^ bits) for i in range(4)])


def by_side(value):
    return value.reshape(2, value.shape[0] // 2, value.shape[1])


class Line:
    def __init__(self):
        self.last = None

    def __call__(self, function, *args):
        if self.last is not None:
            args, _ = lax.optimization_barrier((args, self.last))
        out = function(*args)
        self.last = jax.tree.leaves(out)[0]
        return out


def row_per_chip_shards(
    tokens,
    segment_ids,
    w_qkv,
    b_qv,
    w_out,
    b_out,
    w_up,
    b_up,
    w_down,
    b_down,
    ln_gain,
    ln_bias,
    out_grad,
):
    side, here_y = lax.axis_index("core"), lax.axis_index("y")
    place = jnp.stack([here_y, lax.axis_index("z") & 1]).astype(jnp.int32)
    width, wide = b_qv.shape[1], tokens.shape[1]
    gains, shifts = ln_gain[:, None], ln_bias[:, None]
    line = Line()

    def pair(*parts):
        return line(lambda *all: jnp.concatenate(all), *parts)

    qkv_mine = cross(line(quarter_of, w_qkv.reshape(-1, width)))
    a1_own, sum_dz = line(first_norm, tokens, out_grad, gains[0], shifts[0])
    a1_came = core(a1_own)
    seg_other = core(segment_ids)
    small = cross(jnp.concatenate([b_qv.reshape(-1), b_up]))
    up_quarter = line(quarter_of, w_up)
    down_quarter = line(quarter_of, w_down)

    def ranges(mine, other):
        seg = jnp.concatenate([mine, other])
        start = jnp.sum((seg[None, :] < seg[:, None]).astype(jnp.int32), axis=1)[None]
        ordered = jnp.where(side == 0, seg, jnp.concatenate([other, mine]))
        blocks = ordered.reshape(LEN // BLK, BLK)
        low = jnp.sum((blocks[None, :, -1] < blocks[:, None, 0]).astype(jnp.int32), axis=1)
        return start, jnp.concatenate([(side * (LEN // BLK // 2))[None].astype(jnp.int32), low])

    start, info = line(ranges, segment_ids, seg_other)
    a1 = pair(a1_own, a1_came)
    own = tuple(line(project, a1, w_qkv, b_qv))
    qkv_mine, w_out_now, up_quarter, _ = lax.optimization_barrier((qkv_mine, w_out, up_quarter, own[0]))
    qkv_parts = share(qkv_mine)
    out_other = cross(w_out_now)
    up_mine = cross(up_quarter)
    own = own + tuple(line(partial(attn_fwd, info), *own, start))
    up_mine, down_quarter, _ = lax.optimization_barrier((up_mine, down_quarter, own[3]))
    up_parts = share(up_mine)
    down_mine = cross(down_quarter)
    qkv_other = line(assemble, qkv_mine, qkv_parts).reshape(w_qkv.shape)
    other = tuple(line(project, a1, qkv_other, small[: 2 * width].reshape(2, width)))
    other = other + tuple(line(partial(attn_fwd, info), *other, start))
    down_mine, dz_own, _ = lax.optimization_barrier((down_mine, out_grad, other[3]))
    down_parts = share(down_mine)
    dz_came = core(dz_own)

    here, there = line(partial(sum_dots, nn), [own[3], other[3]], [w_out, out_other])
    came = core(there)
    up_other = line(assemble, up_mine, up_parts)
    mixed, a2_own = line(second_norm, tokens, here, came, b_out[None], gains[1], shifts[1])
    a2_came = core(a2_own)
    dz = pair(dz_own, dz_came)
    a2 = pair(a2_own, a2_came)

    def core_halves(value):
        half = value.shape[0] // 2
        return core(value[:half]), core(value[half:])

    act_other, slope_other = line(up_gelu, a2, up_other, small[2 * width :])
    down_got = cross(line(across_frames, act_other, dz))
    act_own, slope_own = line(up_gelu, a2, w_up, b_up)
    down_own = line(across_frames, act_own, dz)
    du_own, sum_up_own = line(back_act, dz, w_down, slope_own)
    down_other = line(assemble, down_mine, down_parts)
    du_other, sum_up_other = line(back_act, dz, down_other, slope_other)
    here, there = line(partial(sum_dots, nt), [du_own, du_other], [w_up, up_other])
    came = core_halves(there)
    up_got = cross(line(across_frames, a2, du_other))
    grad_h, dattn_own, sums_h = line(norm_back, mixed, here, came, gains[1], out_grad)
    dattn_came = core_halves(dattn_own)
    up_own = line(across_frames, a2, du_own)

    def spread_y(own, got):
        return swap(line(side_sum, 1 - here_y, own, got), "y")

    def near_z(own, got, near):
        send, keep = line(quarter_sums, place, own, got, near)
        return keep, swap_z(send, 1)

    def far_z(keep, came):
        low = line(add_low, keep, came)
        return low, swap_z(low, 2)

    def back_z(low, came):
        mine = line(add_low, low, came)
        near = swap_z(mine, 1)
        return mine, near, swap(mine, "y"), swap(near, "y")

    down_own, down_got = by_side(down_own), by_side(down_got)
    down_near = spread_y(down_own, down_got)
    dattn = pair(dattn_own, *dattn_came)

    def back(entry, weight):
        query, keys, values, out, lse = entry
        cot = line(turn_back, dattn, weight)
        trio = line(partial(attn_bwd, info), query, keys, values, start, out, lse, cot)
        return (trio,) + tuple(line(frame_sums, a1, trio, out, dattn))

    trio_other, attn_other, sum_trio_other = back(other, out_other)
    first_got = cross(attn_other[0])
    down_sum = near_z(down_own, down_got, down_near)
    trio_own, attn_own, sum_trio_own = back(own, w_out)
    up_own, up_got = by_side(up_own), by_side(up_got)
    up_near = spread_y(up_own, up_got)
    down_sum = far_z(*down_sum)
    here, there = line(partial(sum_dots, nt), [trio_own, trio_other], [w_qkv, qkv_other])
    came = core_halves(there)
    y_here, y_there = line(partial(sum_dots, nn), [act_own, act_other], [w_down, down_other])
    y_came = core(y_there)
    first_own, first_got = by_side(attn_own[0]), by_side(first_got)
    first_near = spread_y(first_own, first_got)
    grad_in, _, sums_x = line(norm_back, tokens, here, came, gains[0], grad_h)
    common = line(
        lambda h, z, x: jnp.concatenate([h[2], z[0], x[0], h[0], x[1], h[1]]), sums_h, sum_dz, sums_x
    )
    common_came = core(common)

    def finish(mixed, here, came):
        return (mixed + here + came.astype(f32) + b_down.astype(f32)).astype(bf16)

    block_out = line(finish, mixed, y_here, y_came)

    def ride(whole, trio, up, mine, came):
        vector = jnp.concatenate([trio[0, 0], trio[2, 0], up[0], mine + came])
        return lax.dynamic_update_slice(whole, vector.astype(bf16).reshape(-1, width), (2 * wide, 0))

    second_other = line(ride, attn_other[1], sum_trio_other, sum_up_other, common, common_came)
    second_got = cross(second_other)
    down_sum = back_z(*down_sum)
    second_own = line(ride, attn_own[1], sum_trio_own, sum_up_own, common, common_came)
    up_sum = near_z(up_own, up_got, up_near)
    first_sum = near_z(first_own, first_got, first_near)
    second_own, second_got = by_side(second_own), by_side(second_got)
    second_near = spread_y(second_own, second_got)
    up_sum = far_z(*up_sum)
    first_sum = far_z(*first_sum)
    second_sum = near_z(second_own, second_got, second_near)
    up_sum = back_z(*up_sum)
    second_sum = far_z(*second_sum)
    first_sum = back_z(*first_sum)
    grad_down = line(settle, place, *down_sum)
    second_sum = back_z(*second_sum)
    grad_up = line(settle, place, *up_sum)
    first = line(partial(settle, extra=wide), place, *first_sum)
    second = line(settle, place, *second_sum)
    grad_qkv = lax.dynamic_update_slice(first, second[:wide], (2 * wide, 0)).reshape(w_qkv.shape)
    grad_wout = jnp.swapaxes(second[wide : 2 * wide].reshape(-1, w_out.shape[0], width), 0, 1)
    grad_wout = grad_wout.reshape(w_out.shape)
    vector = second[2 * wide :].reshape(-1)
    units = b_up.shape[0]
    ends = [2 * width, units, wide, wide, 2 * wide, 2 * wide]
    cuts = [sum(ends[:i]) for i in range(len(ends) + 1)]
    grad_bqv, grad_bup, grad_bout, grad_bdown, grad_gain, grad_shift = [
        vector[low:high] for low, high in zip(cuts[:-1], cuts[1:])
    ]
    return (
        block_out,
        grad_in,
        grad_qkv,
        grad_bqv.reshape(b_qv.shape),
        grad_wout,
        grad_bout,
        grad_up,
        grad_bup,
        grad_down,
        grad_bdown,
        grad_gain.reshape(ln_gain.shape),
        grad_shift.reshape(ln_bias.shape),
    )


def solution(mesh):
    rows, frames = ("dp", "mp"), "mp"
    body = tensor_parallel_shards
    if row_per_chip(mesh):
        shape = (mesh.shape["dp"] // 2, 2, mesh.shape["mp"] // 2, 2)
        mesh = Mesh(mesh.devices.reshape(shape), ("z", "y", "x", "core"))
        rows, frames = ("z", "y", "x", "core"), ("x", "core")
        body = row_per_chip_shards
    in_specs = (
        P(rows, None),
        P(rows),
        P(None, None, frames),
        P(None, frames),
        P(frames, None),
        P(),
        P(None, frames),
        P(frames),
        P(frames, None),
        P(),
        P(),
        P(),
        P(rows, None),
    )
    out_specs = (
        P(rows, None),
        P(rows, None),
        P(None, None, frames),
        P(None, frames),
        P(frames, None),
        P(),
        P(None, frames),
        P(frames),
        P(frames, None),
        P(),
        P(),
        P(),
    )
    return jax.shard_map(body, mesh=mesh, in_specs=in_specs, out_specs=out_specs, check_vma=False)
```

```python
from functools import partial

import jax
import jax.numpy as jnp
from jax import lax
from jax.experimental import pallas as pl
from jax.experimental.pallas import tpu as pltpu
from jax.sharding import Mesh
from jax.sharding import PartitionSpec as P

HD = 64
LEN = 1024
QBLK = 512
EPS = 1e-05
BLK = 256

NEG = -1e30
GRANT = 10 << 20
EXTRA = 128
BRIEF = pl.CostEstimate(flops=1, bytes_accessed=1, transcendentals=0)
f32 = jnp.float32
bf16 = jnp.bfloat16


def nt(left, right):
    return lax.dot_general(left, right, (((1,), (1,)), ((), ())), preferred_element_type=f32)


def nn(left, right):
    return lax.dot_general(left, right, (((1,), (0,)), ((), ())), preferred_element_type=f32)


def tn(left, right):
    return lax.dot_general(left, right, (((0,), (0,)), ((), ())), preferred_element_type=f32)


def attn_bias(block, j, first):
    q_pos = block * BLK + lax.broadcasted_iota(jnp.int32, (1, BLK), 1)
    k_pos = j * BLK + lax.broadcasted_iota(jnp.int32, (BLK, BLK), 0)
    return jnp.where((k_pos >= first) & (k_pos <= q_pos), 0.0, NEG)


def head_rows(refs, scratch, heads):
    lane = lax.broadcasted_iota(jnp.int32, (LEN, 2 * HD), 1)
    for ref, out in zip(refs, scratch):
        for h in range(heads):
            pair = ref[:, (h // 2) * 2 * HD : (h // 2 + 1) * 2 * HD]
            out[h] = jnp.where((lane < HD) == (h % 2 == 0), pair, jnp.zeros_like(pair))


def attn_fwd_body(info, q_ref, k_ref, v_ref, st_ref, o_ref, lse_ref, k_heads, v_turned):
    block = pl.program_id(0)
    heads = q_ref.shape[1] // HD
    first = st_ref[...]

    @pl.when(block == 0)
    def _():
        head_rows([k_ref], [k_heads], heads)
        for pair in range(heads // 2):
            turned = v_ref[:, pair * 2 * HD : (pair + 1) * 2 * HD].T
            for h in (0, 1):
                v_turned[2 * pair + h, :HD] = turned[h * HD : (h + 1) * HD]
                v_turned[2 * pair + h, HD:] = jnp.ones((16, LEN), bf16)

    def step(at, carry):
        j = block - at
        row = pl.multiple_of((j ^ info[0]) * BLK, BLK)
        bias = attn_bias(block, j, first)
        out = []
        for h in range(heads):
            top, acc = carry[h]
            query = q_ref[:, (h // 2) * 2 * HD : (h // 2 + 1) * 2 * HD]
            s = nt(k_heads[h, pl.ds(row, BLK), :], query) + bias
            new = jnp.maximum(top, jnp.max(s, axis=0, keepdims=True))
            p = jnp.exp(s - new).astype(bf16)
            acc = acc * jnp.exp(top - new) + nn(v_turned[h, :, pl.ds(row, BLK)], p)
            out.append((new, acc))
        return tuple(out)

    init = tuple((jnp.full((1, BLK), NEG, f32), jnp.zeros((HD + 16, BLK), f32)) for _ in range(heads))
    done = lax.fori_loop(0, block + 1 - info[1 + block], step, init)
    for pair in range(heads // 2):
        both = [acc[:HD] / acc[HD : HD + 1] for _, acc in done[2 * pair : 2 * pair + 2]]
        o_ref[:, pair * 2 * HD : (pair + 1) * 2 * HD] = jnp.concatenate(both, axis=0).T.astype(bf16)
    for h in range(heads):
        top, acc = done[h]
        lse_ref[h : h + 1, :] = top + jnp.log(acc[HD : HD + 1])


def attn_bwd_body(base, info, q_ref, k_ref, v_ref, st_ref, o_ref, lse_ref, do_ref, d_ref, k_heads, v_heads, dk_acc, dv_acc):
    block = pl.program_id(0)
    heads = q_ref.shape[1] // HD
    first = st_ref[...]
    lane = lax.broadcasted_iota(jnp.int32, (BLK, 2 * HD), 1)

    @pl.when(block == 0)
    def _():
        head_rows([k_ref, v_ref], [k_heads, v_heads], heads)
        dk_acc[...] = jnp.zeros_like(dk_acc)
        dv_acc[...] = jnp.zeros_like(dv_acc)

    deltas = []
    for pair in range(heads // 2):
        cols = slice(pair * 2 * HD, (pair + 1) * 2 * HD)
        turned = (do_ref[:, cols].astype(f32) * o_ref[:, cols].astype(f32)).T
        for h in (0, 1):
            deltas.append(jnp.sum(turned[h * HD : (h + 1) * HD], axis=0, keepdims=True))

    def step(j, dqs):
        row = pl.multiple_of((j ^ info[0]) * BLK, BLK)
        bias = attn_bias(block, j, first)
        out = list(dqs)
        for pair in range(heads // 2):
            cols = slice(pair * 2 * HD, (pair + 1) * 2 * HD)
            query, cot = q_ref[:, cols], do_ref[:, cols]
            dk = dk_acc[pl.ds(row, BLK), cols]
            dv = dv_acc[pl.ds(row, BLK), cols]
            for h in (2 * pair, 2 * pair + 1):
                mask = (lane < HD) == (h % 2 == 0)
                keys = k_heads[h, pl.ds(row, BLK), :]
                p = jnp.exp(nt(keys, query) + (bias - lse_ref[base + h : base + h + 1, :]))
                dp = nt(v_heads[h, pl.ds(row, BLK), :], cot)
                ds = (p * (dp - deltas[h])).astype(bf16)
                dv = dv + nn(p.astype(bf16), jnp.where(mask, cot, jnp.zeros_like(cot)))
                dk = dk + nn(ds, jnp.where(mask, query, jnp.zeros_like(query)))
                out[pair] = out[pair] + tn(ds, keys)
            dk_acc[pl.ds(row, BLK), cols] = dk
            dv_acc[pl.ds(row, BLK), cols] = dv
        return tuple(out)

    init = tuple(jnp.zeros((BLK, 2 * HD), f32) for _ in range(heads // 2))
    dqs = lax.fori_loop(info[1 + block], block + 1, step, init)
    here = pl.multiple_of((block ^ info[0]) * BLK, BLK)
    for pair in range(heads // 2):
        cols = slice(pair * 2 * HD, (pair + 1) * 2 * HD)
        d_ref[0, pl.ds(here, BLK), cols] = (dqs[pair] * HD**-0.5).astype(bf16)

    @pl.when(block == pl.num_programs(0) - 1)
    def _():
        d_ref[1] = dk_acc[...].astype(bf16)
        d_ref[2] = dv_acc[...].astype(bf16)


def attn_specs(width):
    small = pl.BlockSpec((BLK, width), lambda i, info: (i ^ info[0], 0))
    whole = pl.BlockSpec((LEN, width), lambda i, info: (0, 0))
    start = pl.BlockSpec((1, BLK), lambda i, info: (0, i ^ info[0]))
    lse = pl.BlockSpec((width // HD, BLK), lambda i, info: (0, i ^ info[0]))
    return small, whole, start, lse


def attn_fwd(info, query, keys, values, start):
    width = query.shape[1]
    heads = width // HD
    small, whole, first, lse = attn_specs(width)
    return pl.pallas_call(
        attn_fwd_body,
        out_shape=(jax.ShapeDtypeStruct(query.shape, bf16), jax.ShapeDtypeStruct((heads, LEN), f32)),
        grid_spec=pltpu.PrefetchScalarGridSpec(
            num_scalar_prefetch=1,
            grid=(LEN // BLK,),
            in_specs=[small, whole, whole, first],
            out_specs=[small, lse],
            scratch_shapes=[pltpu.VMEM((heads, LEN, 2 * HD), bf16), pltpu.VMEM((heads, HD + 16, LEN), bf16)],
        ),
        cost_estimate=BRIEF,
        compiler_params=pltpu.CompilerParams(vmem_limit_bytes=GRANT),
        name="attn_fwd",
    )(info, query, keys, values, start)


def attn_bwd(info, query, keys, values, start, out, lse, cot, part=0, parts=1, prior=None):
    width = query.shape[1] // parts
    heads = width // HD
    small = pl.BlockSpec((BLK, width), lambda i, info: (i ^ info[0], part))
    whole = pl.BlockSpec((LEN, width), lambda i, info: (0, part))
    first = pl.BlockSpec((1, BLK), lambda i, info: (0, i ^ info[0]))
    lse_spec = pl.BlockSpec((heads * parts, BLK), lambda i, info: (0, i ^ info[0]))
    more = () if prior is None else (prior,)

    def body(*refs):
        attn_bwd_body(part * heads, *refs[:8], *refs[8 + len(more) :])

    return pl.pallas_call(
        body,
        out_shape=jax.ShapeDtypeStruct((3,) + query.shape, bf16),
        grid_spec=pltpu.PrefetchScalarGridSpec(
            num_scalar_prefetch=1,
            grid=(LEN // BLK,),
            in_specs=[small, whole, whole, first, small, lse_spec, small]
            + [pl.BlockSpec(memory_space=pl.ANY)] * len(more),
            out_specs=pl.BlockSpec((3, LEN, width), lambda i, info: (0, 0, part)),
            scratch_shapes=[
                pltpu.VMEM((heads, LEN, 2 * HD), bf16),
                pltpu.VMEM((heads, LEN, 2 * HD), bf16),
                pltpu.VMEM((LEN, width), f32),
                pltpu.VMEM((LEN, width), f32),
            ],
        ),
        input_output_aliases={8: 0} if more else {},
        cost_estimate=BRIEF,
        compiler_params=pltpu.CompilerParams(vmem_limit_bytes=GRANT),
        name="attn_bwd",
    )(info, query, keys, values, start, out, lse, cot, *more)


def up_body(a_ref, w_ref, b_ref, g_ref, s_ref):
    rows = a_ref[...]
    for part in range(w_ref.shape[1] // 256):
        cols = slice(part * 256, part * 256 + 256)
        u = nn(rows, w_ref[:, cols]) + b_ref[:, cols].astype(f32)
        size = jnp.abs(u)
        t = 1.0 / (1.0 + 0.3275911 * 0.7071067811865476 * size)
        poly = t * (0.5 * 0.254829592 + t * (0.5 * -0.284496736 + t * (0.5 * 1.421413741 + t * (0.5 * -1.453152027 + t * (0.5 * 1.061405429)))))
        bell = jnp.exp(-0.5 * u * u)
        tail = poly * bell
        cdf = jnp.where(u >= 0, 1.0 - tail, tail)
        g_ref[:, cols] = (u * cdf).astype(bf16)
        s_ref[:, cols] = (cdf + u * bell * 0.3989422804014327).astype(bf16)


def up_gelu(rows, weight, bias):
    m, k = rows.shape
    n = weight.shape[1]
    bm = 256
    shape = jax.ShapeDtypeStruct((m, n), bf16)
    tile = pl.BlockSpec((bm, n), lambda i: (i, 0))
    return pl.pallas_call(
        up_body,
        out_shape=(shape, shape),
        grid=(m // bm,),
        in_specs=[pl.BlockSpec((bm, k), lambda i: (i, 0)), pl.BlockSpec((k, n), lambda i: (0, 0)), pl.BlockSpec((1, n), lambda i: (0, 0))],
        out_specs=(tile, tile),
        cost_estimate=BRIEF,
        compiler_params=pltpu.CompilerParams(vmem_limit_bytes=GRANT),
        name="up_gelu",
    )(rows, weight, bias.reshape(1, n))


def const_spec(shape):
    return pl.BlockSpec(shape, lambda i: (0,) * len(shape))


def row_spec(rows, cols):
    return pl.BlockSpec((rows, cols), lambda i: (i, 0))


def project_body(a_ref, w_ref, b_ref, q_ref, k_ref, v_ref):
    rows = a_ref[...]
    q_ref[...] = (nn(rows, w_ref[0]) + b_ref[0:1].astype(f32)).astype(bf16) * jnp.bfloat16(HD**-0.5)
    k_ref[...] = nn(rows, w_ref[1]).astype(bf16)
    v_ref[...] = (nn(rows, w_ref[2]) + b_ref[1:2].astype(f32)).astype(bf16)


def project(rows, weight, bias):
    m, k = rows.shape
    n = weight.shape[2]
    tile = 256
    shape = jax.ShapeDtypeStruct((m, n), bf16)
    return pl.pallas_call(
        project_body,
        out_shape=(shape, shape, shape),
        grid=(m // tile,),
        in_specs=[row_spec(tile, k), const_spec(weight.shape), const_spec(bias.shape)],
        out_specs=[row_spec(tile, n)] * 3,
        cost_estimate=BRIEF,
        compiler_params=pltpu.CompilerParams(vmem_limit_bytes=GRANT),
        name="project",
    )(rows, weight, bias)


def sum_dots(product, lefts, rights):
    stacked = lefts[0].ndim == 3
    m, k = lefts[0].shape[-2:]
    n = rights[0].shape[-1] if product is nn else rights[0].shape[-2]
    terms = len(lefts)
    tile = 256
    steps = m // tile // 2

    def body(*refs):
        total = None
        for left, right in zip(refs[:terms], refs[terms : 2 * terms]):
            for at in range(left.shape[0] if stacked else 1):
                term = product(left[at], right[at]) if stacked else product(left[...], right[...])
                total = term if total is None else total + term
        here, there = refs[2 * terms :]

        @pl.when(pl.program_id(0) < steps)
        def _():
            there[...] = total.astype(bf16)

        @pl.when(pl.program_id(0) >= steps)
        def _():
            here[...] = total

    def turn(i):
        return jnp.where(i < steps, i + steps, i - steps)

    if stacked:
        left_spec = pl.BlockSpec((lefts[0].shape[0], tile, k), lambda i: (0, turn(i), 0))
    else:
        left_spec = pl.BlockSpec((tile, k), lambda i: (turn(i), 0))
    return pl.pallas_call(
        body,
        out_shape=(jax.ShapeDtypeStruct((m // 2, n), f32), jax.ShapeDtypeStruct((m // 2, n), bf16)),
        grid=(2 * steps,),
        in_specs=[left_spec] * terms + [const_spec(r.shape) for r in rights],
        out_specs=[
            pl.BlockSpec((tile, n), lambda i: (jnp.maximum(i - steps, 0), 0)),
            pl.BlockSpec((tile, n), lambda i: (jnp.minimum(i, steps - 1), 0)),
        ],
        cost_estimate=BRIEF,
        compiler_params=pltpu.CompilerParams(vmem_limit_bytes=GRANT),
        name="sum_dots",
    )(*lefts, *rights)


def center_rows(rows):
    center = rows - jnp.mean(rows, axis=-1, keepdims=True)
    scale = lax.rsqrt(jnp.mean(center * center, axis=-1, keepdims=True) + EPS)
    return center * scale, scale


def first_norm_body(x_ref, g_ref, gain_ref, shift_ref, a_ref, sum_ref):
    normal, _ = center_rows(x_ref[...].astype(f32))
    a_ref[...] = (normal * gain_ref[...] + shift_ref[...]).astype(bf16)

    @pl.when(pl.program_id(0) == 0)
    def _():
        sum_ref[...] = jnp.zeros_like(sum_ref)

    sum_ref[...] += jnp.sum(g_ref[...].astype(f32), axis=0, keepdims=True)


def first_norm(tokens, cotangent, gain, shift):
    m, d = tokens.shape
    tile = 128
    return pl.pallas_call(
        first_norm_body,
        out_shape=(jax.ShapeDtypeStruct((m, d), bf16), jax.ShapeDtypeStruct((1, d), f32)),
        grid=(m // tile,),
        in_specs=[row_spec(tile, d), row_spec(tile, d), const_spec((1, d)), const_spec((1, d))],
        out_specs=[row_spec(tile, d), const_spec((1, d))],
        cost_estimate=BRIEF,
        compiler_params=pltpu.CompilerParams(vmem_limit_bytes=GRANT),
        name="first_norm",
    )(tokens, cotangent, gain, shift)


def second_norm_body(x_ref, here_ref, came_ref, b_ref, gain_ref, shift_ref, h_ref, a_ref):
    mixed = x_ref[...].astype(f32) + (here_ref[...] + came_ref[...].astype(f32)) + b_ref[...].astype(f32)
    h_ref[...] = mixed
    normal, _ = center_rows(mixed)
    a_ref[...] = (normal * gain_ref[...] + shift_ref[...]).astype(bf16)


def second_norm(tokens, here, came, bias, gain, shift):
    m, d = tokens.shape
    tile = 128
    return pl.pallas_call(
        second_norm_body,
        out_shape=(jax.ShapeDtypeStruct((m, d), f32), jax.ShapeDtypeStruct((m, d), bf16)),
        grid=(m // tile,),
        in_specs=[row_spec(tile, d)] * 3 + [const_spec((1, d))] * 3,
        out_specs=[row_spec(tile, d)] * 2,
        cost_estimate=BRIEF,
        compiler_params=pltpu.CompilerParams(vmem_limit_bytes=GRANT),
        name="second_norm",
    )(tokens, here, came, bias, gain, shift)


def norm_back_body(v_ref, here_ref, low_came_ref, high_came_ref, gain_ref, res_ref, out_ref, low_ref, sums_ref):
    normal, scale = center_rows(v_ref[...].astype(f32))
    first = pl.program_id(0) < pl.num_programs(0) // 2
    came = jnp.where(first, low_came_ref[...], high_came_ref[...])
    grad = here_ref[...] + came.astype(f32)
    scaled = grad * gain_ref[...]
    inner = jnp.mean(scaled * normal, axis=-1, keepdims=True)
    back = scale * (scaled - jnp.mean(scaled, axis=-1, keepdims=True) - normal * inner)
    back = back + res_ref[...].astype(f32)
    low = back.astype(bf16)
    out_ref[...] = back
    low_ref[...] = low

    @pl.when(pl.program_id(0) == 0)
    def _():
        sums_ref[...] = jnp.zeros_like(sums_ref)

    sums_ref[0:1] += jnp.sum(grad * normal, axis=0, keepdims=True)
    sums_ref[1:2] += jnp.sum(grad, axis=0, keepdims=True)
    sums_ref[2:3] += jnp.sum(low.astype(f32), axis=0, keepdims=True)


def norm_back(values, here, came, gain, residual):
    m, d = values.shape
    tile = 128
    half = m // tile // 2
    low = pl.BlockSpec((tile, d), lambda i: (jnp.minimum(i, half - 1), 0))
    high = pl.BlockSpec((tile, d), lambda i: (jnp.maximum(i - half, 0), 0))
    return pl.pallas_call(
        norm_back_body,
        out_shape=(
            jax.ShapeDtypeStruct((m, d), f32),
            jax.ShapeDtypeStruct((m, d), bf16),
            jax.ShapeDtypeStruct((8, d), f32),
        ),
        grid=(m // tile,),
        in_specs=[row_spec(tile, d)] * 2 + [low, high, const_spec((1, d)), row_spec(tile, d)],
        out_specs=[row_spec(tile, d)] * 2 + [const_spec((8, d))],
        cost_estimate=BRIEF,
        compiler_params=pltpu.CompilerParams(vmem_limit_bytes=GRANT),
        name="norm_back",
    )(values, here, *came, gain, residual)


def back_act_body(z_ref, w_ref, s_ref, du_ref, sum_ref):
    du = (nt(z_ref[...], w_ref[...]) * s_ref[...].astype(f32)).astype(bf16)
    du_ref[...] = du

    @pl.when(pl.program_id(0) == 0)
    def _():
        sum_ref[...] = jnp.zeros_like(sum_ref)

    sum_ref[...] += jnp.sum(du.astype(f32), axis=0, keepdims=True)


def back_act(cotangent, weight, slope):
    m, d = cotangent.shape
    n = weight.shape[0]
    tile = 256
    return pl.pallas_call(
        back_act_body,
        out_shape=(jax.ShapeDtypeStruct((m, n), bf16), jax.ShapeDtypeStruct((1, n), f32)),
        grid=(m // tile,),
        in_specs=[row_spec(tile, d), const_spec((n, d)), row_spec(tile, n)],
        out_specs=[row_spec(tile, n), const_spec((1, n))],
        cost_estimate=BRIEF,
        compiler_params=pltpu.CompilerParams(vmem_limit_bytes=GRANT),
        name="back_act",
    )(cotangent, weight, slope)


def frame_sums_body(a_ref, d_ref, o_ref, g_ref, one_ref, two_ref, sums_ref, a_turned):
    rows, width = g_ref.shape[1], o_ref.shape[1]
    count = rows // width
    a_turned[...] = a_ref[...].T
    for at in range(4 * count):
        kind, part = divmod(at, count)
        out = one_ref if at < 2 * count else two_ref
        if kind < 3:
            block = nn(a_turned[part * width : (part + 1) * width, :], d_ref[kind])
        else:
            block = tn(o_ref[...], g_ref[:, part * width : (part + 1) * width])
        low = (at % (2 * count)) * width
        out[low : low + width, :] = block.astype(bf16)
    two_ref[2 * rows :, :] = jnp.zeros((EXTRA, width), bf16)
    for kind in range(3):
        sums_ref[kind] = jnp.sum(d_ref[kind].astype(f32), axis=0, keepdims=True)


def frame_sums(rows, trio, out, cotangent):
    t, d = rows.shape
    n = trio.shape[2]
    half = jax.ShapeDtypeStruct((2 * d, n), bf16)
    one, two, sums = pl.pallas_call(
        frame_sums_body,
        out_shape=(half, jax.ShapeDtypeStruct((2 * d + EXTRA, n), bf16), jax.ShapeDtypeStruct((3, 1, n), f32)),
        grid=(1,),
        in_specs=[const_spec((t, d)), const_spec((3, t, n)), const_spec((t, n)), const_spec((t, d))],
        out_specs=[const_spec((2 * d, n)), const_spec((2 * d + EXTRA, n)), const_spec((3, 1, n))],
        scratch_shapes=[pltpu.VMEM((d, t), bf16)],
        cost_estimate=BRIEF,
        compiler_params=pltpu.CompilerParams(vmem_limit_bytes=GRANT),
        name="frame_sums",
    )(rows, trio, out, cotangent)
    return (one, two), sums


def frames_body(a_ref, g_ref, out_ref, turned):
    tile = out_ref.shape[0]
    turned[...] = a_ref[...].T
    out_ref[...] = nn(turned[...], g_ref[...]).astype(bf16)


def across_frames(left, right):
    t, m = left.shape
    n = right.shape[1]
    tile = 256
    return pl.pallas_call(
        frames_body,
        out_shape=jax.ShapeDtypeStruct((m, n), bf16),
        grid=(m // tile,),
        in_specs=[pl.BlockSpec((t, tile), lambda i: (0, i)), const_spec((t, n))],
        out_specs=row_spec(tile, n),
        scratch_shapes=[pltpu.VMEM((tile, t), bf16)],
        cost_estimate=BRIEF,
        compiler_params=pltpu.CompilerParams(vmem_limit_bytes=GRANT),
        name="across_frames",
    )(left, right)


def turn_back_body(a_ref, w_ref, out_ref):
    out_ref[...] = nt(a_ref[...], w_ref[...]).astype(bf16)


def turn_back(rows, weight):
    m, k = rows.shape
    n = weight.shape[0]
    tile = 256
    return pl.pallas_call(
        turn_back_body,
        out_shape=jax.ShapeDtypeStruct((m, n), bf16),
        grid=(m // tile,),
        in_specs=[row_spec(tile, k), const_spec((n, k))],
        out_specs=row_spec(tile, n),
        cost_estimate=BRIEF,
        compiler_params=pltpu.CompilerParams(vmem_limit_bytes=GRANT),
        name="turn_back",
    )(rows, weight)


def side_sum_body(info, *refs):
    total = refs[0][0].astype(f32)
    for ref in refs[1:-1]:
        total = total + (ref[0] if len(ref.shape) == 3 else ref[...]).astype(f32)
    refs[-1][...] = total.astype(bf16)


def side_sum(side, own, got, near=None):
    _, rows, cols = own.shape
    tile = rows // 4
    pick_spec = pl.BlockSpec((1, tile, cols), lambda i, info: (info[0], i, 0))
    flat = pl.BlockSpec((tile, cols), lambda i, info: (i, 0))
    args = [own, got] + ([] if near is None else [near])
    return pl.pallas_call(
        side_sum_body,
        out_shape=jax.ShapeDtypeStruct((rows, cols), bf16),
        grid_spec=pltpu.PrefetchScalarGridSpec(
            num_scalar_prefetch=1,
            grid=(4,),
            in_specs=[pick_spec, pick_spec] + [flat] * (len(args) - 2),
            out_specs=flat,
        ),
        cost_estimate=BRIEF,
        compiler_params=pltpu.CompilerParams(vmem_limit_bytes=GRANT),
        name="side_sum",
    )(side[None], *args)


def add_low_body(a_ref, b_ref, out_ref):
    out_ref[...] = (a_ref[...].astype(f32) + b_ref[...].astype(f32)).astype(bf16)


def add_low(left, right):
    rows, cols = left.shape
    tile = rows // 2
    return pl.pallas_call(
        add_low_body,
        out_shape=jax.ShapeDtypeStruct((rows, cols), bf16),
        grid=(2,),
        in_specs=[row_spec(tile, cols)] * 2,
        out_specs=row_spec(tile, cols),
        cost_estimate=BRIEF,
        compiler_params=pltpu.CompilerParams(vmem_limit_bytes=GRANT),
        name="add_low",
    )(left, right)


def quarter_sums_body(info, own_ref, got_ref, near_ref, send_ref, keep_ref):
    total = own_ref[0, 0].astype(f32) + got_ref[0, 0].astype(f32) + near_ref[0].astype(f32)

    @pl.when(pl.program_id(0) == 0)
    def _():
        send_ref[...] = total.astype(bf16)

    @pl.when(pl.program_id(0) == 1)
    def _():
        keep_ref[...] = total.astype(bf16)


def quarter_sums(place, own, got, near):
    _, rows, cols = own.shape
    rows = rows // 2
    tile = rows // 2
    deep = pl.BlockSpec((1, 1, tile, cols), lambda f, i, info: (info[0], info[1] ^ 1 ^ f, i, 0))
    flat = pl.BlockSpec((1, tile, cols), lambda f, i, info: (info[1] ^ 1 ^ f, i, 0))
    shape = jax.ShapeDtypeStruct((rows, cols), bf16)
    return pl.pallas_call(
        quarter_sums_body,
        out_shape=(shape, shape),
        grid_spec=pltpu.PrefetchScalarGridSpec(
            num_scalar_prefetch=1,
            grid=(2, 2),
            in_specs=[deep, deep, flat],
            out_specs=[
                pl.BlockSpec((tile, cols), lambda f, i, info: (jnp.where(f == 0, i, 1), 0)),
                pl.BlockSpec((tile, cols), lambda f, i, info: (jnp.where(f == 0, 0, i), 0)),
            ],
        ),
        cost_estimate=BRIEF,
        compiler_params=pltpu.CompilerParams(vmem_limit_bytes=GRANT),
        name="quarter_sums",
    )(place, own.reshape(2, 2, rows, cols), got.reshape(2, 2, rows, cols), near.reshape(2, rows, cols))


def settle_body(info, mine_ref, other_ref, *rest):
    for at, ref in enumerate((mine_ref, other_ref)):

        @pl.when(pl.program_id(0) == at)
        def _(ref=ref):
            rest[-1][0] = ref[...].astype(f32)


def settle(place, mine, other, flip=0, prior=None, extra=0):
    rows, cols = mine.shape
    tile = rows // 2
    first = pl.BlockSpec((tile, cols), lambda f, i, info: (jnp.where(f == 0, i, 1), 0))
    second = pl.BlockSpec((tile, cols), lambda f, i, info: (jnp.where(f == 0, 0, i), 0))
    more = () if prior is None else (prior.reshape(-1, rows, cols),)
    out = pl.pallas_call(
        settle_body,
        out_shape=jax.ShapeDtypeStruct((4 + extra // rows, rows, cols), f32),
        grid_spec=pltpu.PrefetchScalarGridSpec(
            num_scalar_prefetch=1,
            grid=(2, 2),
            in_specs=[first, second] + [pl.BlockSpec(memory_space=pl.ANY)] * len(more),
            out_specs=pl.BlockSpec(
                (1, tile, cols), lambda f, i, info: (2 * (info[0] ^ f) + (info[1] ^ flip), i, 0)
            ),
        ),
        input_output_aliases={3: 0} if more else {},
        cost_estimate=BRIEF,
        compiler_params=pltpu.CompilerParams(vmem_limit_bytes=GRANT),
        name="settle",
    )(place, mine, other, *more)
    return out.reshape(-1, cols)


def finish_body(h_ref, here_ref, came_ref, b_ref, out_ref):
    out_ref[...] = (h_ref[...] + here_ref[...] + came_ref[...].astype(f32) + b_ref[...].astype(f32)).astype(bf16)


def finish(mixed, here, came, bias):
    m, d = mixed.shape
    tile = 128
    return pl.pallas_call(
        finish_body,
        out_shape=jax.ShapeDtypeStruct((m, d), bf16),
        grid=(m // tile,),
        in_specs=[row_spec(tile, d)] * 3 + [const_spec((1, d))],
        out_specs=row_spec(tile, d),
        cost_estimate=BRIEF,
        compiler_params=pltpu.CompilerParams(vmem_limit_bytes=GRANT),
        name="finish",
    )(mixed, here, came, bias)


def ride_body(vector_ref, whole_ref, out_ref):
    count, cols = vector_ref.shape
    rest = jnp.zeros((out_ref.shape[0] - count, cols), f32)
    out_ref[...] = jnp.concatenate([vector_ref[...], rest], axis=0).astype(bf16)


def ride(whole, vector):
    rows, cols = whole.shape
    vector = jnp.pad(vector.reshape(-1, cols), ((0, -(vector.size // cols) % 8), (0, 0)))
    return pl.pallas_call(
        ride_body,
        out_shape=jax.ShapeDtypeStruct((rows, cols), bf16),
        grid=(1,),
        in_specs=[const_spec(vector.shape), pl.BlockSpec(memory_space=pl.ANY)],
        out_specs=pl.BlockSpec((EXTRA, cols), lambda i: (rows // EXTRA - 1, 0)),
        input_output_aliases={1: 0},
        cost_estimate=BRIEF,
        compiler_params=pltpu.CompilerParams(vmem_limit_bytes=GRANT),
        name="ride",
    )(vector, whole)


def norm_rows(values, gain, shift):
    center = values - jnp.mean(values, axis=-1, keepdims=True)
    spread = jnp.mean(center * center, axis=-1, keepdims=True)
    return center * lax.rsqrt(spread + EPS) * gain + shift


def split_heads(flat, rows):
    return flat.reshape(rows, LEN, flat.shape[1] // HD, HD)


def block_scores(query, keys, seg_q, seg_k, offset):
    scores = jnp.einsum(
        "rqhd,rkhd->rhqk", query, keys, preferred_element_type=jnp.float32
    ) * HD ** (-0.5)
    q_pos = offset + jnp.arange(query.shape[1], dtype=jnp.int32)
    k_pos = jnp.arange(keys.shape[1], dtype=jnp.int32)
    allowed = (seg_q[:, :, None] == seg_k[:, None, :]) & (
        k_pos[None, None, :] <= q_pos[None, :, None]
    )
    return jnp.where(allowed[:, None], scores, -1e30)


def attention_forward(query, keys, values, seg_all):
    rows = query.shape[0] // LEN
    q4 = split_heads(query, rows)
    k4 = split_heads(keys, rows)
    v4 = split_heads(values, rows)
    seg2 = seg_all.reshape(rows, LEN)
    outputs = []
    totals = []
    for block in range(LEN // QBLK):
        first = block * QBLK
        end = first + QBLK
        scores = block_scores(
            q4[:, first:end], k4[:, :end], seg2[:, first:end], seg2[:, :end], first
        )
        top = jnp.max(scores, axis=-1, keepdims=True)
        expd = jnp.exp(scores - top)
        summed = jnp.sum(expd, axis=-1, keepdims=True)
        weights = (expd / summed).astype(jnp.bfloat16)
        outputs.append(
            jnp.einsum("rhqk,rkhd->rqhd", weights, v4[:, :end], preferred_element_type=jnp.float32)
        )
        totals.append(top + jnp.log(summed))
    attended = jnp.concatenate(outputs, axis=1).reshape(query.shape).astype(jnp.bfloat16)
    return (attended, totals)


def attention_backward(query, keys, values, seg_all, totals, grad_att):
    rows = query.shape[0] // LEN
    q4 = split_heads(query, rows)
    k4 = split_heads(keys, rows)
    v4 = split_heads(values, rows)
    g4 = split_heads(grad_att, rows)
    seg2 = seg_all.reshape(rows, LEN)
    scale = HD ** (-0.5)
    grad_k = jnp.zeros(k4.shape, jnp.float32)
    grad_v = jnp.zeros(v4.shape, jnp.float32)
    grad_q_parts = []
    for block in range(LEN // QBLK):
        first = block * QBLK
        end = first + QBLK
        scores = block_scores(
            q4[:, first:end], k4[:, :end], seg2[:, first:end], seg2[:, :end], first
        )
        probs = jnp.exp(scores - totals[block])
        weights = probs.astype(jnp.bfloat16)
        grad_w = jnp.einsum(
            "rqhd,rkhd->rhqk", g4[:, first:end], v4[:, :end], preferred_element_type=jnp.float32
        )
        delta = jnp.sum(probs * grad_w, axis=-1, keepdims=True)
        grad_s = (probs * (grad_w - delta)).astype(jnp.bfloat16)
        grad_q_parts.append(
            jnp.einsum("rhqk,rkhd->rqhd", grad_s, k4[:, :end], preferred_element_type=jnp.float32)
            * scale
        )
        padding = ((0, 0), (0, LEN - end), (0, 0), (0, 0))
        grad_k = grad_k + jnp.pad(
            jnp.einsum(
                "rhqk,rqhd->rkhd", grad_s, q4[:, first:end], preferred_element_type=jnp.float32
            )
            * scale,
            padding,
        )
        grad_v = grad_v + jnp.pad(
            jnp.einsum(
                "rhqk,rqhd->rkhd", weights, g4[:, first:end], preferred_element_type=jnp.float32
            ),
            padding,
        )
    shape = query.shape
    grad_q = jnp.concatenate(grad_q_parts, axis=1).reshape(shape).astype(jnp.bfloat16)
    return (
        grad_q,
        grad_k.reshape(shape).astype(jnp.bfloat16),
        grad_v.reshape(shape).astype(jnp.bfloat16),
    )


def tensor_parallel_shards(
    tokens,
    segment_ids,
    w_qkv,
    b_qv,
    w_out,
    b_out,
    w_up,
    b_up,
    w_down,
    b_down,
    ln_gain,
    ln_bias,
    out_grad,
):
    resid = tokens.astype(jnp.float32)
    qv_bias = b_qv.astype(jnp.float32)
    up_bias = b_up.astype(jnp.float32)
    local_rows = tokens.shape[0]
    normed, first_back = jax.vjp(norm_rows, resid, ln_gain[0], ln_bias[0])
    lowered = normed.astype(jnp.bfloat16)
    joined, seg_all = (
        lax.all_gather(lowered, "mp", axis=0, tiled=True),
        lax.all_gather(segment_ids, "mp", axis=0, tiled=True),
    )
    query = (jnp.dot(joined, w_qkv[0], preferred_element_type=jnp.float32) + qv_bias[0]).astype(
        jnp.bfloat16
    )
    keys = jnp.dot(joined, w_qkv[1], preferred_element_type=jnp.float32).astype(jnp.bfloat16)
    values = (jnp.dot(joined, w_qkv[2], preferred_element_type=jnp.float32) + qv_bias[1]).astype(
        jnp.bfloat16
    )
    query, keys, values = (query, keys, values)
    attended, totals = attention_forward(query, keys, values, seg_all)
    attn_sum = lax.psum_scatter(
        jnp.dot(attended, w_out, preferred_element_type=jnp.float32).astype(jnp.bfloat16),
        "mp",
        scatter_dimension=0,
        tiled=True,
    ).astype(jnp.float32)
    mixed = resid + attn_sum + b_out.astype(jnp.float32)
    normed2, second_back = jax.vjp(norm_rows, mixed, ln_gain[1], ln_bias[1])
    lowered2 = normed2.astype(jnp.bfloat16)
    joined2 = lax.all_gather(lowered2, "mp", axis=0, tiled=True)
    pre_act = jnp.dot(joined2, w_up, preferred_element_type=jnp.float32) + up_bias
    pre_act, activ = (pre_act, jax.nn.gelu(pre_act, approximate=False).astype(jnp.bfloat16))
    block_out = (
        mixed
        + lax.psum_scatter(
            jnp.dot(activ, w_down, preferred_element_type=jnp.float32).astype(jnp.bfloat16),
            "mp",
            scatter_dimension=0,
            tiled=True,
        ).astype(jnp.float32)
        + b_down.astype(jnp.float32)
    ).astype(jnp.bfloat16)
    grad_y = out_grad.astype(jnp.float32)
    grad_z = lax.all_gather(out_grad, "mp", axis=0, tiled=True)
    grad_down = jnp.einsum("tf,td->fd", activ, grad_z, preferred_element_type=jnp.float32)
    grad_bdown = jnp.sum(grad_z, axis=0, dtype=jnp.float32)
    grad_act = jnp.einsum("td,fd->tf", grad_z, w_down, preferred_element_type=jnp.float32)
    gelu_back = jax.vjp(lambda value: jax.nn.gelu(value, approximate=False), pre_act)[1]
    grad_pre = gelu_back(grad_act)[0].astype(jnp.bfloat16)
    grad_up = jnp.einsum("td,tf->df", joined2, grad_pre, preferred_element_type=jnp.float32)
    grad_bup = jnp.sum(grad_pre, axis=0, dtype=jnp.float32)
    grad_n2 = lax.psum_scatter(
        jnp.einsum("tf,df->td", grad_pre, w_up, preferred_element_type=jnp.float32).astype(
            jnp.bfloat16
        ),
        "mp",
        scatter_dimension=0,
        tiled=True,
    ).astype(jnp.float32)
    grad_h, grad_g2, grad_s2 = second_back(grad_n2)
    grad_h = grad_h + grad_y
    grad_branch = lax.all_gather(grad_h.astype(jnp.bfloat16), "mp", axis=0, tiled=True)
    grad_wout = jnp.einsum("tc,td->cd", attended, grad_branch, preferred_element_type=jnp.float32)
    grad_bout = jnp.sum(grad_branch, axis=0, dtype=jnp.float32)
    grad_att = jnp.einsum(
        "td,cd->tc", grad_branch, w_out, preferred_element_type=jnp.float32
    ).astype(jnp.bfloat16)
    grad_q, grad_k, grad_v = attention_backward(query, keys, values, seg_all, totals, grad_att)
    grad_qkv = jnp.stack(
        [
            jnp.einsum("td,tc->dc", joined, piece, preferred_element_type=jnp.float32)
            for piece in (grad_q, grad_k, grad_v)
        ]
    )
    grad_bqv = jnp.stack(
        [jnp.sum(grad_q, axis=0, dtype=jnp.float32), jnp.sum(grad_v, axis=0, dtype=jnp.float32)]
    )
    summed = jnp.zeros((local_rows * lax.axis_size("mp"), w_qkv.shape[1]), jnp.float32)
    for index, piece in enumerate((grad_q, grad_k, grad_v)):
        summed = summed + jnp.einsum(
            "tc,dc->td", piece, w_qkv[index], preferred_element_type=jnp.float32
        )
    grad_n1 = lax.psum_scatter(
        summed.astype(jnp.bfloat16), "mp", scatter_dimension=0, tiled=True
    ).astype(jnp.float32)
    grad_x, grad_g1, grad_s1 = first_back(grad_n1)
    grad_in = grad_x + grad_h
    weight_totals = (
        lax.psum(grad_qkv.astype(jnp.bfloat16), "dp").astype(jnp.float32),
        lax.psum(grad_bqv.astype(jnp.bfloat16), "dp").astype(jnp.float32),
        lax.psum(grad_wout.astype(jnp.bfloat16), "dp").astype(jnp.float32),
        lax.psum(grad_bout.astype(jnp.bfloat16), "dp").astype(jnp.float32),
        lax.psum(grad_up.astype(jnp.bfloat16), "dp").astype(jnp.float32),
        lax.psum(grad_bup.astype(jnp.bfloat16), "dp").astype(jnp.float32),
        lax.psum(grad_down.astype(jnp.bfloat16), "dp").astype(jnp.float32),
        lax.psum(grad_bdown.astype(jnp.bfloat16), "dp").astype(jnp.float32),
    )
    norm_totals = lax.psum(
        (jnp.stack([grad_g1, grad_g2]), jnp.stack([grad_s1, grad_s2])), ("dp", "mp")
    )
    return (block_out, grad_in) + tuple(weight_totals) + tuple(norm_totals)


def row_per_chip(mesh):
    return mesh.shape["mp"] == 4 and mesh.shape["dp"] == 8


def swap(value, axis):
    return lax.ppermute(value, axis, [(0, 1), (1, 0)])


def core(value):
    return swap(value, "core")


def cross(value):
    return swap(value, "x")


def after(value, *others):
    return lax.optimization_barrier((value,) + others)[0]


def take(value, at):
    return lax.dynamic_index_in_dim(value, at, 0, keepdims=False)


def place(whole, piece, at):
    return lax.dynamic_update_index_in_dim(whole, piece, at, 0)


def quarter_of(weight):
    me = lax.axis_index("y") + 2 * (lax.axis_index("z") & 1)
    return take(weight.reshape(4, -1, weight.shape[-1]), me)


def share(mine):
    out = [swap(mine, "y")]
    for bits in (2, 3):
        out.append(lax.ppermute(mine, ("z", "y"), [(i, i ^ bits) for i in range(8)]))
    return out


def assemble(mine, others):
    me = lax.axis_index("y") + 2 * (lax.axis_index("z") & 1)
    whole = place(jnp.zeros((4,) + mine.shape, mine.dtype), mine, me)
    for bits, piece in zip((1, 2, 3), others):
        whole = place(whole, piece, me ^ bits)
    return whole.reshape(-1, mine.shape[-1])


def swap_z(value, bits):
    return lax.ppermute(value, "z", [(i, i ^ bits) for i in range(4)])


def by_side(value):
    return value.reshape(2, value.shape[0] // 2, value.shape[1])


class Line:
    def __init__(self):
        self.last = None

    def __call__(self, function, *args):
        if self.last is not None:
            args, _ = lax.optimization_barrier((args, self.last))
        out = function(*args)
        self.last = jax.tree.leaves(out)[0]
        return out


def row_per_chip_shards(
    tokens,
    segment_ids,
    w_qkv,
    b_qv,
    w_out,
    b_out,
    w_up,
    b_up,
    w_down,
    b_down,
    ln_gain,
    ln_bias,
    out_grad,
):
    side, here_y = lax.axis_index("core"), lax.axis_index("y")
    place = jnp.stack([here_y, lax.axis_index("z") & 1]).astype(jnp.int32)
    width, wide = b_qv.shape[1], tokens.shape[1]
    gains, shifts = ln_gain[:, None], ln_bias[:, None]
    line = Line()

    def pair(*parts):
        return line(lambda *all: jnp.concatenate(all), *parts)

    qkv_mine = cross(line(quarter_of, w_qkv.reshape(-1, width)))
    a1_own, sum_dz = line(first_norm, tokens, out_grad, gains[0], shifts[0])
    a1_came = core(a1_own)
    seg_other = core(segment_ids)
    small = cross(jnp.concatenate([b_qv.reshape(-1), b_up]))
    up_quarter = line(quarter_of, w_up)
    down_quarter = line(quarter_of, w_down)

    def ranges(mine, other):
        seg = jnp.concatenate([mine, other])
        start = jnp.sum((seg[None, :] < seg[:, None]).astype(jnp.int32), axis=1)[None]
        ordered = jnp.where(side == 0, seg, jnp.concatenate([other, mine]))
        blocks = ordered.reshape(LEN // BLK, BLK)
        low = jnp.sum((blocks[None, :, -1] < blocks[:, None, 0]).astype(jnp.int32), axis=1)
        return start, jnp.concatenate([(side * (LEN // BLK // 2))[None].astype(jnp.int32), low])

    start, info = line(ranges, segment_ids, seg_other)
    a1 = pair(a1_own, a1_came)
    own = tuple(line(project, a1, w_qkv, b_qv))
    qkv_mine, w_out_now, up_quarter, _ = lax.optimization_barrier((qkv_mine, w_out, up_quarter, own[0]))
    qkv_parts = share(qkv_mine)
    out_other = cross(w_out_now)
    up_mine = cross(up_quarter)
    own = own + tuple(line(partial(attn_fwd, info), *own, start))
    up_mine, down_quarter, _ = lax.optimization_barrier((up_mine, down_quarter, own[3]))
    up_parts = share(up_mine)
    down_mine = cross(down_quarter)
    qkv_other = line(assemble, qkv_mine, qkv_parts).reshape(w_qkv.shape)
    other = tuple(line(project, a1, qkv_other, small[: 2 * width].reshape(2, width)))
    other = other + tuple(line(partial(attn_fwd, info), *other, start))
    down_mine, dz_own, _ = lax.optimization_barrier((down_mine, out_grad, other[3]))
    down_parts = share(down_mine)
    dz_came = core(dz_own)

    here, there = line(partial(sum_dots, nn), [own[3], other[3]], [w_out, out_other])
    came = core(there)
    up_other = line(assemble, up_mine, up_parts)
    mixed, a2_own = line(second_norm, tokens, here, came, b_out[None], gains[1], shifts[1])
    a2_came = core(a2_own)
    dz = pair(dz_own, dz_came)
    a2 = pair(a2_own, a2_came)

    def core_halves(value):
        half = value.shape[0] // 2
        return core(value[:half]), core(value[half:])

    act_other, slope_other = line(up_gelu, a2, up_other, small[2 * width :])
    down_got = cross(line(across_frames, act_other, dz))
    act_own, slope_own = line(up_gelu, a2, w_up, b_up)
    down_own = line(across_frames, act_own, dz)
    du_own, sum_up_own = line(back_act, dz, w_down, slope_own)
    down_other = line(assemble, down_mine, down_parts)
    du_other, sum_up_other = line(back_act, dz, down_other, slope_other)
    here, there = line(partial(sum_dots, nt), [du_own, du_other], [w_up, up_other])
    came = core_halves(there)
    up_got = cross(line(across_frames, a2, du_other))
    grad_h, dattn_own, sums_h = line(norm_back, mixed, here, came, gains[1], out_grad)
    dattn_came = core_halves(dattn_own)
    up_own = line(across_frames, a2, du_own)

    def spread_y(own, got):
        return swap(line(side_sum, 1 - here_y, own, got), "y")

    def near_z(own, got, near):
        send, keep = line(quarter_sums, place, own, got, near)
        return keep, swap_z(send, 1)

    def far_z(keep, came):
        low = line(add_low, keep, came)
        return low, swap_z(low, 2)

    def back_z(low, came):
        mine = line(add_low, low, came)
        near = swap_z(mine, 1)
        return (mine, swap(mine, "y")), (near, swap(near, "y"))

    def put(pair, prior=None, extra=0):
        fill = partial(settle, flip=0 if prior is None else 1, extra=extra)
        return line(lambda mine, other, prior: fill(place, mine, other, prior=prior), *pair, prior)

    down_own, down_got = by_side(down_own), by_side(down_got)
    down_near = spread_y(down_own, down_got)
    dattn = pair(dattn_own, *dattn_came)

    def back(entry, weight):
        query, keys, values, out, lse = entry
        cot = line(turn_back, dattn, weight)
        trio = line(partial(attn_bwd, info), query, keys, values, start, out, lse, cot)
        return (trio,) + tuple(line(frame_sums, a1, trio, out, dattn))

    trio_other, attn_other, sum_trio_other = back(other, out_other)
    first_got = cross(attn_other[0])
    down_sum = near_z(down_own, down_got, down_near)
    y_here, y_there = line(partial(sum_dots, nn), [act_own, act_other], [w_down, down_other])
    y_came = core(y_there)
    query, keys, values, out, lse = own
    cot = line(turn_back, dattn, w_out)
    down_sum = far_z(*down_sum)
    up_own, up_got = by_side(up_own), by_side(up_got)
    up_near = spread_y(up_own, up_got)
    trio_own = line(partial(attn_bwd, info), query, keys, values, start, out, lse, cot)
    attn_own, sum_trio_own = line(frame_sums, a1, trio_own, out, dattn)
    first_own, first_got = by_side(attn_own[0]), by_side(first_got)
    down_sum = back_z(*down_sum)
    block_out = line(finish, mixed, y_here, y_came, b_down[None])
    first_near = spread_y(first_own, first_got)
    here, there = line(partial(sum_dots, nt), [trio_own, trio_other], [w_qkv, qkv_other])
    came = core_halves(there)
    up_sum = near_z(up_own, up_got, up_near)
    down_sum = down_sum[0], (line(lambda value: value, down_sum[1][0]), down_sum[1][1])
    grad_in, _, sums_x = line(norm_back, tokens, here, came, gains[0], grad_h)
    common = line(
        lambda h, z, x: jnp.concatenate([h[2], z[0], x[0], h[0], x[1], h[1]]), sums_h, sum_dz, sums_x
    )
    common_came = core(common)

    first_sum = near_z(first_own, first_got, first_near)
    up_sum = far_z(*up_sum)
    vectors = line(
        lambda mine, came, *parts: [
            jnp.concatenate([trio[0, 0], trio[2, 0], up[0], mine + came]) for trio, up in parts
        ],
        common, common_came, (sum_trio_own, sum_up_own), (sum_trio_other, sum_up_other),
    )
    second_other = line(ride, attn_other[1], vectors[1])
    second_got = cross(second_other)
    second_own = line(ride, attn_own[1], vectors[0])
    first_sum = far_z(*first_sum)
    grad_down = put(down_sum[0])
    grad_down = put(down_sum[1], grad_down)
    up_sum = back_z(*up_sum)
    second_own, second_got = by_side(second_own), by_side(second_got)
    second_near = spread_y(second_own, second_got)
    first_sum = back_z(*first_sum)
    second_sum = near_z(second_own, second_got, second_near)
    grad_up = put(up_sum[0])
    second_sum = far_z(*second_sum)
    first = put(first_sum[0], extra=wide)
    second_sum = back_z(*second_sum)
    grad_up = put(up_sum[1], grad_up)
    first = put(first_sum[1], first, extra=wide)
    second = put(second_sum[0])
    second = put(second_sum[1], second)
    grad_qkv = lax.dynamic_update_slice(first, second[:wide], (2 * wide, 0)).reshape(w_qkv.shape)
    grad_wout = jnp.swapaxes(second[wide : 2 * wide].reshape(-1, w_out.shape[0], width), 0, 1)
    grad_wout = grad_wout.reshape(w_out.shape)
    vector = second[2 * wide :].reshape(-1)
    units = b_up.shape[0]
    ends = [2 * width, units, wide, wide, 2 * wide, 2 * wide]
    cuts = [sum(ends[:i]) for i in range(len(ends) + 1)]
    grad_bqv, grad_bup, grad_bout, grad_bdown, grad_gain, grad_shift = [
        vector[low:high] for low, high in zip(cuts[:-1], cuts[1:])
    ]
    return (
        block_out,
        grad_in,
        grad_qkv,
        grad_bqv.reshape(b_qv.shape),
        grad_wout,
        grad_bout,
        grad_up,
        grad_bup,
        grad_down,
        grad_bdown,
        grad_gain.reshape(ln_gain.shape),
        grad_shift.reshape(ln_bias.shape),
    )


def solution(mesh):
    rows, frames = ("dp", "mp"), "mp"
    body = tensor_parallel_shards
    if row_per_chip(mesh):
        shape = (mesh.shape["dp"] // 2, 2, mesh.shape["mp"] // 2, 2)
        mesh = Mesh(mesh.devices.reshape(shape), ("z", "y", "x", "core"))
        rows, frames = ("z", "y", "x", "core"), ("x", "core")
        body = row_per_chip_shards
    in_specs = (
        P(rows, None),
        P(rows),
        P(None, None, frames),
        P(None, frames),
        P(frames, None),
        P(),
        P(None, frames),
        P(frames),
        P(frames, None),
        P(),
        P(),
        P(),
        P(rows, None),
    )
    out_specs = (
        P(rows, None),
        P(rows, None),
        P(None, None, frames),
        P(None, frames),
        P(frames, None),
        P(),
        P(None, frames),
        P(frames),
        P(frames, None),
        P(),
        P(),
        P(),
    )
    return jax.shard_map(body, mesh=mesh, in_specs=in_specs, out_specs=out_specs, check_vma=False)
```

```python
from functools import partial

import jax
import jax.numpy as jnp
from jax import lax
from jax.experimental import pallas as pl
from jax.experimental.pallas import tpu as pltpu
from jax.sharding import Mesh
from jax.sharding import PartitionSpec as P

HD = 64
LEN = 1024
QBLK = 512
EPS = 1e-05
BLK = 256

NEG = -1e30
GRANT = 10 << 20
EXTRA = 128
BRIEF = pl.CostEstimate(flops=1, bytes_accessed=1, transcendentals=0)
f32 = jnp.float32
bf16 = jnp.bfloat16


def nt(left, right):
    return lax.dot_general(left, right, (((1,), (1,)), ((), ())), preferred_element_type=f32)


def nn(left, right):
    return lax.dot_general(left, right, (((1,), (0,)), ((), ())), preferred_element_type=f32)


def tn(left, right):
    return lax.dot_general(left, right, (((0,), (0,)), ((), ())), preferred_element_type=f32)


def attn_bias(block, j, first):
    q_pos = block * BLK + lax.broadcasted_iota(jnp.int32, (1, BLK), 1)
    k_pos = j * BLK + lax.broadcasted_iota(jnp.int32, (BLK, BLK), 0)
    return jnp.where((k_pos >= first) & (k_pos <= q_pos), 0.0, NEG)


def head_rows(refs, scratch, heads):
    lane = lax.broadcasted_iota(jnp.int32, (LEN, 2 * HD), 1)
    for ref, out in zip(refs, scratch):
        for h in range(heads):
            pair = ref[:, (h // 2) * 2 * HD : (h // 2 + 1) * 2 * HD]
            out[h] = jnp.where((lane < HD) == (h % 2 == 0), pair, jnp.zeros_like(pair))


def attn_fwd_body(info, q_ref, k_ref, v_ref, st_ref, o_ref, lse_ref, k_heads, v_turned):
    block = pl.program_id(0)
    heads = q_ref.shape[1] // HD
    first = st_ref[...]

    @pl.when(block == 0)
    def _():
        head_rows([k_ref], [k_heads], heads)
        for pair in range(heads // 2):
            turned = v_ref[:, pair * 2 * HD : (pair + 1) * 2 * HD].T
            for h in (0, 1):
                v_turned[2 * pair + h, :HD] = turned[h * HD : (h + 1) * HD]
                v_turned[2 * pair + h, HD:] = jnp.ones((16, LEN), bf16)

    def step(at, carry):
        j = block - at
        row = pl.multiple_of((j ^ info[0]) * BLK, BLK)
        bias = attn_bias(block, j, first)
        out = []
        for h in range(heads):
            top, acc = carry[h]
            query = q_ref[:, (h // 2) * 2 * HD : (h // 2 + 1) * 2 * HD]
            s = nt(k_heads[h, pl.ds(row, BLK), :], query) + bias
            new = jnp.maximum(top, jnp.max(s, axis=0, keepdims=True))
            p = jnp.exp(s - new).astype(bf16)
            acc = acc * jnp.exp(top - new) + nn(v_turned[h, :, pl.ds(row, BLK)], p)
            out.append((new, acc))
        return tuple(out)

    init = tuple((jnp.full((1, BLK), NEG, f32), jnp.zeros((HD + 16, BLK), f32)) for _ in range(heads))
    done = lax.fori_loop(0, block + 1 - info[1 + block], step, init)
    for pair in range(heads // 2):
        both = [acc[:HD] / acc[HD : HD + 1] for _, acc in done[2 * pair : 2 * pair + 2]]
        o_ref[:, pair * 2 * HD : (pair + 1) * 2 * HD] = jnp.concatenate(both, axis=0).T.astype(bf16)
    for h in range(heads):
        top, acc = done[h]
        lse_ref[h : h + 1, :] = top + jnp.log(acc[HD : HD + 1])


def attn_bwd_body(base, info, q_ref, k_ref, v_ref, st_ref, o_ref, lse_ref, do_ref, d_ref, k_heads, v_heads, dk_acc, dv_acc):
    block = pl.program_id(0)
    heads = q_ref.shape[1] // HD
    first = st_ref[...]
    lane = lax.broadcasted_iota(jnp.int32, (BLK, 2 * HD), 1)

    @pl.when(block == 0)
    def _():
        head_rows([k_ref, v_ref], [k_heads, v_heads], heads)
        dk_acc[...] = jnp.zeros_like(dk_acc)
        dv_acc[...] = jnp.zeros_like(dv_acc)

    deltas = []
    for pair in range(heads // 2):
        cols = slice(pair * 2 * HD, (pair + 1) * 2 * HD)
        turned = (do_ref[:, cols].astype(f32) * o_ref[:, cols].astype(f32)).T
        for h in (0, 1):
            deltas.append(jnp.sum(turned[h * HD : (h + 1) * HD], axis=0, keepdims=True))

    def step(j, dqs):
        row = pl.multiple_of((j ^ info[0]) * BLK, BLK)
        bias = attn_bias(block, j, first)
        out = list(dqs)
        for pair in range(heads // 2):
            cols = slice(pair * 2 * HD, (pair + 1) * 2 * HD)
            query, cot = q_ref[:, cols], do_ref[:, cols]
            dk = dk_acc[pl.ds(row, BLK), cols]
            dv = dv_acc[pl.ds(row, BLK), cols]
            for h in (2 * pair, 2 * pair + 1):
                mask = (lane < HD) == (h % 2 == 0)
                keys = k_heads[h, pl.ds(row, BLK), :]
                p = jnp.exp(nt(keys, query) + (bias - lse_ref[base + h : base + h + 1, :]))
                dp = nt(v_heads[h, pl.ds(row, BLK), :], cot)
                ds = (p * (dp - deltas[h])).astype(bf16)
                dv = dv + nn(p.astype(bf16), jnp.where(mask, cot, jnp.zeros_like(cot)))
                dk = dk + nn(ds, jnp.where(mask, query, jnp.zeros_like(query)))
                out[pair] = out[pair] + tn(ds, keys)
            dk_acc[pl.ds(row, BLK), cols] = dk
            dv_acc[pl.ds(row, BLK), cols] = dv
        return tuple(out)

    init = tuple(jnp.zeros((BLK, 2 * HD), f32) for _ in range(heads // 2))
    dqs = lax.fori_loop(info[1 + block], block + 1, step, init)
    here = pl.multiple_of((block ^ info[0]) * BLK, BLK)
    for pair in range(heads // 2):
        cols = slice(pair * 2 * HD, (pair + 1) * 2 * HD)
        d_ref[0, pl.ds(here, BLK), cols] = (dqs[pair] * HD**-0.5).astype(bf16)

    @pl.when(block == pl.num_programs(0) - 1)
    def _():
        d_ref[1] = dk_acc[...].astype(bf16)
        d_ref[2] = dv_acc[...].astype(bf16)


def attn_specs(width):
    small = pl.BlockSpec((BLK, width), lambda i, info: (i ^ info[0], 0))
    whole = pl.BlockSpec((LEN, width), lambda i, info: (0, 0))
    start = pl.BlockSpec((1, BLK), lambda i, info: (0, i ^ info[0]))
    lse = pl.BlockSpec((width // HD, BLK), lambda i, info: (0, i ^ info[0]))
    return small, whole, start, lse


def attn_fwd(info, query, keys, values, start):
    width = query.shape[1]
    heads = width // HD
    small, whole, first, lse = attn_specs(width)
    return pl.pallas_call(
        attn_fwd_body,
        out_shape=(jax.ShapeDtypeStruct(query.shape, bf16), jax.ShapeDtypeStruct((heads, LEN), f32)),
        grid_spec=pltpu.PrefetchScalarGridSpec(
            num_scalar_prefetch=1,
            grid=(LEN // BLK,),
            in_specs=[small, whole, whole, first],
            out_specs=[small, lse],
            scratch_shapes=[pltpu.VMEM((heads, LEN, 2 * HD), bf16), pltpu.VMEM((heads, HD + 16, LEN), bf16)],
        ),
        cost_estimate=BRIEF,
        compiler_params=pltpu.CompilerParams(vmem_limit_bytes=GRANT),
        name="attn_fwd",
    )(info, query, keys, values, start)


def attn_bwd(info, query, keys, values, start, out, lse, cot, part=0, parts=1, prior=None):
    width = query.shape[1] // parts
    heads = width // HD
    small = pl.BlockSpec((BLK, width), lambda i, info: (i ^ info[0], part))
    whole = pl.BlockSpec((LEN, width), lambda i, info: (0, part))
    first = pl.BlockSpec((1, BLK), lambda i, info: (0, i ^ info[0]))
    lse_spec = pl.BlockSpec((heads * parts, BLK), lambda i, info: (0, i ^ info[0]))
    more = () if prior is None else (prior,)

    def body(*refs):
        attn_bwd_body(part * heads, *refs[:8], *refs[8 + len(more) :])

    return pl.pallas_call(
        body,
        out_shape=jax.ShapeDtypeStruct((3,) + query.shape, bf16),
        grid_spec=pltpu.PrefetchScalarGridSpec(
            num_scalar_prefetch=1,
            grid=(LEN // BLK,),
            in_specs=[small, whole, whole, first, small, lse_spec, small]
            + [pl.BlockSpec(memory_space=pl.ANY)] * len(more),
            out_specs=pl.BlockSpec((3, LEN, width), lambda i, info: (0, 0, part)),
            scratch_shapes=[
                pltpu.VMEM((heads, LEN, 2 * HD), bf16),
                pltpu.VMEM((heads, LEN, 2 * HD), bf16),
                pltpu.VMEM((LEN, width), f32),
                pltpu.VMEM((LEN, width), f32),
            ],
        ),
        input_output_aliases={8: 0} if more else {},
        cost_estimate=BRIEF,
        compiler_params=pltpu.CompilerParams(vmem_limit_bytes=GRANT),
        name="attn_bwd",
    )(info, query, keys, values, start, out, lse, cot, *more)


def up_body(a_ref, w_ref, b_ref, g_ref, s_ref):
    rows = a_ref[...]
    for part in range(w_ref.shape[1] // 256):
        cols = slice(part * 256, part * 256 + 256)
        u = nn(rows, w_ref[:, cols]) + b_ref[:, cols].astype(f32)
        size = jnp.abs(u)
        t = 1.0 / (1.0 + 0.3275911 * 0.7071067811865476 * size)
        poly = t * (0.5 * 0.254829592 + t * (0.5 * -0.284496736 + t * (0.5 * 1.421413741 + t * (0.5 * -1.453152027 + t * (0.5 * 1.061405429)))))
        bell = jnp.exp(-0.5 * u * u)
        tail = poly * bell
        cdf = jnp.where(u >= 0, 1.0 - tail, tail)
        g_ref[:, cols] = (u * cdf).astype(bf16)
        s_ref[:, cols] = (cdf + u * bell * 0.3989422804014327).astype(bf16)


def up_gelu(rows, weight, bias):
    m, k = rows.shape
    n = weight.shape[1]
    bm = 256
    shape = jax.ShapeDtypeStruct((m, n), bf16)
    tile = pl.BlockSpec((bm, n), lambda i: (i, 0))
    return pl.pallas_call(
        up_body,
        out_shape=(shape, shape),
        grid=(m // bm,),
        in_specs=[pl.BlockSpec((bm, k), lambda i: (i, 0)), pl.BlockSpec((k, n), lambda i: (0, 0)), pl.BlockSpec((1, n), lambda i: (0, 0))],
        out_specs=(tile, tile),
        cost_estimate=BRIEF,
        compiler_params=pltpu.CompilerParams(vmem_limit_bytes=GRANT),
        name="up_gelu",
    )(rows, weight, bias.reshape(1, n))


def const_spec(shape):
    return pl.BlockSpec(shape, lambda i: (0,) * len(shape))


def row_spec(rows, cols):
    return pl.BlockSpec((rows, cols), lambda i: (i, 0))


def project_body(a_ref, w_ref, b_ref, q_ref, k_ref, v_ref):
    rows = a_ref[...]
    q_ref[...] = (nn(rows, w_ref[0]) + b_ref[0:1].astype(f32)).astype(bf16) * jnp.bfloat16(HD**-0.5)
    k_ref[...] = nn(rows, w_ref[1]).astype(bf16)
    v_ref[...] = (nn(rows, w_ref[2]) + b_ref[1:2].astype(f32)).astype(bf16)


def project(rows, weight, bias):
    m, k = rows.shape
    n = weight.shape[2]
    tile = 256
    shape = jax.ShapeDtypeStruct((m, n), bf16)
    return pl.pallas_call(
        project_body,
        out_shape=(shape, shape, shape),
        grid=(m // tile,),
        in_specs=[row_spec(tile, k), const_spec(weight.shape), const_spec(bias.shape)],
        out_specs=[row_spec(tile, n)] * 3,
        cost_estimate=BRIEF,
        compiler_params=pltpu.CompilerParams(vmem_limit_bytes=GRANT),
        name="project",
    )(rows, weight, bias)


def sum_dots(product, lefts, rights):
    stacked = lefts[0].ndim == 3
    m, k = lefts[0].shape[-2:]
    n = rights[0].shape[-1] if product is nn else rights[0].shape[-2]
    terms = len(lefts)
    tile = 256
    steps = m // tile // 2

    def body(*refs):
        total = None
        for left, right in zip(refs[:terms], refs[terms : 2 * terms]):
            for at in range(left.shape[0] if stacked else 1):
                term = product(left[at], right[at]) if stacked else product(left[...], right[...])
                total = term if total is None else total + term
        here, there = refs[2 * terms :]

        @pl.when(pl.program_id(0) < steps)
        def _():
            there[...] = total.astype(bf16)

        @pl.when(pl.program_id(0) >= steps)
        def _():
            here[...] = total

    def turn(i):
        return jnp.where(i < steps, i + steps, i - steps)

    if stacked:
        left_spec = pl.BlockSpec((lefts[0].shape[0], tile, k), lambda i: (0, turn(i), 0))
    else:
        left_spec = pl.BlockSpec((tile, k), lambda i: (turn(i), 0))
    return pl.pallas_call(
        body,
        out_shape=(jax.ShapeDtypeStruct((m // 2, n), f32), jax.ShapeDtypeStruct((m // 2, n), bf16)),
        grid=(2 * steps,),
        in_specs=[left_spec] * terms + [const_spec(r.shape) for r in rights],
        out_specs=[
            pl.BlockSpec((tile, n), lambda i: (jnp.maximum(i - steps, 0), 0)),
            pl.BlockSpec((tile, n), lambda i: (jnp.minimum(i, steps - 1), 0)),
        ],
        cost_estimate=BRIEF,
        compiler_params=pltpu.CompilerParams(vmem_limit_bytes=GRANT),
        name="sum_dots",
    )(*lefts, *rights)


def center_rows(rows):
    center = rows - jnp.mean(rows, axis=-1, keepdims=True)
    scale = lax.rsqrt(jnp.mean(center * center, axis=-1, keepdims=True) + EPS)
    return center * scale, scale


def first_norm_body(x_ref, g_ref, gain_ref, shift_ref, a_ref, sum_ref):
    normal, _ = center_rows(x_ref[...].astype(f32))
    a_ref[...] = (normal * gain_ref[...] + shift_ref[...]).astype(bf16)

    @pl.when(pl.program_id(0) == 0)
    def _():
        sum_ref[...] = jnp.zeros_like(sum_ref)

    sum_ref[...] += jnp.sum(g_ref[...].astype(f32), axis=0, keepdims=True)


def first_norm(tokens, cotangent, gain, shift):
    m, d = tokens.shape
    tile = 128
    return pl.pallas_call(
        first_norm_body,
        out_shape=(jax.ShapeDtypeStruct((m, d), bf16), jax.ShapeDtypeStruct((1, d), f32)),
        grid=(m // tile,),
        in_specs=[row_spec(tile, d), row_spec(tile, d), const_spec((1, d)), const_spec((1, d))],
        out_specs=[row_spec(tile, d), const_spec((1, d))],
        cost_estimate=BRIEF,
        compiler_params=pltpu.CompilerParams(vmem_limit_bytes=GRANT),
        name="first_norm",
    )(tokens, cotangent, gain, shift)


def second_norm_body(x_ref, here_ref, came_ref, b_ref, gain_ref, shift_ref, h_ref, a_ref):
    mixed = x_ref[...].astype(f32) + (here_ref[...] + came_ref[...].astype(f32)) + b_ref[...].astype(f32)
    h_ref[...] = mixed
    normal, _ = center_rows(mixed)
    a_ref[...] = (normal * gain_ref[...] + shift_ref[...]).astype(bf16)


def second_norm(tokens, here, came, bias, gain, shift):
    m, d = tokens.shape
    tile = 128
    return pl.pallas_call(
        second_norm_body,
        out_shape=(jax.ShapeDtypeStruct((m, d), f32), jax.ShapeDtypeStruct((m, d), bf16)),
        grid=(m // tile,),
        in_specs=[row_spec(tile, d)] * 3 + [const_spec((1, d))] * 3,
        out_specs=[row_spec(tile, d)] * 2,
        cost_estimate=BRIEF,
        compiler_params=pltpu.CompilerParams(vmem_limit_bytes=GRANT),
        name="second_norm",
    )(tokens, here, came, bias, gain, shift)


def norm_back_body(v_ref, here_ref, low_came_ref, high_came_ref, gain_ref, res_ref, out_ref, low_ref, sums_ref):
    normal, scale = center_rows(v_ref[...].astype(f32))
    first = pl.program_id(0) < pl.num_programs(0) // 2
    came = jnp.where(first, low_came_ref[...], high_came_ref[...])
    grad = here_ref[...] + came.astype(f32)
    scaled = grad * gain_ref[...]
    inner = jnp.mean(scaled * normal, axis=-1, keepdims=True)
    back = scale * (scaled - jnp.mean(scaled, axis=-1, keepdims=True) - normal * inner)
    back = back + res_ref[...].astype(f32)
    low = back.astype(bf16)
    out_ref[...] = back
    low_ref[...] = low

    @pl.when(pl.program_id(0) == 0)
    def _():
        sums_ref[...] = jnp.zeros_like(sums_ref)

    sums_ref[0:1] += jnp.sum(grad * normal, axis=0, keepdims=True)
    sums_ref[1:2] += jnp.sum(grad, axis=0, keepdims=True)
    sums_ref[2:3] += jnp.sum(low.astype(f32), axis=0, keepdims=True)


def norm_back(values, here, came, gain, residual):
    m, d = values.shape
    tile = 128
    half = m // tile // 2
    low = pl.BlockSpec((tile, d), lambda i: (jnp.minimum(i, half - 1), 0))
    high = pl.BlockSpec((tile, d), lambda i: (jnp.maximum(i - half, 0), 0))
    return pl.pallas_call(
        norm_back_body,
        out_shape=(
            jax.ShapeDtypeStruct((m, d), f32),
            jax.ShapeDtypeStruct((m, d), bf16),
            jax.ShapeDtypeStruct((8, d), f32),
        ),
        grid=(m // tile,),
        in_specs=[row_spec(tile, d)] * 2 + [low, high, const_spec((1, d)), row_spec(tile, d)],
        out_specs=[row_spec(tile, d)] * 2 + [const_spec((8, d))],
        cost_estimate=BRIEF,
        compiler_params=pltpu.CompilerParams(vmem_limit_bytes=GRANT),
        name="norm_back",
    )(values, here, *came, gain, residual)


def back_act_body(z_ref, w_ref, s_ref, du_ref, sum_ref):
    du = (nt(z_ref[...], w_ref[...]) * s_ref[...].astype(f32)).astype(bf16)
    du_ref[...] = du

    @pl.when(pl.program_id(0) == 0)
    def _():
        sum_ref[...] = jnp.zeros_like(sum_ref)

    sum_ref[...] += jnp.sum(du.astype(f32), axis=0, keepdims=True)


def back_act(cotangent, weight, slope):
    m, d = cotangent.shape
    n = weight.shape[0]
    tile = 256
    return pl.pallas_call(
        back_act_body,
        out_shape=(jax.ShapeDtypeStruct((m, n), bf16), jax.ShapeDtypeStruct((1, n), f32)),
        grid=(m // tile,),
        in_specs=[row_spec(tile, d), const_spec((n, d)), row_spec(tile, n)],
        out_specs=[row_spec(tile, n), const_spec((1, n))],
        cost_estimate=BRIEF,
        compiler_params=pltpu.CompilerParams(vmem_limit_bytes=GRANT),
        name="back_act",
    )(cotangent, weight, slope)


def frame_sums_body(a_ref, d_ref, o_ref, g_ref, one_ref, two_ref, sums_ref, a_turned):
    rows, width = g_ref.shape[1], o_ref.shape[1]
    count = rows // width
    a_turned[...] = a_ref[...].T
    for at in range(4 * count):
        kind, part = divmod(at, count)
        out = one_ref if at < 2 * count else two_ref
        if kind < 3:
            block = nn(a_turned[part * width : (part + 1) * width, :], d_ref[kind])
        else:
            block = tn(o_ref[...], g_ref[:, part * width : (part + 1) * width])
        low = (at % (2 * count)) * width
        out[low : low + width, :] = block.astype(bf16)
    two_ref[2 * rows :, :] = jnp.zeros((EXTRA, width), bf16)
    for kind in range(3):
        sums_ref[kind] = jnp.sum(d_ref[kind].astype(f32), axis=0, keepdims=True)


def frame_sums(rows, trio, out, cotangent):
    t, d = rows.shape
    n = trio.shape[2]
    half = jax.ShapeDtypeStruct((2 * d, n), bf16)
    one, two, sums = pl.pallas_call(
        frame_sums_body,
        out_shape=(half, jax.ShapeDtypeStruct((2 * d + EXTRA, n), bf16), jax.ShapeDtypeStruct((3, 1, n), f32)),
        grid=(1,),
        in_specs=[const_spec((t, d)), const_spec((3, t, n)), const_spec((t, n)), const_spec((t, d))],
        out_specs=[const_spec((2 * d, n)), const_spec((2 * d + EXTRA, n)), const_spec((3, 1, n))],
        scratch_shapes=[pltpu.VMEM((d, t), bf16)],
        cost_estimate=BRIEF,
        compiler_params=pltpu.CompilerParams(vmem_limit_bytes=GRANT),
        name="frame_sums",
    )(rows, trio, out, cotangent)
    return (one, two), sums


def frames_body(a_ref, g_ref, out_ref, turned):
    tile = out_ref.shape[0]
    turned[...] = a_ref[...].T
    out_ref[...] = nn(turned[...], g_ref[...]).astype(bf16)


def across_frames(left, right):
    t, m = left.shape
    n = right.shape[1]
    tile = 256
    return pl.pallas_call(
        frames_body,
        out_shape=jax.ShapeDtypeStruct((m, n), bf16),
        grid=(m // tile,),
        in_specs=[pl.BlockSpec((t, tile), lambda i: (0, i)), const_spec((t, n))],
        out_specs=row_spec(tile, n),
        scratch_shapes=[pltpu.VMEM((tile, t), bf16)],
        cost_estimate=BRIEF,
        compiler_params=pltpu.CompilerParams(vmem_limit_bytes=GRANT),
        name="across_frames",
    )(left, right)


def turn_back_body(a_ref, w_ref, out_ref):
    out_ref[...] = nt(a_ref[...], w_ref[...]).astype(bf16)


def turn_back(rows, weight):
    m, k = rows.shape
    n = weight.shape[0]
    tile = 256
    return pl.pallas_call(
        turn_back_body,
        out_shape=jax.ShapeDtypeStruct((m, n), bf16),
        grid=(m // tile,),
        in_specs=[row_spec(tile, k), const_spec((n, k))],
        out_specs=row_spec(tile, n),
        cost_estimate=BRIEF,
        compiler_params=pltpu.CompilerParams(vmem_limit_bytes=GRANT),
        name="turn_back",
    )(rows, weight)


def side_sum_body(info, *refs):
    total = refs[0][0].astype(f32)
    for ref in refs[1:-1]:
        total = total + (ref[0] if len(ref.shape) == 3 else ref[...]).astype(f32)
    refs[-1][...] = total.astype(bf16)


def side_sum(side, own, got, near=None):
    _, rows, cols = own.shape
    tile = rows // 4
    pick_spec = pl.BlockSpec((1, tile, cols), lambda i, info: (info[0], i, 0))
    flat = pl.BlockSpec((tile, cols), lambda i, info: (i, 0))
    args = [own, got] + ([] if near is None else [near])
    return pl.pallas_call(
        side_sum_body,
        out_shape=jax.ShapeDtypeStruct((rows, cols), bf16),
        grid_spec=pltpu.PrefetchScalarGridSpec(
            num_scalar_prefetch=1,
            grid=(4,),
            in_specs=[pick_spec, pick_spec] + [flat] * (len(args) - 2),
            out_specs=flat,
        ),
        cost_estimate=BRIEF,
        compiler_params=pltpu.CompilerParams(vmem_limit_bytes=GRANT),
        name="side_sum",
    )(side[None], *args)


def add_low_body(a_ref, b_ref, out_ref):
    out_ref[...] = (a_ref[...].astype(f32) + b_ref[...].astype(f32)).astype(bf16)


def add_low(left, right):
    rows, cols = left.shape
    tile = rows // 2
    return pl.pallas_call(
        add_low_body,
        out_shape=jax.ShapeDtypeStruct((rows, cols), bf16),
        grid=(2,),
        in_specs=[row_spec(tile, cols)] * 2,
        out_specs=row_spec(tile, cols),
        cost_estimate=BRIEF,
        compiler_params=pltpu.CompilerParams(vmem_limit_bytes=GRANT),
        name="add_low",
    )(left, right)


def quarter_sums_body(info, own_ref, got_ref, near_ref, send_ref, keep_ref):
    total = own_ref[0, 0].astype(f32) + got_ref[0, 0].astype(f32) + near_ref[0].astype(f32)

    @pl.when(pl.program_id(0) == 0)
    def _():
        send_ref[...] = total.astype(bf16)

    @pl.when(pl.program_id(0) == 1)
    def _():
        keep_ref[...] = total.astype(bf16)


def quarter_sums(place, own, got, near):
    _, rows, cols = own.shape
    rows = rows // 2
    tile = rows // 2
    deep = pl.BlockSpec((1, 1, tile, cols), lambda f, i, info: (info[0], info[1] ^ 1 ^ f, i, 0))
    flat = pl.BlockSpec((1, tile, cols), lambda f, i, info: (info[1] ^ 1 ^ f, i, 0))
    shape = jax.ShapeDtypeStruct((rows, cols), bf16)
    return pl.pallas_call(
        quarter_sums_body,
        out_shape=(shape, shape),
        grid_spec=pltpu.PrefetchScalarGridSpec(
            num_scalar_prefetch=1,
            grid=(2, 2),
            in_specs=[deep, deep, flat],
            out_specs=[
                pl.BlockSpec((tile, cols), lambda f, i, info: (jnp.where(f == 0, i, 1), 0)),
                pl.BlockSpec((tile, cols), lambda f, i, info: (jnp.where(f == 0, 0, i), 0)),
            ],
        ),
        cost_estimate=BRIEF,
        compiler_params=pltpu.CompilerParams(vmem_limit_bytes=GRANT),
        name="quarter_sums",
    )(place, own.reshape(2, 2, rows, cols), got.reshape(2, 2, rows, cols), near.reshape(2, rows, cols))


def settle_body(info, mine_ref, other_ref, *rest):
    for at, ref in enumerate((mine_ref, other_ref)):

        @pl.when(pl.program_id(0) == at)
        def _(ref=ref):
            rest[-1][0] = ref[...].astype(f32)


def settle(place, mine, other, flip=0, prior=None, extra=0):
    rows, cols = mine.shape
    tile = rows // 2
    first = pl.BlockSpec((tile, cols), lambda f, i, info: (jnp.where(f == 0, i, 1), 0))
    second = pl.BlockSpec((tile, cols), lambda f, i, info: (jnp.where(f == 0, 0, i), 0))
    more = () if prior is None else (prior.reshape(-1, rows, cols),)
    out = pl.pallas_call(
        settle_body,
        out_shape=jax.ShapeDtypeStruct((4 + extra // rows, rows, cols), f32),
        grid_spec=pltpu.PrefetchScalarGridSpec(
            num_scalar_prefetch=1,
            grid=(2, 2),
            in_specs=[first, second] + [pl.BlockSpec(memory_space=pl.ANY)] * len(more),
            out_specs=pl.BlockSpec(
                (1, tile, cols), lambda f, i, info: (2 * (info[0] ^ f) + (info[1] ^ flip), i, 0)
            ),
        ),
        input_output_aliases={3: 0} if more else {},
        cost_estimate=BRIEF,
        compiler_params=pltpu.CompilerParams(vmem_limit_bytes=GRANT),
        name="settle",
    )(place, mine, other, *more)
    return out.reshape(-1, cols)


def finish_body(h_ref, here_ref, came_ref, b_ref, out_ref):
    out_ref[...] = (h_ref[...] + here_ref[...] + came_ref[...].astype(f32) + b_ref[...].astype(f32)).astype(bf16)


def finish(mixed, here, came, bias):
    m, d = mixed.shape
    tile = 128
    return pl.pallas_call(
        finish_body,
        out_shape=jax.ShapeDtypeStruct((m, d), bf16),
        grid=(m // tile,),
        in_specs=[row_spec(tile, d)] * 3 + [const_spec((1, d))],
        out_specs=row_spec(tile, d),
        cost_estimate=BRIEF,
        compiler_params=pltpu.CompilerParams(vmem_limit_bytes=GRANT),
        name="finish",
    )(mixed, here, came, bias)


def common_body(h_ref, z_ref, x_ref, out_ref):
    out_ref[...] = jnp.zeros_like(out_ref)
    rows = [h_ref[2:3], z_ref[0:1], x_ref[0:1], h_ref[0:1], x_ref[1:2], h_ref[1:2]]
    for at, row in enumerate(rows):
        out_ref[at : at + 1] = row


def common_rows(sums_h, sum_dz, sums_x):
    return pl.pallas_call(
        common_body,
        out_shape=jax.ShapeDtypeStruct(sums_h.shape, f32),
        cost_estimate=BRIEF,
        compiler_params=pltpu.CompilerParams(vmem_limit_bytes=GRANT),
        name="common_rows",
    )(sums_h, sum_dz, sums_x)


def ride_body(trio_ref, up_ref, mine_ref, came_ref, whole_ref, out_ref, lines):
    cols = out_ref.shape[1]
    lines[...] = jnp.zeros_like(lines)
    lines[0:1] = trio_ref[0]
    lines[1:2] = trio_ref[2]
    at = 2
    for part in range(up_ref.shape[1] // cols):
        lines[at : at + 1] = up_ref[:, part * cols : (part + 1) * cols]
        at += 1
    both = mine_ref[...] + came_ref[...]
    for row in range(6):
        for part in range(both.shape[1] // cols):
            lines[at : at + 1] = both[row : row + 1, part * cols : (part + 1) * cols]
            at += 1
    out_ref[...] = lines[...].astype(bf16)


def ride(whole, trio, up, mine, came):
    rows, cols = whole.shape
    return pl.pallas_call(
        ride_body,
        out_shape=jax.ShapeDtypeStruct((rows, cols), bf16),
        grid=(1,),
        in_specs=[const_spec(value.shape) for value in (trio, up, mine, came)]
        + [pl.BlockSpec(memory_space=pl.ANY)],
        out_specs=pl.BlockSpec((EXTRA, cols), lambda i: (rows // EXTRA - 1, 0)),
        scratch_shapes=[pltpu.VMEM((EXTRA, cols), f32)],
        input_output_aliases={4: 0},
        cost_estimate=BRIEF,
        compiler_params=pltpu.CompilerParams(vmem_limit_bytes=GRANT),
        name="ride",
    )(trio, up, mine, came, whole)


def norm_rows(values, gain, shift):
    center = values - jnp.mean(values, axis=-1, keepdims=True)
    spread = jnp.mean(center * center, axis=-1, keepdims=True)
    return center * lax.rsqrt(spread + EPS) * gain + shift


def split_heads(flat, rows):
    return flat.reshape(rows, LEN, flat.shape[1] // HD, HD)


def block_scores(query, keys, seg_q, seg_k, offset):
    scores = jnp.einsum(
        "rqhd,rkhd->rhqk", query, keys, preferred_element_type=jnp.float32
    ) * HD ** (-0.5)
    q_pos = offset + jnp.arange(query.shape[1], dtype=jnp.int32)
    k_pos = jnp.arange(keys.shape[1], dtype=jnp.int32)
    allowed = (seg_q[:, :, None] == seg_k[:, None, :]) & (
        k_pos[None, None, :] <= q_pos[None, :, None]
    )
    return jnp.where(allowed[:, None], scores, -1e30)


def attention_forward(query, keys, values, seg_all):
    rows = query.shape[0] // LEN
    q4 = split_heads(query, rows)
    k4 = split_heads(keys, rows)
    v4 = split_heads(values, rows)
    seg2 = seg_all.reshape(rows, LEN)
    outputs = []
    totals = []
    for block in range(LEN // QBLK):
        first = block * QBLK
        end = first + QBLK
        scores = block_scores(
            q4[:, first:end], k4[:, :end], seg2[:, first:end], seg2[:, :end], first
        )
        top = jnp.max(scores, axis=-1, keepdims=True)
        expd = jnp.exp(scores - top)
        summed = jnp.sum(expd, axis=-1, keepdims=True)
        weights = (expd / summed).astype(jnp.bfloat16)
        outputs.append(
            jnp.einsum("rhqk,rkhd->rqhd", weights, v4[:, :end], preferred_element_type=jnp.float32)
        )
        totals.append(top + jnp.log(summed))
    attended = jnp.concatenate(outputs, axis=1).reshape(query.shape).astype(jnp.bfloat16)
    return (attended, totals)


def attention_backward(query, keys, values, seg_all, totals, grad_att):
    rows = query.shape[0] // LEN
    q4 = split_heads(query, rows)
    k4 = split_heads(keys, rows)
    v4 = split_heads(values, rows)
    g4 = split_heads(grad_att, rows)
    seg2 = seg_all.reshape(rows, LEN)
    scale = HD ** (-0.5)
    grad_k = jnp.zeros(k4.shape, jnp.float32)
    grad_v = jnp.zeros(v4.shape, jnp.float32)
    grad_q_parts = []
    for block in range(LEN // QBLK):
        first = block * QBLK
        end = first + QBLK
        scores = block_scores(
            q4[:, first:end], k4[:, :end], seg2[:, first:end], seg2[:, :end], first
        )
        probs = jnp.exp(scores - totals[block])
        weights = probs.astype(jnp.bfloat16)
        grad_w = jnp.einsum(
            "rqhd,rkhd->rhqk", g4[:, first:end], v4[:, :end], preferred_element_type=jnp.float32
        )
        delta = jnp.sum(probs * grad_w, axis=-1, keepdims=True)
        grad_s = (probs * (grad_w - delta)).astype(jnp.bfloat16)
        grad_q_parts.append(
            jnp.einsum("rhqk,rkhd->rqhd", grad_s, k4[:, :end], preferred_element_type=jnp.float32)
            * scale
        )
        padding = ((0, 0), (0, LEN - end), (0, 0), (0, 0))
        grad_k = grad_k + jnp.pad(
            jnp.einsum(
                "rhqk,rqhd->rkhd", grad_s, q4[:, first:end], preferred_element_type=jnp.float32
            )
            * scale,
            padding,
        )
        grad_v = grad_v + jnp.pad(
            jnp.einsum(
                "rhqk,rqhd->rkhd", weights, g4[:, first:end], preferred_element_type=jnp.float32
            ),
            padding,
        )
    shape = query.shape
    grad_q = jnp.concatenate(grad_q_parts, axis=1).reshape(shape).astype(jnp.bfloat16)
    return (
        grad_q,
        grad_k.reshape(shape).astype(jnp.bfloat16),
        grad_v.reshape(shape).astype(jnp.bfloat16),
    )


def tensor_parallel_shards(
    tokens,
    segment_ids,
    w_qkv,
    b_qv,
    w_out,
    b_out,
    w_up,
    b_up,
    w_down,
    b_down,
    ln_gain,
    ln_bias,
    out_grad,
):
    resid = tokens.astype(jnp.float32)
    qv_bias = b_qv.astype(jnp.float32)
    up_bias = b_up.astype(jnp.float32)
    local_rows = tokens.shape[0]
    normed, first_back = jax.vjp(norm_rows, resid, ln_gain[0], ln_bias[0])
    lowered = normed.astype(jnp.bfloat16)
    joined, seg_all = (
        lax.all_gather(lowered, "mp", axis=0, tiled=True),
        lax.all_gather(segment_ids, "mp", axis=0, tiled=True),
    )
    query = (jnp.dot(joined, w_qkv[0], preferred_element_type=jnp.float32) + qv_bias[0]).astype(
        jnp.bfloat16
    )
    keys = jnp.dot(joined, w_qkv[1], preferred_element_type=jnp.float32).astype(jnp.bfloat16)
    values = (jnp.dot(joined, w_qkv[2], preferred_element_type=jnp.float32) + qv_bias[1]).astype(
        jnp.bfloat16
    )
    query, keys, values = (query, keys, values)
    attended, totals = attention_forward(query, keys, values, seg_all)
    attn_sum = lax.psum_scatter(
        jnp.dot(attended, w_out, preferred_element_type=jnp.float32).astype(jnp.bfloat16),
        "mp",
        scatter_dimension=0,
        tiled=True,
    ).astype(jnp.float32)
    mixed = resid + attn_sum + b_out.astype(jnp.float32)
    normed2, second_back = jax.vjp(norm_rows, mixed, ln_gain[1], ln_bias[1])
    lowered2 = normed2.astype(jnp.bfloat16)
    joined2 = lax.all_gather(lowered2, "mp", axis=0, tiled=True)
    pre_act = jnp.dot(joined2, w_up, preferred_element_type=jnp.float32) + up_bias
    pre_act, activ = (pre_act, jax.nn.gelu(pre_act, approximate=False).astype(jnp.bfloat16))
    block_out = (
        mixed
        + lax.psum_scatter(
            jnp.dot(activ, w_down, preferred_element_type=jnp.float32).astype(jnp.bfloat16),
            "mp",
            scatter_dimension=0,
            tiled=True,
        ).astype(jnp.float32)
        + b_down.astype(jnp.float32)
    ).astype(jnp.bfloat16)
    grad_y = out_grad.astype(jnp.float32)
    grad_z = lax.all_gather(out_grad, "mp", axis=0, tiled=True)
    grad_down = jnp.einsum("tf,td->fd", activ, grad_z, preferred_element_type=jnp.float32)
    grad_bdown = jnp.sum(grad_z, axis=0, dtype=jnp.float32)
    grad_act = jnp.einsum("td,fd->tf", grad_z, w_down, preferred_element_type=jnp.float32)
    gelu_back = jax.vjp(lambda value: jax.nn.gelu(value, approximate=False), pre_act)[1]
    grad_pre = gelu_back(grad_act)[0].astype(jnp.bfloat16)
    grad_up = jnp.einsum("td,tf->df", joined2, grad_pre, preferred_element_type=jnp.float32)
    grad_bup = jnp.sum(grad_pre, axis=0, dtype=jnp.float32)
    grad_n2 = lax.psum_scatter(
        jnp.einsum("tf,df->td", grad_pre, w_up, preferred_element_type=jnp.float32).astype(
            jnp.bfloat16
        ),
        "mp",
        scatter_dimension=0,
        tiled=True,
    ).astype(jnp.float32)
    grad_h, grad_g2, grad_s2 = second_back(grad_n2)
    grad_h = grad_h + grad_y
    grad_branch = lax.all_gather(grad_h.astype(jnp.bfloat16), "mp", axis=0, tiled=True)
    grad_wout = jnp.einsum("tc,td->cd", attended, grad_branch, preferred_element_type=jnp.float32)
    grad_bout = jnp.sum(grad_branch, axis=0, dtype=jnp.float32)
    grad_att = jnp.einsum(
        "td,cd->tc", grad_branch, w_out, preferred_element_type=jnp.float32
    ).astype(jnp.bfloat16)
    grad_q, grad_k, grad_v = attention_backward(query, keys, values, seg_all, totals, grad_att)
    grad_qkv = jnp.stack(
        [
            jnp.einsum("td,tc->dc", joined, piece, preferred_element_type=jnp.float32)
            for piece in (grad_q, grad_k, grad_v)
        ]
    )
    grad_bqv = jnp.stack(
        [jnp.sum(grad_q, axis=0, dtype=jnp.float32), jnp.sum(grad_v, axis=0, dtype=jnp.float32)]
    )
    summed = jnp.zeros((local_rows * lax.axis_size("mp"), w_qkv.shape[1]), jnp.float32)
    for index, piece in enumerate((grad_q, grad_k, grad_v)):
        summed = summed + jnp.einsum(
            "tc,dc->td", piece, w_qkv[index], preferred_element_type=jnp.float32
        )
    grad_n1 = lax.psum_scatter(
        summed.astype(jnp.bfloat16), "mp", scatter_dimension=0, tiled=True
    ).astype(jnp.float32)
    grad_x, grad_g1, grad_s1 = first_back(grad_n1)
    grad_in = grad_x + grad_h
    weight_totals = (
        lax.psum(grad_qkv.astype(jnp.bfloat16), "dp").astype(jnp.float32),
        lax.psum(grad_bqv.astype(jnp.bfloat16), "dp").astype(jnp.float32),
        lax.psum(grad_wout.astype(jnp.bfloat16), "dp").astype(jnp.float32),
        lax.psum(grad_bout.astype(jnp.bfloat16), "dp").astype(jnp.float32),
        lax.psum(grad_up.astype(jnp.bfloat16), "dp").astype(jnp.float32),
        lax.psum(grad_bup.astype(jnp.bfloat16), "dp").astype(jnp.float32),
        lax.psum(grad_down.astype(jnp.bfloat16), "dp").astype(jnp.float32),
        lax.psum(grad_bdown.astype(jnp.bfloat16), "dp").astype(jnp.float32),
    )
    norm_totals = lax.psum(
        (jnp.stack([grad_g1, grad_g2]), jnp.stack([grad_s1, grad_s2])), ("dp", "mp")
    )
    return (block_out, grad_in) + tuple(weight_totals) + tuple(norm_totals)


def row_per_chip(mesh):
    return mesh.shape["mp"] == 4 and mesh.shape["dp"] == 8


def swap(value, axis):
    return lax.ppermute(value, axis, [(0, 1), (1, 0)])


def core(value):
    return swap(value, "core")


def cross(value):
    return swap(value, "x")


def after(value, *others):
    return lax.optimization_barrier((value,) + others)[0]


def take(value, at):
    return lax.dynamic_index_in_dim(value, at, 0, keepdims=False)


def place(whole, piece, at):
    return lax.dynamic_update_index_in_dim(whole, piece, at, 0)


def quarter_of(weight):
    me = lax.axis_index("y") + 2 * (lax.axis_index("z") & 1)
    return take(weight.reshape(4, -1, weight.shape[-1]), me)


def share(mine):
    out = [swap(mine, "y")]
    for bits in (2, 3):
        out.append(lax.ppermute(mine, ("z", "y"), [(i, i ^ bits) for i in range(8)]))
    return out


def assemble(mine, others):
    me = lax.axis_index("y") + 2 * (lax.axis_index("z") & 1)
    whole = place(jnp.zeros((4,) + mine.shape, mine.dtype), mine, me)
    for bits, piece in zip((1, 2, 3), others):
        whole = place(whole, piece, me ^ bits)
    return whole.reshape(-1, mine.shape[-1])


def swap_z(value, bits):
    return lax.ppermute(value, "z", [(i, i ^ bits) for i in range(4)])


def by_side(value):
    return value.reshape(2, value.shape[0] // 2, value.shape[1])


class Line:
    def __init__(self):
        self.last = None

    def __call__(self, function, *args):
        if self.last is not None:
            args, _ = lax.optimization_barrier((args, self.last))
        out = function(*args)
        self.last = jax.tree.leaves(out)[0]
        return out


def row_per_chip_shards(
    tokens,
    segment_ids,
    w_qkv,
    b_qv,
    w_out,
    b_out,
    w_up,
    b_up,
    w_down,
    b_down,
    ln_gain,
    ln_bias,
    out_grad,
):
    side, here_y = lax.axis_index("core"), lax.axis_index("y")
    place = jnp.stack([here_y, lax.axis_index("z") & 1]).astype(jnp.int32)
    width, wide = b_qv.shape[1], tokens.shape[1]
    gains, shifts = ln_gain[:, None], ln_bias[:, None]
    line = Line()

    def pair(*parts):
        return line(lambda *all: jnp.concatenate(all), *parts)

    qkv_mine = cross(line(quarter_of, w_qkv.reshape(-1, width)))
    a1_own, sum_dz = line(first_norm, tokens, out_grad, gains[0], shifts[0])
    a1_came = core(a1_own)
    seg_other = core(segment_ids)
    small = cross(jnp.concatenate([b_qv.reshape(-1), b_up]))
    up_quarter = line(quarter_of, w_up)
    down_quarter = line(quarter_of, w_down)

    def ranges(mine, other):
        seg = jnp.concatenate([mine, other])
        start = jnp.sum((seg[None, :] < seg[:, None]).astype(jnp.int32), axis=1)[None]
        ordered = jnp.where(side == 0, seg, jnp.concatenate([other, mine]))
        blocks = ordered.reshape(LEN // BLK, BLK)
        low = jnp.sum((blocks[None, :, -1] < blocks[:, None, 0]).astype(jnp.int32), axis=1)
        return start, jnp.concatenate([(side * (LEN // BLK // 2))[None].astype(jnp.int32), low])

    start, info = line(ranges, segment_ids, seg_other)
    a1 = pair(a1_own, a1_came)
    own = tuple(line(project, a1, w_qkv, b_qv))
    qkv_mine, w_out_now, up_quarter, _ = lax.optimization_barrier((qkv_mine, w_out, up_quarter, own[0]))
    qkv_parts = share(qkv_mine)
    out_other = cross(w_out_now)
    up_mine = cross(up_quarter)
    own = own + tuple(line(partial(attn_fwd, info), *own, start))
    up_mine, down_quarter, _ = lax.optimization_barrier((up_mine, down_quarter, own[3]))
    up_parts = share(up_mine)
    down_mine = cross(down_quarter)
    qkv_other = line(assemble, qkv_mine, qkv_parts).reshape(w_qkv.shape)
    other = tuple(line(project, a1, qkv_other, small[: 2 * width].reshape(2, width)))
    other = other + tuple(line(partial(attn_fwd, info), *other, start))
    down_mine, dz_own, _ = lax.optimization_barrier((down_mine, out_grad, other[3]))
    down_parts = share(down_mine)
    dz_came = core(dz_own)

    here, there = line(partial(sum_dots, nn), [own[3], other[3]], [w_out, out_other])
    came = core(there)
    up_other = line(assemble, up_mine, up_parts)
    mixed, a2_own = line(second_norm, tokens, here, came, b_out[None], gains[1], shifts[1])
    a2_came = core(a2_own)
    dz = pair(dz_own, dz_came)
    a2 = pair(a2_own, a2_came)

    def core_halves(value):
        half = value.shape[0] // 2
        return core(value[:half]), core(value[half:])

    act_other, slope_other = line(up_gelu, a2, up_other, small[2 * width :])
    down_got = cross(line(across_frames, act_other, dz))
    act_own, slope_own = line(up_gelu, a2, w_up, b_up)
    down_own = line(across_frames, act_own, dz)
    du_own, sum_up_own = line(back_act, dz, w_down, slope_own)
    down_other = line(assemble, down_mine, down_parts)
    du_other, sum_up_other = line(back_act, dz, down_other, slope_other)
    here, there = line(partial(sum_dots, nt), [du_own, du_other], [w_up, up_other])
    came = core_halves(there)
    up_got = cross(line(across_frames, a2, du_other))
    grad_h, dattn_own, sums_h = line(norm_back, mixed, here, came, gains[1], out_grad)
    dattn_came = core_halves(dattn_own)
    up_own = line(across_frames, a2, du_own)

    def spread_y(own, got):
        return swap(line(side_sum, 1 - here_y, own, got), "y")

    def near_z(own, got, near):
        send, keep = line(quarter_sums, place, own, got, near)
        return keep, swap_z(send, 1)

    def far_z(keep, came):
        low = line(add_low, keep, came)
        return low, swap_z(low, 2)

    def back_z(low, came):
        mine = line(add_low, low, came)
        near = swap_z(mine, 1)
        return (mine, swap(mine, "y")), (near, swap(near, "y"))

    def wait_near(total):
        near, other = total[1]
        return total[0], (line(lambda value: value, near), other)

    def put(pair, prior=None, extra=0):
        fill = partial(settle, flip=0 if prior is None else 1, extra=extra)
        return line(lambda mine, other, prior: fill(place, mine, other, prior=prior), *pair, prior)

    down_own, down_got = by_side(down_own), by_side(down_got)
    down_near = spread_y(down_own, down_got)
    dattn = pair(dattn_own, *dattn_came)

    def back(entry, weight):
        query, keys, values, out, lse = entry
        cot = line(turn_back, dattn, weight)
        trio = line(partial(attn_bwd, info), query, keys, values, start, out, lse, cot)
        return (trio,) + tuple(line(frame_sums, a1, trio, out, dattn))

    trio_other, attn_other, sum_trio_other = back(other, out_other)
    first_got = cross(attn_other[0])
    down_sum = near_z(down_own, down_got, down_near)
    y_here, y_there = line(partial(sum_dots, nn), [act_own, act_other], [w_down, down_other])
    y_came = core(y_there)
    query, keys, values, out, lse = own
    cot = line(turn_back, dattn, w_out)
    down_sum = far_z(*down_sum)
    up_own, up_got = by_side(up_own), by_side(up_got)
    up_near = spread_y(up_own, up_got)
    trio_own = line(partial(attn_bwd, info), query, keys, values, start, out, lse, cot)
    attn_own, sum_trio_own = line(frame_sums, a1, trio_own, out, dattn)
    first_own, first_got = by_side(attn_own[0]), by_side(first_got)
    down_sum = back_z(*down_sum)
    block_out = line(finish, mixed, y_here, y_came, b_down[None])
    first_near = spread_y(first_own, first_got)
    here, there = line(partial(sum_dots, nt), [trio_own, trio_other], [w_qkv, qkv_other])
    came = core_halves(there)
    up_sum = near_z(up_own, up_got, up_near)
    down_sum = wait_near(down_sum)
    grad_in, _, sums_x = line(norm_back, tokens, here, came, gains[0], grad_h)
    common = line(common_rows, sums_h, sum_dz, sums_x)
    common_came = core(common)

    first_sum = near_z(first_own, first_got, first_near)
    up_sum = far_z(*up_sum)
    second_other = line(ride, attn_other[1], sum_trio_other, sum_up_other, common, common_came)
    second_got = cross(second_other)
    second_own = line(ride, attn_own[1], sum_trio_own, sum_up_own, common, common_came)
    first_sum = far_z(*first_sum)
    grad_down = put(down_sum[0])
    grad_down = put(down_sum[1], grad_down)
    up_sum = back_z(*up_sum)
    second_own, second_got = by_side(second_own), by_side(second_got)
    second_near = spread_y(second_own, second_got)
    first_sum = back_z(*first_sum)
    second_sum = near_z(second_own, second_got, second_near)
    up_sum = wait_near(up_sum)
    grad_up = put(up_sum[0])
    first_sum = wait_near(first_sum)
    second_sum = far_z(*second_sum)
    first = put(first_sum[0], extra=wide)
    grad_up = put(up_sum[1], grad_up)
    first = put(first_sum[1], first, extra=wide)
    second_sum = back_z(*second_sum)
    second = put(second_sum[0])
    second = put(second_sum[1], second)
    grad_qkv = lax.dynamic_update_slice(first, second[:wide], (2 * wide, 0)).reshape(w_qkv.shape)
    grad_wout = jnp.swapaxes(second[wide : 2 * wide].reshape(-1, w_out.shape[0], width), 0, 1)
    grad_wout = grad_wout.reshape(w_out.shape)
    vector = second[2 * wide :].reshape(-1)
    units = b_up.shape[0]
    ends = [2 * width, units, wide, wide, 2 * wide, 2 * wide]
    cuts = [sum(ends[:i]) for i in range(len(ends) + 1)]
    grad_bqv, grad_bup, grad_bout, grad_bdown, grad_gain, grad_shift = [
        vector[low:high] for low, high in zip(cuts[:-1], cuts[1:])
    ]
    return (
        block_out,
        grad_in,
        grad_qkv,
        grad_bqv.reshape(b_qv.shape),
        grad_wout,
        grad_bout,
        grad_up,
        grad_bup,
        grad_down,
        grad_bdown,
        grad_gain.reshape(ln_gain.shape),
        grad_shift.reshape(ln_bias.shape),
    )


def solution(mesh):
    rows, frames = ("dp", "mp"), "mp"
    body = tensor_parallel_shards
    if row_per_chip(mesh):
        shape = (mesh.shape["dp"] // 2, 2, mesh.shape["mp"] // 2, 2)
        mesh = Mesh(mesh.devices.reshape(shape), ("z", "y", "x", "core"))
        rows, frames = ("z", "y", "x", "core"), ("x", "core")
        body = row_per_chip_shards
    in_specs = (
        P(rows, None),
        P(rows),
        P(None, None, frames),
        P(None, frames),
        P(frames, None),
        P(),
        P(None, frames),
        P(frames),
        P(frames, None),
        P(),
        P(),
        P(),
        P(rows, None),
    )
    out_specs = (
        P(rows, None),
        P(rows, None),
        P(None, None, frames),
        P(None, frames),
        P(frames, None),
        P(),
        P(None, frames),
        P(frames),
        P(frames, None),
        P(),
        P(),
        P(),
    )
    return jax.shard_map(body, mesh=mesh, in_specs=in_specs, out_specs=out_specs, check_vma=False)
```

```python
from functools import partial

import jax
import jax.numpy as jnp
from jax import lax
from jax.experimental import pallas as pl
from jax.experimental.pallas import tpu as pltpu
from jax.sharding import Mesh
from jax.sharding import PartitionSpec as P

HD = 64
LEN = 1024
QBLK = 512
EPS = 1e-05
BLK = 256

NEG = -1e30
GRANT = 10 << 20
EXTRA = 128
BRIEF = pl.CostEstimate(flops=1, bytes_accessed=1, transcendentals=0)
f32 = jnp.float32
bf16 = jnp.bfloat16


def nt(left, right):
    return lax.dot_general(left, right, (((1,), (1,)), ((), ())), preferred_element_type=f32)


def nn(left, right):
    return lax.dot_general(left, right, (((1,), (0,)), ((), ())), preferred_element_type=f32)


def tn(left, right):
    return lax.dot_general(left, right, (((0,), (0,)), ((), ())), preferred_element_type=f32)


def attn_bias(block, j, first):
    q_pos = block * BLK + lax.broadcasted_iota(jnp.int32, (1, BLK), 1)
    k_pos = j * BLK + lax.broadcasted_iota(jnp.int32, (BLK, BLK), 0)
    return jnp.where((k_pos >= first) & (k_pos <= q_pos), 0.0, NEG)


def head_rows(refs, scratch, heads):
    lane = lax.broadcasted_iota(jnp.int32, (LEN, 2 * HD), 1)
    for ref, out in zip(refs, scratch):
        for h in range(heads):
            pair = ref[:, (h // 2) * 2 * HD : (h // 2 + 1) * 2 * HD]
            out[h] = jnp.where((lane < HD) == (h % 2 == 0), pair, jnp.zeros_like(pair))


def attn_fwd_body(info, q_ref, k_ref, v_ref, st_ref, o_ref, lse_ref, k_heads, v_turned):
    block = pl.program_id(0)
    heads = q_ref.shape[1] // HD
    first = st_ref[...]

    @pl.when(block == 0)
    def _():
        head_rows([k_ref], [k_heads], heads)
        for pair in range(heads // 2):
            turned = v_ref[:, pair * 2 * HD : (pair + 1) * 2 * HD].T
            for h in (0, 1):
                v_turned[2 * pair + h, :HD] = turned[h * HD : (h + 1) * HD]
                v_turned[2 * pair + h, HD:] = jnp.ones((16, LEN), bf16)

    def step(at, carry):
        j = block - at
        row = pl.multiple_of((j ^ info[0]) * BLK, BLK)
        bias = attn_bias(block, j, first)
        out = []
        for h in range(heads):
            top, acc = carry[h]
            query = q_ref[:, (h // 2) * 2 * HD : (h // 2 + 1) * 2 * HD]
            s = nt(k_heads[h, pl.ds(row, BLK), :], query) + bias
            new = jnp.maximum(top, jnp.max(s, axis=0, keepdims=True))
            p = jnp.exp(s - new).astype(bf16)
            acc = acc * jnp.exp(top - new) + nn(v_turned[h, :, pl.ds(row, BLK)], p)
            out.append((new, acc))
        return tuple(out)

    init = tuple((jnp.full((1, BLK), NEG, f32), jnp.zeros((HD + 16, BLK), f32)) for _ in range(heads))
    done = lax.fori_loop(0, block + 1 - info[1 + block], step, init)
    for pair in range(heads // 2):
        both = [acc[:HD] / acc[HD : HD + 1] for _, acc in done[2 * pair : 2 * pair + 2]]
        o_ref[:, pair * 2 * HD : (pair + 1) * 2 * HD] = jnp.concatenate(both, axis=0).T.astype(bf16)
    for h in range(heads):
        top, acc = done[h]
        lse_ref[h : h + 1, :] = top + jnp.log(acc[HD : HD + 1])


def attn_bwd_body(base, info, q_ref, k_ref, v_ref, st_ref, o_ref, lse_ref, do_ref, d_ref, k_heads, v_heads, dk_acc, dv_acc):
    block = pl.program_id(0)
    heads = q_ref.shape[1] // HD
    first = st_ref[...]
    lane = lax.broadcasted_iota(jnp.int32, (BLK, 2 * HD), 1)

    @pl.when(block == 0)
    def _():
        head_rows([k_ref, v_ref], [k_heads, v_heads], heads)
        dk_acc[...] = jnp.zeros_like(dk_acc)
        dv_acc[...] = jnp.zeros_like(dv_acc)

    deltas = []
    for pair in range(heads // 2):
        cols = slice(pair * 2 * HD, (pair + 1) * 2 * HD)
        turned = (do_ref[:, cols].astype(f32) * o_ref[:, cols].astype(f32)).T
        for h in (0, 1):
            deltas.append(jnp.sum(turned[h * HD : (h + 1) * HD], axis=0, keepdims=True))

    def step(j, dqs):
        row = pl.multiple_of((j ^ info[0]) * BLK, BLK)
        bias = attn_bias(block, j, first)
        out = list(dqs)
        for pair in range(heads // 2):
            cols = slice(pair * 2 * HD, (pair + 1) * 2 * HD)
            query, cot = q_ref[:, cols], do_ref[:, cols]
            dk = dk_acc[pl.ds(row, BLK), cols]
            dv = dv_acc[pl.ds(row, BLK), cols]
            for h in (2 * pair, 2 * pair + 1):
                mask = (lane < HD) == (h % 2 == 0)
                keys = k_heads[h, pl.ds(row, BLK), :]
                p = jnp.exp(nt(keys, query) + (bias - lse_ref[base + h : base + h + 1, :]))
                dp = nt(v_heads[h, pl.ds(row, BLK), :], cot)
                ds = (p * (dp - deltas[h])).astype(bf16)
                dv = dv + nn(p.astype(bf16), jnp.where(mask, cot, jnp.zeros_like(cot)))
                dk = dk + nn(ds, jnp.where(mask, query, jnp.zeros_like(query)))
                out[pair] = out[pair] + tn(ds, keys)
            dk_acc[pl.ds(row, BLK), cols] = dk
            dv_acc[pl.ds(row, BLK), cols] = dv
        return tuple(out)

    init = tuple(jnp.zeros((BLK, 2 * HD), f32) for _ in range(heads // 2))
    dqs = lax.fori_loop(info[1 + block], block + 1, step, init)
    here = pl.multiple_of((block ^ info[0]) * BLK, BLK)
    for pair in range(heads // 2):
        cols = slice(pair * 2 * HD, (pair + 1) * 2 * HD)
        d_ref[0, pl.ds(here, BLK), cols] = (dqs[pair] * HD**-0.5).astype(bf16)

    @pl.when(block == pl.num_programs(0) - 1)
    def _():
        d_ref[1] = dk_acc[...].astype(bf16)
        d_ref[2] = dv_acc[...].astype(bf16)


def attn_specs(width):
    small = pl.BlockSpec((BLK, width), lambda i, info: (i ^ info[0], 0))
    whole = pl.BlockSpec((LEN, width), lambda i, info: (0, 0))
    start = pl.BlockSpec((1, BLK), lambda i, info: (0, i ^ info[0]))
    lse = pl.BlockSpec((width // HD, BLK), lambda i, info: (0, i ^ info[0]))
    return small, whole, start, lse


def attn_fwd(info, query, keys, values, start):
    width = query.shape[1]
    heads = width // HD
    small, whole, first, lse = attn_specs(width)
    return pl.pallas_call(
        attn_fwd_body,
        out_shape=(jax.ShapeDtypeStruct(query.shape, bf16), jax.ShapeDtypeStruct((heads, LEN), f32)),
        grid_spec=pltpu.PrefetchScalarGridSpec(
            num_scalar_prefetch=1,
            grid=(LEN // BLK,),
            in_specs=[small, whole, whole, first],
            out_specs=[small, lse],
            scratch_shapes=[pltpu.VMEM((heads, LEN, 2 * HD), bf16), pltpu.VMEM((heads, HD + 16, LEN), bf16)],
        ),
        cost_estimate=BRIEF,
        compiler_params=pltpu.CompilerParams(vmem_limit_bytes=GRANT),
        name="attn_fwd",
    )(info, query, keys, values, start)


def attn_bwd(info, query, keys, values, start, out, lse, cot, part=0, parts=1, prior=None):
    width = query.shape[1] // parts
    heads = width // HD
    small = pl.BlockSpec((BLK, width), lambda i, info: (i ^ info[0], part))
    whole = pl.BlockSpec((LEN, width), lambda i, info: (0, part))
    first = pl.BlockSpec((1, BLK), lambda i, info: (0, i ^ info[0]))
    lse_spec = pl.BlockSpec((heads * parts, BLK), lambda i, info: (0, i ^ info[0]))
    more = () if prior is None else (prior,)

    def body(*refs):
        attn_bwd_body(part * heads, *refs[:8], *refs[8 + len(more) :])

    return pl.pallas_call(
        body,
        out_shape=jax.ShapeDtypeStruct((3,) + query.shape, bf16),
        grid_spec=pltpu.PrefetchScalarGridSpec(
            num_scalar_prefetch=1,
            grid=(LEN // BLK,),
            in_specs=[small, whole, whole, first, small, lse_spec, small]
            + [pl.BlockSpec(memory_space=pl.ANY)] * len(more),
            out_specs=pl.BlockSpec((3, LEN, width), lambda i, info: (0, 0, part)),
            scratch_shapes=[
                pltpu.VMEM((heads, LEN, 2 * HD), bf16),
                pltpu.VMEM((heads, LEN, 2 * HD), bf16),
                pltpu.VMEM((LEN, width), f32),
                pltpu.VMEM((LEN, width), f32),
            ],
        ),
        input_output_aliases={8: 0} if more else {},
        cost_estimate=BRIEF,
        compiler_params=pltpu.CompilerParams(vmem_limit_bytes=GRANT),
        name="attn_bwd",
    )(info, query, keys, values, start, out, lse, cot, *more)


def up_body(a_ref, w_ref, b_ref, g_ref, s_ref):
    rows = a_ref[...]
    for part in range(w_ref.shape[1] // 256):
        cols = slice(part * 256, part * 256 + 256)
        u = nn(rows, w_ref[:, cols]) + b_ref[:, cols].astype(f32)
        size = jnp.abs(u)
        t = 1.0 / (1.0 + 0.3275911 * 0.7071067811865476 * size)
        poly = t * (0.5 * 0.254829592 + t * (0.5 * -0.284496736 + t * (0.5 * 1.421413741 + t * (0.5 * -1.453152027 + t * (0.5 * 1.061405429)))))
        bell = jnp.exp(-0.5 * u * u)
        tail = poly * bell
        cdf = jnp.where(u >= 0, 1.0 - tail, tail)
        g_ref[:, cols] = (u * cdf).astype(bf16)
        s_ref[:, cols] = (cdf + u * bell * 0.3989422804014327).astype(bf16)


def up_gelu(rows, weight, bias):
    m, k = rows.shape
    n = weight.shape[1]
    bm = 256
    shape = jax.ShapeDtypeStruct((m, n), bf16)
    tile = pl.BlockSpec((bm, n), lambda i: (i, 0))
    return pl.pallas_call(
        up_body,
        out_shape=(shape, shape),
        grid=(m // bm,),
        in_specs=[pl.BlockSpec((bm, k), lambda i: (i, 0)), pl.BlockSpec((k, n), lambda i: (0, 0)), pl.BlockSpec((1, n), lambda i: (0, 0))],
        out_specs=(tile, tile),
        cost_estimate=BRIEF,
        compiler_params=pltpu.CompilerParams(vmem_limit_bytes=GRANT),
        name="up_gelu",
    )(rows, weight, bias.reshape(1, n))


def const_spec(shape):
    return pl.BlockSpec(shape, lambda i: (0,) * len(shape))


def row_spec(rows, cols):
    return pl.BlockSpec((rows, cols), lambda i: (i, 0))


def project_body(a_ref, w_ref, b_ref, q_ref, k_ref, v_ref):
    rows = a_ref[...]
    q_ref[...] = (nn(rows, w_ref[0]) + b_ref[0:1].astype(f32)).astype(bf16) * jnp.bfloat16(HD**-0.5)
    k_ref[...] = nn(rows, w_ref[1]).astype(bf16)
    v_ref[...] = (nn(rows, w_ref[2]) + b_ref[1:2].astype(f32)).astype(bf16)


def project(rows, weight, bias):
    m, k = rows.shape
    n = weight.shape[2]
    tile = 256
    shape = jax.ShapeDtypeStruct((m, n), bf16)
    return pl.pallas_call(
        project_body,
        out_shape=(shape, shape, shape),
        grid=(m // tile,),
        in_specs=[row_spec(tile, k), const_spec(weight.shape), const_spec(bias.shape)],
        out_specs=[row_spec(tile, n)] * 3,
        cost_estimate=BRIEF,
        compiler_params=pltpu.CompilerParams(vmem_limit_bytes=GRANT),
        name="project",
    )(rows, weight, bias)


def sum_dots(product, lefts, rights):
    stacked = lefts[0].ndim == 3
    m, k = lefts[0].shape[-2:]
    n = rights[0].shape[-1] if product is nn else rights[0].shape[-2]
    terms = len(lefts)
    tile = 256
    steps = m // tile // 2

    def body(*refs):
        total = None
        for left, right in zip(refs[:terms], refs[terms : 2 * terms]):
            for at in range(left.shape[0] if stacked else 1):
                term = product(left[at], right[at]) if stacked else product(left[...], right[...])
                total = term if total is None else total + term
        here, there = refs[2 * terms :]

        @pl.when(pl.program_id(0) < steps)
        def _():
            there[...] = total.astype(bf16)

        @pl.when(pl.program_id(0) >= steps)
        def _():
            here[...] = total

    def turn(i):
        return jnp.where(i < steps, i + steps, i - steps)

    if stacked:
        left_spec = pl.BlockSpec((lefts[0].shape[0], tile, k), lambda i: (0, turn(i), 0))
    else:
        left_spec = pl.BlockSpec((tile, k), lambda i: (turn(i), 0))
    return pl.pallas_call(
        body,
        out_shape=(jax.ShapeDtypeStruct((m // 2, n), f32), jax.ShapeDtypeStruct((m // 2, n), bf16)),
        grid=(2 * steps,),
        in_specs=[left_spec] * terms + [const_spec(r.shape) for r in rights],
        out_specs=[
            pl.BlockSpec((tile, n), lambda i: (jnp.maximum(i - steps, 0), 0)),
            pl.BlockSpec((tile, n), lambda i: (jnp.minimum(i, steps - 1), 0)),
        ],
        cost_estimate=BRIEF,
        compiler_params=pltpu.CompilerParams(vmem_limit_bytes=GRANT),
        name="sum_dots",
    )(*lefts, *rights)


def center_rows(rows):
    center = rows - jnp.mean(rows, axis=-1, keepdims=True)
    scale = lax.rsqrt(jnp.mean(center * center, axis=-1, keepdims=True) + EPS)
    return center * scale, scale


def first_norm_body(x_ref, g_ref, gain_ref, shift_ref, a_ref, sum_ref):
    normal, _ = center_rows(x_ref[...].astype(f32))
    a_ref[...] = (normal * gain_ref[...] + shift_ref[...]).astype(bf16)

    @pl.when(pl.program_id(0) == 0)
    def _():
        sum_ref[...] = jnp.zeros_like(sum_ref)

    sum_ref[...] += jnp.sum(g_ref[...].astype(f32), axis=0, keepdims=True)


def first_norm(tokens, cotangent, gain, shift):
    m, d = tokens.shape
    tile = 128
    return pl.pallas_call(
        first_norm_body,
        out_shape=(jax.ShapeDtypeStruct((m, d), bf16), jax.ShapeDtypeStruct((1, d), f32)),
        grid=(m // tile,),
        in_specs=[row_spec(tile, d), row_spec(tile, d), const_spec((1, d)), const_spec((1, d))],
        out_specs=[row_spec(tile, d), const_spec((1, d))],
        cost_estimate=BRIEF,
        compiler_params=pltpu.CompilerParams(vmem_limit_bytes=GRANT),
        name="first_norm",
    )(tokens, cotangent, gain, shift)


def second_norm_body(x_ref, here_ref, came_ref, b_ref, gain_ref, shift_ref, h_ref, a_ref):
    mixed = x_ref[...].astype(f32) + (here_ref[...] + came_ref[...].astype(f32)) + b_ref[...].astype(f32)
    h_ref[...] = mixed
    normal, _ = center_rows(mixed)
    a_ref[...] = (normal * gain_ref[...] + shift_ref[...]).astype(bf16)


def second_norm(tokens, here, came, bias, gain, shift):
    m, d = tokens.shape
    tile = 128
    return pl.pallas_call(
        second_norm_body,
        out_shape=(jax.ShapeDtypeStruct((m, d), f32), jax.ShapeDtypeStruct((m, d), bf16)),
        grid=(m // tile,),
        in_specs=[row_spec(tile, d)] * 3 + [const_spec((1, d))] * 3,
        out_specs=[row_spec(tile, d)] * 2,
        cost_estimate=BRIEF,
        compiler_params=pltpu.CompilerParams(vmem_limit_bytes=GRANT),
        name="second_norm",
    )(tokens, here, came, bias, gain, shift)


def norm_back_body(v_ref, here_ref, low_came_ref, high_came_ref, gain_ref, res_ref, out_ref, low_ref, sums_ref):
    normal, scale = center_rows(v_ref[...].astype(f32))
    first = pl.program_id(0) < pl.num_programs(0) // 2
    came = jnp.where(first, low_came_ref[...], high_came_ref[...])
    grad = here_ref[...] + came.astype(f32)
    scaled = grad * gain_ref[...]
    inner = jnp.mean(scaled * normal, axis=-1, keepdims=True)
    back = scale * (scaled - jnp.mean(scaled, axis=-1, keepdims=True) - normal * inner)
    back = back + res_ref[...].astype(f32)
    low = back.astype(bf16)
    out_ref[...] = back
    low_ref[...] = low

    @pl.when(pl.program_id(0) == 0)
    def _():
        sums_ref[...] = jnp.zeros_like(sums_ref)

    sums_ref[0:1] += jnp.sum(grad * normal, axis=0, keepdims=True)
    sums_ref[1:2] += jnp.sum(grad, axis=0, keepdims=True)
    sums_ref[2:3] += jnp.sum(low.astype(f32), axis=0, keepdims=True)


def norm_back(values, here, came, gain, residual):
    m, d = values.shape
    tile = 128
    half = m // tile // 2
    low = pl.BlockSpec((tile, d), lambda i: (jnp.minimum(i, half - 1), 0))
    high = pl.BlockSpec((tile, d), lambda i: (jnp.maximum(i - half, 0), 0))
    return pl.pallas_call(
        norm_back_body,
        out_shape=(
            jax.ShapeDtypeStruct((m, d), f32),
            jax.ShapeDtypeStruct((m, d), bf16),
            jax.ShapeDtypeStruct((8, d), f32),
        ),
        grid=(m // tile,),
        in_specs=[row_spec(tile, d)] * 2 + [low, high, const_spec((1, d)), row_spec(tile, d)],
        out_specs=[row_spec(tile, d)] * 2 + [const_spec((8, d))],
        cost_estimate=BRIEF,
        compiler_params=pltpu.CompilerParams(vmem_limit_bytes=GRANT),
        name="norm_back",
    )(values, here, *came, gain, residual)


def back_act_body(z_ref, w_ref, s_ref, du_ref, sum_ref):
    du = (nt(z_ref[...], w_ref[...]) * s_ref[...].astype(f32)).astype(bf16)
    du_ref[...] = du

    @pl.when(pl.program_id(0) == 0)
    def _():
        sum_ref[...] = jnp.zeros_like(sum_ref)

    sum_ref[...] += jnp.sum(du.astype(f32), axis=0, keepdims=True)


def back_act(cotangent, weight, slope):
    m, d = cotangent.shape
    n = weight.shape[0]
    tile = 256
    return pl.pallas_call(
        back_act_body,
        out_shape=(jax.ShapeDtypeStruct((m, n), bf16), jax.ShapeDtypeStruct((1, n), f32)),
        grid=(m // tile,),
        in_specs=[row_spec(tile, d), const_spec((n, d)), row_spec(tile, n)],
        out_specs=[row_spec(tile, n), const_spec((1, n))],
        cost_estimate=BRIEF,
        compiler_params=pltpu.CompilerParams(vmem_limit_bytes=GRANT),
        name="back_act",
    )(cotangent, weight, slope)


def frame_sums_body(a_ref, d_ref, o_ref, g_ref, one_ref, two_ref, sums_ref, a_turned):
    rows, width = g_ref.shape[1], o_ref.shape[1]
    count = rows // width
    a_turned[...] = a_ref[...].T
    for at in range(4 * count):
        kind, part = divmod(at, count)
        out = one_ref if at < 2 * count else two_ref
        if kind < 3:
            block = nn(a_turned[part * width : (part + 1) * width, :], d_ref[kind])
        else:
            block = tn(o_ref[...], g_ref[:, part * width : (part + 1) * width])
        low = (at % (2 * count)) * width
        out[low : low + width, :] = block.astype(bf16)
    two_ref[2 * rows :, :] = jnp.zeros((EXTRA, width), bf16)
    for kind in range(3):
        sums_ref[kind] = jnp.sum(d_ref[kind].astype(f32), axis=0, keepdims=True)


def frame_sums(rows, trio, out, cotangent):
    t, d = rows.shape
    n = trio.shape[2]
    half = jax.ShapeDtypeStruct((2 * d, n), bf16)
    one, two, sums = pl.pallas_call(
        frame_sums_body,
        out_shape=(half, jax.ShapeDtypeStruct((2 * d + EXTRA, n), bf16), jax.ShapeDtypeStruct((3, 1, n), f32)),
        grid=(1,),
        in_specs=[const_spec((t, d)), const_spec((3, t, n)), const_spec((t, n)), const_spec((t, d))],
        out_specs=[const_spec((2 * d, n)), const_spec((2 * d + EXTRA, n)), const_spec((3, 1, n))],
        scratch_shapes=[pltpu.VMEM((d, t), bf16)],
        cost_estimate=BRIEF,
        compiler_params=pltpu.CompilerParams(vmem_limit_bytes=GRANT),
        name="frame_sums",
    )(rows, trio, out, cotangent)
    return (one, two), sums


def frames_body(a_ref, g_ref, out_ref, turned):
    tile = out_ref.shape[0]
    turned[...] = a_ref[...].T
    out_ref[...] = nn(turned[...], g_ref[...]).astype(bf16)


def across_frames(left, right):
    t, m = left.shape
    n = right.shape[1]
    tile = 256
    return pl.pallas_call(
        frames_body,
        out_shape=jax.ShapeDtypeStruct((m, n), bf16),
        grid=(m // tile,),
        in_specs=[pl.BlockSpec((t, tile), lambda i: (0, i)), const_spec((t, n))],
        out_specs=row_spec(tile, n),
        scratch_shapes=[pltpu.VMEM((tile, t), bf16)],
        cost_estimate=BRIEF,
        compiler_params=pltpu.CompilerParams(vmem_limit_bytes=GRANT),
        name="across_frames",
    )(left, right)


def turn_back_body(a_ref, w_ref, out_ref):
    out_ref[...] = nt(a_ref[...], w_ref[...]).astype(bf16)


def turn_back(rows, weight):
    m, k = rows.shape
    n = weight.shape[0]
    tile = 256
    return pl.pallas_call(
        turn_back_body,
        out_shape=jax.ShapeDtypeStruct((m, n), bf16),
        grid=(m // tile,),
        in_specs=[row_spec(tile, k), const_spec((n, k))],
        out_specs=row_spec(tile, n),
        cost_estimate=BRIEF,
        compiler_params=pltpu.CompilerParams(vmem_limit_bytes=GRANT),
        name="turn_back",
    )(rows, weight)


def side_sum_body(info, *refs):
    total = refs[0][0].astype(f32)
    for ref in refs[1:-1]:
        total = total + (ref[0] if len(ref.shape) == 3 else ref[...]).astype(f32)
    refs[-1][...] = total.astype(bf16)


def side_sum(side, own, got, near=None):
    _, rows, cols = own.shape
    tile = rows // 4
    pick_spec = pl.BlockSpec((1, tile, cols), lambda i, info: (info[0], i, 0))
    flat = pl.BlockSpec((tile, cols), lambda i, info: (i, 0))
    args = [own, got] + ([] if near is None else [near])
    return pl.pallas_call(
        side_sum_body,
        out_shape=jax.ShapeDtypeStruct((rows, cols), bf16),
        grid_spec=pltpu.PrefetchScalarGridSpec(
            num_scalar_prefetch=1,
            grid=(4,),
            in_specs=[pick_spec, pick_spec] + [flat] * (len(args) - 2),
            out_specs=flat,
        ),
        cost_estimate=BRIEF,
        compiler_params=pltpu.CompilerParams(vmem_limit_bytes=GRANT),
        name="side_sum",
    )(side[None], *args)


def add_low_body(a_ref, b_ref, out_ref):
    out_ref[...] = (a_ref[...].astype(f32) + b_ref[...].astype(f32)).astype(bf16)


def add_low(left, right):
    rows, cols = left.shape
    tile = rows // 2
    return pl.pallas_call(
        add_low_body,
        out_shape=jax.ShapeDtypeStruct((rows, cols), bf16),
        grid=(2,),
        in_specs=[row_spec(tile, cols)] * 2,
        out_specs=row_spec(tile, cols),
        cost_estimate=BRIEF,
        compiler_params=pltpu.CompilerParams(vmem_limit_bytes=GRANT),
        name="add_low",
    )(left, right)


def quarter_sums_body(info, own_ref, got_ref, near_ref, send_ref, keep_ref):
    total = own_ref[0, 0].astype(f32) + got_ref[0, 0].astype(f32) + near_ref[0].astype(f32)

    @pl.when(pl.program_id(0) == 0)
    def _():
        send_ref[...] = total.astype(bf16)

    @pl.when(pl.program_id(0) == 1)
    def _():
        keep_ref[...] = total.astype(bf16)


def quarter_sums(place, own, got, near):
    _, rows, cols = own.shape
    rows = rows // 2
    tile = rows // 2
    deep = pl.BlockSpec((1, 1, tile, cols), lambda f, i, info: (info[0], info[1] ^ 1 ^ f, i, 0))
    flat = pl.BlockSpec((1, tile, cols), lambda f, i, info: (info[1] ^ 1 ^ f, i, 0))
    shape = jax.ShapeDtypeStruct((rows, cols), bf16)
    return pl.pallas_call(
        quarter_sums_body,
        out_shape=(shape, shape),
        grid_spec=pltpu.PrefetchScalarGridSpec(
            num_scalar_prefetch=1,
            grid=(2, 2),
            in_specs=[deep, deep, flat],
            out_specs=[
                pl.BlockSpec((tile, cols), lambda f, i, info: (jnp.where(f == 0, i, 1), 0)),
                pl.BlockSpec((tile, cols), lambda f, i, info: (jnp.where(f == 0, 0, i), 0)),
            ],
        ),
        cost_estimate=BRIEF,
        compiler_params=pltpu.CompilerParams(vmem_limit_bytes=GRANT),
        name="quarter_sums",
    )(place, own.reshape(2, 2, rows, cols), got.reshape(2, 2, rows, cols), near.reshape(2, rows, cols))


def settle_body(info, mine_ref, other_ref, *rest):
    for at, ref in enumerate((mine_ref, other_ref)):

        @pl.when(pl.program_id(0) == at)
        def _(ref=ref):
            rest[-1][0] = ref[...].astype(f32)


def settle(place, mine, other, flip=0, prior=None, extra=0):
    rows, cols = mine.shape
    tile = rows // 2
    first = pl.BlockSpec((tile, cols), lambda f, i, info: (jnp.where(f == 0, i, 1), 0))
    second = pl.BlockSpec((tile, cols), lambda f, i, info: (jnp.where(f == 0, 0, i), 0))
    more = () if prior is None else (prior.reshape(-1, rows, cols),)
    out = pl.pallas_call(
        settle_body,
        out_shape=jax.ShapeDtypeStruct((4 + extra // rows, rows, cols), f32),
        grid_spec=pltpu.PrefetchScalarGridSpec(
            num_scalar_prefetch=1,
            grid=(2, 2),
            in_specs=[first, second] + [pl.BlockSpec(memory_space=pl.ANY)] * len(more),
            out_specs=pl.BlockSpec(
                (1, tile, cols), lambda f, i, info: (2 * (info[0] ^ f) + (info[1] ^ flip), i, 0)
            ),
        ),
        input_output_aliases={3: 0} if more else {},
        cost_estimate=BRIEF,
        compiler_params=pltpu.CompilerParams(vmem_limit_bytes=GRANT),
        name="settle",
    )(place, mine, other, *more)
    return out.reshape(-1, cols)


def finish_body(h_ref, here_ref, came_ref, b_ref, out_ref):
    out_ref[...] = (h_ref[...] + here_ref[...] + came_ref[...].astype(f32) + b_ref[...].astype(f32)).astype(bf16)


def finish(mixed, here, came, bias):
    m, d = mixed.shape
    tile = 128
    return pl.pallas_call(
        finish_body,
        out_shape=jax.ShapeDtypeStruct((m, d), bf16),
        grid=(m // tile,),
        in_specs=[row_spec(tile, d)] * 3 + [const_spec((1, d))],
        out_specs=row_spec(tile, d),
        cost_estimate=BRIEF,
        compiler_params=pltpu.CompilerParams(vmem_limit_bytes=GRANT),
        name="finish",
    )(mixed, here, came, bias)


def common_body(h_ref, z_ref, x_ref, out_ref):
    out_ref[...] = jnp.zeros_like(out_ref)
    rows = [h_ref[2:3], z_ref[0:1], x_ref[0:1], h_ref[0:1], x_ref[1:2], h_ref[1:2]]
    for at, row in enumerate(rows):
        out_ref[at : at + 1] = row


def common_rows(sums_h, sum_dz, sums_x):
    return pl.pallas_call(
        common_body,
        out_shape=jax.ShapeDtypeStruct(sums_h.shape, f32),
        cost_estimate=BRIEF,
        compiler_params=pltpu.CompilerParams(vmem_limit_bytes=GRANT),
        name="common_rows",
    )(sums_h, sum_dz, sums_x)


def lines_body(trio_ref, up_ref, mine_ref, came_ref, out_ref):
    cols = out_ref.shape[1]
    out_ref[...] = jnp.zeros_like(out_ref)
    out_ref[0:1] = trio_ref[0]
    out_ref[1:2] = trio_ref[2]
    at = 2
    for part in range(up_ref.shape[1] // cols):
        out_ref[at : at + 1] = up_ref[:, part * cols : (part + 1) * cols]
        at += 1
    both = mine_ref[...] + came_ref[...]
    for row in range(6):
        for part in range(both.shape[1] // cols):
            out_ref[at : at + 1] = both[row : row + 1, part * cols : (part + 1) * cols]
            at += 1


def lines_of(trio, up, mine, came):
    return pl.pallas_call(
        lines_body,
        out_shape=jax.ShapeDtypeStruct((EXTRA // 4, trio.shape[2]), f32),
        cost_estimate=BRIEF,
        compiler_params=pltpu.CompilerParams(vmem_limit_bytes=GRANT),
        name="lines_of",
    )(trio, up, mine, came)


def ride_body(mine_ref, came_ref, whole_ref, out_ref, lines):
    lines[...] = jnp.zeros_like(lines)
    lines[: mine_ref.shape[0]] = mine_ref[...] + came_ref[...]
    out_ref[...] = lines[...].astype(bf16)


def ride(whole, mine, came):
    rows, cols = whole.shape
    return pl.pallas_call(
        ride_body,
        out_shape=jax.ShapeDtypeStruct((rows, cols), bf16),
        grid=(1,),
        in_specs=[const_spec(mine.shape), const_spec(came.shape), pl.BlockSpec(memory_space=pl.ANY)],
        out_specs=pl.BlockSpec((EXTRA, cols), lambda i: (rows // EXTRA - 1, 0)),
        scratch_shapes=[pltpu.VMEM((EXTRA, cols), f32)],
        input_output_aliases={2: 0},
        cost_estimate=BRIEF,
        compiler_params=pltpu.CompilerParams(vmem_limit_bytes=GRANT),
        name="ride",
    )(mine, came, whole)


def norm_rows(values, gain, shift):
    center = values - jnp.mean(values, axis=-1, keepdims=True)
    spread = jnp.mean(center * center, axis=-1, keepdims=True)
    return center * lax.rsqrt(spread + EPS) * gain + shift


def split_heads(flat, rows):
    return flat.reshape(rows, LEN, flat.shape[1] // HD, HD)


def block_scores(query, keys, seg_q, seg_k, offset):
    scores = jnp.einsum(
        "rqhd,rkhd->rhqk", query, keys, preferred_element_type=jnp.float32
    ) * HD ** (-0.5)
    q_pos = offset + jnp.arange(query.shape[1], dtype=jnp.int32)
    k_pos = jnp.arange(keys.shape[1], dtype=jnp.int32)
    allowed = (seg_q[:, :, None] == seg_k[:, None, :]) & (
        k_pos[None, None, :] <= q_pos[None, :, None]
    )
    return jnp.where(allowed[:, None], scores, -1e30)


def attention_forward(query, keys, values, seg_all):
    rows = query.shape[0] // LEN
    q4 = split_heads(query, rows)
    k4 = split_heads(keys, rows)
    v4 = split_heads(values, rows)
    seg2 = seg_all.reshape(rows, LEN)
    outputs = []
    totals = []
    for block in range(LEN // QBLK):
        first = block * QBLK
        end = first + QBLK
        scores = block_scores(
            q4[:, first:end], k4[:, :end], seg2[:, first:end], seg2[:, :end], first
        )
        top = jnp.max(scores, axis=-1, keepdims=True)
        expd = jnp.exp(scores - top)
        summed = jnp.sum(expd, axis=-1, keepdims=True)
        weights = (expd / summed).astype(jnp.bfloat16)
        outputs.append(
            jnp.einsum("rhqk,rkhd->rqhd", weights, v4[:, :end], preferred_element_type=jnp.float32)
        )
        totals.append(top + jnp.log(summed))
    attended = jnp.concatenate(outputs, axis=1).reshape(query.shape).astype(jnp.bfloat16)
    return (attended, totals)


def attention_backward(query, keys, values, seg_all, totals, grad_att):
    rows = query.shape[0] // LEN
    q4 = split_heads(query, rows)
    k4 = split_heads(keys, rows)
    v4 = split_heads(values, rows)
    g4 = split_heads(grad_att, rows)
    seg2 = seg_all.reshape(rows, LEN)
    scale = HD ** (-0.5)
    grad_k = jnp.zeros(k4.shape, jnp.float32)
    grad_v = jnp.zeros(v4.shape, jnp.float32)
    grad_q_parts = []
    for block in range(LEN // QBLK):
        first = block * QBLK
        end = first + QBLK
        scores = block_scores(
            q4[:, first:end], k4[:, :end], seg2[:, first:end], seg2[:, :end], first
        )
        probs = jnp.exp(scores - totals[block])
        weights = probs.astype(jnp.bfloat16)
        grad_w = jnp.einsum(
            "rqhd,rkhd->rhqk", g4[:, first:end], v4[:, :end], preferred_element_type=jnp.float32
        )
        delta = jnp.sum(probs * grad_w, axis=-1, keepdims=True)
        grad_s = (probs * (grad_w - delta)).astype(jnp.bfloat16)
        grad_q_parts.append(
            jnp.einsum("rhqk,rkhd->rqhd", grad_s, k4[:, :end], preferred_element_type=jnp.float32)
            * scale
        )
        padding = ((0, 0), (0, LEN - end), (0, 0), (0, 0))
        grad_k = grad_k + jnp.pad(
            jnp.einsum(
                "rhqk,rqhd->rkhd", grad_s, q4[:, first:end], preferred_element_type=jnp.float32
            )
            * scale,
            padding,
        )
        grad_v = grad_v + jnp.pad(
            jnp.einsum(
                "rhqk,rqhd->rkhd", weights, g4[:, first:end], preferred_element_type=jnp.float32
            ),
            padding,
        )
    shape = query.shape
    grad_q = jnp.concatenate(grad_q_parts, axis=1).reshape(shape).astype(jnp.bfloat16)
    return (
        grad_q,
        grad_k.reshape(shape).astype(jnp.bfloat16),
        grad_v.reshape(shape).astype(jnp.bfloat16),
    )


def tensor_parallel_shards(
    tokens,
    segment_ids,
    w_qkv,
    b_qv,
    w_out,
    b_out,
    w_up,
    b_up,
    w_down,
    b_down,
    ln_gain,
    ln_bias,
    out_grad,
):
    resid = tokens.astype(jnp.float32)
    qv_bias = b_qv.astype(jnp.float32)
    up_bias = b_up.astype(jnp.float32)
    local_rows = tokens.shape[0]
    normed, first_back = jax.vjp(norm_rows, resid, ln_gain[0], ln_bias[0])
    lowered = normed.astype(jnp.bfloat16)
    joined, seg_all = (
        lax.all_gather(lowered, "mp", axis=0, tiled=True),
        lax.all_gather(segment_ids, "mp", axis=0, tiled=True),
    )
    query = (jnp.dot(joined, w_qkv[0], preferred_element_type=jnp.float32) + qv_bias[0]).astype(
        jnp.bfloat16
    )
    keys = jnp.dot(joined, w_qkv[1], preferred_element_type=jnp.float32).astype(jnp.bfloat16)
    values = (jnp.dot(joined, w_qkv[2], preferred_element_type=jnp.float32) + qv_bias[1]).astype(
        jnp.bfloat16
    )
    query, keys, values = (query, keys, values)
    attended, totals = attention_forward(query, keys, values, seg_all)
    attn_sum = lax.psum_scatter(
        jnp.dot(attended, w_out, preferred_element_type=jnp.float32).astype(jnp.bfloat16),
        "mp",
        scatter_dimension=0,
        tiled=True,
    ).astype(jnp.float32)
    mixed = resid + attn_sum + b_out.astype(jnp.float32)
    normed2, second_back = jax.vjp(norm_rows, mixed, ln_gain[1], ln_bias[1])
    lowered2 = normed2.astype(jnp.bfloat16)
    joined2 = lax.all_gather(lowered2, "mp", axis=0, tiled=True)
    pre_act = jnp.dot(joined2, w_up, preferred_element_type=jnp.float32) + up_bias
    pre_act, activ = (pre_act, jax.nn.gelu(pre_act, approximate=False).astype(jnp.bfloat16))
    block_out = (
        mixed
        + lax.psum_scatter(
            jnp.dot(activ, w_down, preferred_element_type=jnp.float32).astype(jnp.bfloat16),
            "mp",
            scatter_dimension=0,
            tiled=True,
        ).astype(jnp.float32)
        + b_down.astype(jnp.float32)
    ).astype(jnp.bfloat16)
    grad_y = out_grad.astype(jnp.float32)
    grad_z = lax.all_gather(out_grad, "mp", axis=0, tiled=True)
    grad_down = jnp.einsum("tf,td->fd", activ, grad_z, preferred_element_type=jnp.float32)
    grad_bdown = jnp.sum(grad_z, axis=0, dtype=jnp.float32)
    grad_act = jnp.einsum("td,fd->tf", grad_z, w_down, preferred_element_type=jnp.float32)
    gelu_back = jax.vjp(lambda value: jax.nn.gelu(value, approximate=False), pre_act)[1]
    grad_pre = gelu_back(grad_act)[0].astype(jnp.bfloat16)
    grad_up = jnp.einsum("td,tf->df", joined2, grad_pre, preferred_element_type=jnp.float32)
    grad_bup = jnp.sum(grad_pre, axis=0, dtype=jnp.float32)
    grad_n2 = lax.psum_scatter(
        jnp.einsum("tf,df->td", grad_pre, w_up, preferred_element_type=jnp.float32).astype(
            jnp.bfloat16
        ),
        "mp",
        scatter_dimension=0,
        tiled=True,
    ).astype(jnp.float32)
    grad_h, grad_g2, grad_s2 = second_back(grad_n2)
    grad_h = grad_h + grad_y
    grad_branch = lax.all_gather(grad_h.astype(jnp.bfloat16), "mp", axis=0, tiled=True)
    grad_wout = jnp.einsum("tc,td->cd", attended, grad_branch, preferred_element_type=jnp.float32)
    grad_bout = jnp.sum(grad_branch, axis=0, dtype=jnp.float32)
    grad_att = jnp.einsum(
        "td,cd->tc", grad_branch, w_out, preferred_element_type=jnp.float32
    ).astype(jnp.bfloat16)
    grad_q, grad_k, grad_v = attention_backward(query, keys, values, seg_all, totals, grad_att)
    grad_qkv = jnp.stack(
        [
            jnp.einsum("td,tc->dc", joined, piece, preferred_element_type=jnp.float32)
            for piece in (grad_q, grad_k, grad_v)
        ]
    )
    grad_bqv = jnp.stack(
        [jnp.sum(grad_q, axis=0, dtype=jnp.float32), jnp.sum(grad_v, axis=0, dtype=jnp.float32)]
    )
    summed = jnp.zeros((local_rows * lax.axis_size("mp"), w_qkv.shape[1]), jnp.float32)
    for index, piece in enumerate((grad_q, grad_k, grad_v)):
        summed = summed + jnp.einsum(
            "tc,dc->td", piece, w_qkv[index], preferred_element_type=jnp.float32
        )
    grad_n1 = lax.psum_scatter(
        summed.astype(jnp.bfloat16), "mp", scatter_dimension=0, tiled=True
    ).astype(jnp.float32)
    grad_x, grad_g1, grad_s1 = first_back(grad_n1)
    grad_in = grad_x + grad_h
    weight_totals = (
        lax.psum(grad_qkv.astype(jnp.bfloat16), "dp").astype(jnp.float32),
        lax.psum(grad_bqv.astype(jnp.bfloat16), "dp").astype(jnp.float32),
        lax.psum(grad_wout.astype(jnp.bfloat16), "dp").astype(jnp.float32),
        lax.psum(grad_bout.astype(jnp.bfloat16), "dp").astype(jnp.float32),
        lax.psum(grad_up.astype(jnp.bfloat16), "dp").astype(jnp.float32),
        lax.psum(grad_bup.astype(jnp.bfloat16), "dp").astype(jnp.float32),
        lax.psum(grad_down.astype(jnp.bfloat16), "dp").astype(jnp.float32),
        lax.psum(grad_bdown.astype(jnp.bfloat16), "dp").astype(jnp.float32),
    )
    norm_totals = lax.psum(
        (jnp.stack([grad_g1, grad_g2]), jnp.stack([grad_s1, grad_s2])), ("dp", "mp")
    )
    return (block_out, grad_in) + tuple(weight_totals) + tuple(norm_totals)


def row_per_chip(mesh):
    return mesh.shape["mp"] == 4 and mesh.shape["dp"] == 8


def swap(value, axis):
    return lax.ppermute(value, axis, [(0, 1), (1, 0)])


def core(value):
    return swap(value, "core")


def cross(value):
    return swap(value, "x")


def after(value, *others):
    return lax.optimization_barrier((value,) + others)[0]


def take(value, at):
    return lax.dynamic_index_in_dim(value, at, 0, keepdims=False)


def place(whole, piece, at):
    return lax.dynamic_update_index_in_dim(whole, piece, at, 0)


def quarter_of(weight):
    me = lax.axis_index("y") + 2 * (lax.axis_index("z") & 1)
    return take(weight.reshape(4, -1, weight.shape[-1]), me)


def share(mine):
    out = [swap(mine, "y")]
    for bits in (2, 3):
        out.append(lax.ppermute(mine, ("z", "y"), [(i, i ^ bits) for i in range(8)]))
    return out


def assemble(mine, others):
    me = lax.axis_index("y") + 2 * (lax.axis_index("z") & 1)
    whole = place(jnp.zeros((4,) + mine.shape, mine.dtype), mine, me)
    for bits, piece in zip((1, 2, 3), others):
        whole = place(whole, piece, me ^ bits)
    return whole.reshape(-1, mine.shape[-1])


def swap_z(value, bits):
    return lax.ppermute(value, "z", [(i, i ^ bits) for i in range(4)])


def by_side(value):
    return value.reshape(2, value.shape[0] // 2, value.shape[1])


class Line:
    def __init__(self):
        self.last = None

    def __call__(self, function, *args):
        if self.last is not None:
            args, _ = lax.optimization_barrier((args, self.last))
        out = function(*args)
        self.last = jax.tree.leaves(out)[0]
        return out


def row_per_chip_shards(
    tokens,
    segment_ids,
    w_qkv,
    b_qv,
    w_out,
    b_out,
    w_up,
    b_up,
    w_down,
    b_down,
    ln_gain,
    ln_bias,
    out_grad,
):
    side, here_y = lax.axis_index("core"), lax.axis_index("y")
    place = jnp.stack([here_y, lax.axis_index("z") & 1]).astype(jnp.int32)
    width, wide = b_qv.shape[1], tokens.shape[1]
    gains, shifts = ln_gain[:, None], ln_bias[:, None]
    line = Line()

    def pair(*parts):
        return line(lambda *all: jnp.concatenate(all), *parts)

    qkv_mine = cross(line(quarter_of, w_qkv.reshape(-1, width)))
    a1_own, sum_dz = line(first_norm, tokens, out_grad, gains[0], shifts[0])
    a1_came = core(a1_own)
    seg_other = core(segment_ids)
    small = cross(jnp.concatenate([b_qv.reshape(-1), b_up]))
    up_quarter = line(quarter_of, w_up)
    down_quarter = line(quarter_of, w_down)

    def ranges(mine, other):
        seg = jnp.concatenate([mine, other])
        start = jnp.sum((seg[None, :] < seg[:, None]).astype(jnp.int32), axis=1)[None]
        ordered = jnp.where(side == 0, seg, jnp.concatenate([other, mine]))
        blocks = ordered.reshape(LEN // BLK, BLK)
        low = jnp.sum((blocks[None, :, -1] < blocks[:, None, 0]).astype(jnp.int32), axis=1)
        return start, jnp.concatenate([(side * (LEN // BLK // 2))[None].astype(jnp.int32), low])

    start, info = line(ranges, segment_ids, seg_other)
    a1 = pair(a1_own, a1_came)
    own = tuple(line(project, a1, w_qkv, b_qv))
    qkv_mine, w_out_now, up_quarter, _ = lax.optimization_barrier((qkv_mine, w_out, up_quarter, own[0]))
    qkv_parts = share(qkv_mine)
    out_other = cross(w_out_now)
    up_mine = cross(up_quarter)
    own = own + tuple(line(partial(attn_fwd, info), *own, start))
    up_mine, down_quarter, _ = lax.optimization_barrier((up_mine, down_quarter, own[3]))
    up_parts = share(up_mine)
    down_mine = cross(down_quarter)
    qkv_other = line(assemble, qkv_mine, qkv_parts).reshape(w_qkv.shape)
    other = tuple(line(project, a1, qkv_other, small[: 2 * width].reshape(2, width)))
    other = other + tuple(line(partial(attn_fwd, info), *other, start))
    down_mine, dz_own, _ = lax.optimization_barrier((down_mine, out_grad, other[3]))
    down_parts = share(down_mine)
    dz_came = core(dz_own)

    here, there = line(partial(sum_dots, nn), [own[3], other[3]], [w_out, out_other])
    came = core(there)
    up_other = line(assemble, up_mine, up_parts)
    mixed, a2_own = line(second_norm, tokens, here, came, b_out[None], gains[1], shifts[1])
    a2_came = core(a2_own)
    dz = pair(dz_own, dz_came)
    a2 = pair(a2_own, a2_came)

    def core_halves(value):
        half = value.shape[0] // 2
        return core(value[:half]), core(value[half:])

    act_other, slope_other = line(up_gelu, a2, up_other, small[2 * width :])
    down_got = cross(line(across_frames, act_other, dz))
    act_own, slope_own = line(up_gelu, a2, w_up, b_up)
    down_own = line(across_frames, act_own, dz)
    du_own, sum_up_own = line(back_act, dz, w_down, slope_own)
    down_other = line(assemble, down_mine, down_parts)
    du_other, sum_up_other = line(back_act, dz, down_other, slope_other)
    here, there = line(partial(sum_dots, nt), [du_own, du_other], [w_up, up_other])
    came = core_halves(there)
    up_got = cross(line(across_frames, a2, du_other))
    grad_h, dattn_own, sums_h = line(norm_back, mixed, here, came, gains[1], out_grad)
    dattn_came = core_halves(dattn_own)
    up_own = line(across_frames, a2, du_own)

    def spread_y(own, got):
        return swap(line(side_sum, 1 - here_y, own, got), "y")

    def near_z(own, got, near):
        send, keep = line(quarter_sums, place, own, got, near)
        return keep, swap_z(send, 1)

    def far_z(keep, came):
        low = line(add_low, keep, came)
        return low, swap_z(low, 2)

    def back_z(low, came):
        mine = line(add_low, low, came)
        near = swap_z(mine, 1)
        return (mine, swap(mine, "y")), (near, swap(near, "y"))

    def wait_near(total):
        near, other = total[1]
        return total[0], (line(lambda value: value, near), other)

    def put(pair, prior=None, extra=0):
        fill = partial(settle, flip=0 if prior is None else 1, extra=extra)
        return line(lambda mine, other, prior: fill(place, mine, other, prior=prior), *pair, prior)

    down_own, down_got = by_side(down_own), by_side(down_got)
    down_near = spread_y(down_own, down_got)
    dattn = pair(dattn_own, *dattn_came)

    def back(entry, weight):
        query, keys, values, out, lse = entry
        cot = line(turn_back, dattn, weight)
        trio = line(partial(attn_bwd, info), query, keys, values, start, out, lse, cot)
        return (trio,) + tuple(line(frame_sums, a1, trio, out, dattn))

    trio_other, attn_other, sum_trio_other = back(other, out_other)
    first_got = cross(attn_other[0])
    second_got = cross(attn_other[1])
    down_sum = near_z(down_own, down_got, down_near)
    y_here, y_there = line(partial(sum_dots, nn), [act_own, act_other], [w_down, down_other])
    y_came = core(y_there)
    query, keys, values, out, lse = own
    cot = line(turn_back, dattn, w_out)
    down_sum = far_z(*down_sum)
    up_own, up_got = by_side(up_own), by_side(up_got)
    up_near = spread_y(up_own, up_got)
    trio_own = line(partial(attn_bwd, info), query, keys, values, start, out, lse, cot)
    attn_own, sum_trio_own = line(frame_sums, a1, trio_own, out, dattn)
    first_own, first_got = by_side(attn_own[0]), by_side(first_got)
    down_sum = back_z(*down_sum)
    block_out = line(finish, mixed, y_here, y_came, b_down[None])
    first_near = spread_y(first_own, first_got)
    here, there = line(partial(sum_dots, nt), [trio_own, trio_other], [w_qkv, qkv_other])
    came = core_halves(there)
    up_sum = near_z(up_own, up_got, up_near)
    down_sum = wait_near(down_sum)
    grad_in, _, sums_x = line(norm_back, tokens, here, came, gains[0], grad_h)
    common = line(common_rows, sums_h, sum_dz, sums_x)
    common_came = core(common)

    first_sum = near_z(first_own, first_got, first_near)
    up_sum = far_z(*up_sum)
    lines_came = cross(line(lines_of, sum_trio_other, sum_up_other, common, common_came))
    lines_own = line(lines_of, sum_trio_own, sum_up_own, common, common_came)
    second_own = line(ride, attn_own[1], lines_own, lines_came)
    second_own, second_got = by_side(second_own), by_side(second_got)
    second_near = spread_y(second_own, second_got)
    first_sum = far_z(*first_sum)
    grad_down = put(down_sum[0])
    grad_down = put(down_sum[1], grad_down)
    up_sum = back_z(*up_sum)
    first_sum = back_z(*first_sum)
    second_sum = near_z(second_own, second_got, second_near)
    up_sum = wait_near(up_sum)
    grad_up = put(up_sum[0])
    first_sum = wait_near(first_sum)
    second_sum = far_z(*second_sum)
    first = put(first_sum[0], extra=wide)
    grad_up = put(up_sum[1], grad_up)
    first = put(first_sum[1], first, extra=wide)
    second_sum = back_z(*second_sum)
    second = put(second_sum[0])
    second = put(second_sum[1], second)
    grad_qkv = lax.dynamic_update_slice(first, second[:wide], (2 * wide, 0)).reshape(w_qkv.shape)
    grad_wout = jnp.swapaxes(second[wide : 2 * wide].reshape(-1, w_out.shape[0], width), 0, 1)
    grad_wout = grad_wout.reshape(w_out.shape)
    vector = second[2 * wide :].reshape(-1)
    units = b_up.shape[0]
    ends = [2 * width, units, wide, wide, 2 * wide, 2 * wide]
    cuts = [sum(ends[:i]) for i in range(len(ends) + 1)]
    grad_bqv, grad_bup, grad_bout, grad_bdown, grad_gain, grad_shift = [
        vector[low:high] for low, high in zip(cuts[:-1], cuts[1:])
    ]
    return (
        block_out,
        grad_in,
        grad_qkv,
        grad_bqv.reshape(b_qv.shape),
        grad_wout,
        grad_bout,
        grad_up,
        grad_bup,
        grad_down,
        grad_bdown,
        grad_gain.reshape(ln_gain.shape),
        grad_shift.reshape(ln_bias.shape),
    )


def solution(mesh):
    rows, frames = ("dp", "mp"), "mp"
    body = tensor_parallel_shards
    if row_per_chip(mesh):
        shape = (mesh.shape["dp"] // 2, 2, mesh.shape["mp"] // 2, 2)
        mesh = Mesh(mesh.devices.reshape(shape), ("z", "y", "x", "core"))
        rows, frames = ("z", "y", "x", "core"), ("x", "core")
        body = row_per_chip_shards
    in_specs = (
        P(rows, None),
        P(rows),
        P(None, None, frames),
        P(None, frames),
        P(frames, None),
        P(),
        P(None, frames),
        P(frames),
        P(frames, None),
        P(),
        P(),
        P(),
        P(rows, None),
    )
    out_specs = (
        P(rows, None),
        P(rows, None),
        P(None, None, frames),
        P(None, frames),
        P(frames, None),
        P(),
        P(None, frames),
        P(frames),
        P(frames, None),
        P(),
        P(),
        P(),
    )
    return jax.shard_map(body, mesh=mesh, in_specs=in_specs, out_specs=out_specs, check_vma=False)
```

```python
from functools import partial

import jax
import jax.numpy as jnp
from jax import lax
from jax.experimental import pallas as pl
from jax.experimental.pallas import tpu as pltpu
from jax.sharding import Mesh
from jax.sharding import PartitionSpec as P

HD = 64
LEN = 1024
QBLK = 512
EPS = 1e-05
BLK = 256

NEG = -1e30
GRANT = 10 << 20
EXTRA = 128
BRIEF = pl.CostEstimate(flops=1, bytes_accessed=1, transcendentals=0)
f32 = jnp.float32
bf16 = jnp.bfloat16


def nt(left, right):
    return lax.dot_general(left, right, (((1,), (1,)), ((), ())), preferred_element_type=f32)


def nn(left, right):
    return lax.dot_general(left, right, (((1,), (0,)), ((), ())), preferred_element_type=f32)


def tn(left, right):
    return lax.dot_general(left, right, (((0,), (0,)), ((), ())), preferred_element_type=f32)


def attn_bias(block, j, first):
    q_pos = block * BLK + lax.broadcasted_iota(jnp.int32, (1, BLK), 1)
    k_pos = j * BLK + lax.broadcasted_iota(jnp.int32, (BLK, BLK), 0)
    return jnp.where((k_pos >= first) & (k_pos <= q_pos), 0.0, NEG)


def head_rows(refs, scratch, heads):
    lane = lax.broadcasted_iota(jnp.int32, (LEN, 2 * HD), 1)
    for ref, out in zip(refs, scratch):
        for h in range(heads):
            pair = ref[:, (h // 2) * 2 * HD : (h // 2 + 1) * 2 * HD]
            out[h] = jnp.where((lane < HD) == (h % 2 == 0), pair, jnp.zeros_like(pair))


def attn_fwd_body(info, q_ref, k_ref, v_ref, st_ref, o_ref, lse_ref, k_heads, v_turned):
    block = pl.program_id(0)
    heads = q_ref.shape[1] // HD
    first = st_ref[...]

    @pl.when(block == 0)
    def _():
        head_rows([k_ref], [k_heads], heads)
        for pair in range(heads // 2):
            turned = v_ref[:, pair * 2 * HD : (pair + 1) * 2 * HD].T
            for h in (0, 1):
                v_turned[2 * pair + h, :HD] = turned[h * HD : (h + 1) * HD]
                v_turned[2 * pair + h, HD:] = jnp.ones((16, LEN), bf16)

    def step(at, carry):
        j = block - at
        row = pl.multiple_of((j ^ info[0]) * BLK, BLK)
        bias = attn_bias(block, j, first)
        out = []
        for h in range(heads):
            top, acc = carry[h]
            query = q_ref[:, (h // 2) * 2 * HD : (h // 2 + 1) * 2 * HD]
            s = nt(k_heads[h, pl.ds(row, BLK), :], query) + bias
            new = jnp.maximum(top, jnp.max(s, axis=0, keepdims=True))
            p = jnp.exp(s - new).astype(bf16)
            acc = acc * jnp.exp(top - new) + nn(v_turned[h, :, pl.ds(row, BLK)], p)
            out.append((new, acc))
        return tuple(out)

    init = tuple((jnp.full((1, BLK), NEG, f32), jnp.zeros((HD + 16, BLK), f32)) for _ in range(heads))
    done = lax.fori_loop(0, block + 1 - info[1 + block], step, init)
    for pair in range(heads // 2):
        both = [acc[:HD] / acc[HD : HD + 1] for _, acc in done[2 * pair : 2 * pair + 2]]
        o_ref[:, pair * 2 * HD : (pair + 1) * 2 * HD] = jnp.concatenate(both, axis=0).T.astype(bf16)
    for h in range(heads):
        top, acc = done[h]
        lse_ref[h : h + 1, :] = top + jnp.log(acc[HD : HD + 1])


def attn_bwd_body(base, info, q_ref, k_ref, v_ref, st_ref, o_ref, lse_ref, do_ref, d_ref, k_heads, v_heads, dk_acc, dv_acc):
    block = pl.program_id(0)
    heads = q_ref.shape[1] // HD
    first = st_ref[...]
    lane = lax.broadcasted_iota(jnp.int32, (BLK, 2 * HD), 1)

    @pl.when(block == 0)
    def _():
        head_rows([k_ref, v_ref], [k_heads, v_heads], heads)
        dk_acc[...] = jnp.zeros_like(dk_acc)
        dv_acc[...] = jnp.zeros_like(dv_acc)

    deltas = []
    for pair in range(heads // 2):
        cols = slice(pair * 2 * HD, (pair + 1) * 2 * HD)
        turned = (do_ref[:, cols].astype(f32) * o_ref[:, cols].astype(f32)).T
        for h in (0, 1):
            deltas.append(jnp.sum(turned[h * HD : (h + 1) * HD], axis=0, keepdims=True))

    def step(j, dqs):
        row = pl.multiple_of((j ^ info[0]) * BLK, BLK)
        bias = attn_bias(block, j, first)
        out = list(dqs)
        for pair in range(heads // 2):
            cols = slice(pair * 2 * HD, (pair + 1) * 2 * HD)
            query, cot = q_ref[:, cols], do_ref[:, cols]
            dk = dk_acc[pl.ds(row, BLK), cols]
            dv = dv_acc[pl.ds(row, BLK), cols]
            for h in (2 * pair, 2 * pair + 1):
                mask = (lane < HD) == (h % 2 == 0)
                keys = k_heads[h, pl.ds(row, BLK), :]
                p = jnp.exp(nt(keys, query) + (bias - lse_ref[base + h : base + h + 1, :]))
                dp = nt(v_heads[h, pl.ds(row, BLK), :], cot)
                ds = (p * (dp - deltas[h])).astype(bf16)
                dv = dv + nn(p.astype(bf16), jnp.where(mask, cot, jnp.zeros_like(cot)))
                dk = dk + nn(ds, jnp.where(mask, query, jnp.zeros_like(query)))
                out[pair] = out[pair] + tn(ds, keys)
            dk_acc[pl.ds(row, BLK), cols] = dk
            dv_acc[pl.ds(row, BLK), cols] = dv
        return tuple(out)

    init = tuple(jnp.zeros((BLK, 2 * HD), f32) for _ in range(heads // 2))
    dqs = lax.fori_loop(info[1 + block], block + 1, step, init)
    here = pl.multiple_of((block ^ info[0]) * BLK, BLK)
    for pair in range(heads // 2):
        cols = slice(pair * 2 * HD, (pair + 1) * 2 * HD)
        d_ref[0, pl.ds(here, BLK), cols] = (dqs[pair] * HD**-0.5).astype(bf16)

    @pl.when(block == pl.num_programs(0) - 1)
    def _():
        d_ref[1] = dk_acc[...].astype(bf16)
        d_ref[2] = dv_acc[...].astype(bf16)


def attn_specs(width):
    small = pl.BlockSpec((BLK, width), lambda i, info: (i ^ info[0], 0))
    whole = pl.BlockSpec((LEN, width), lambda i, info: (0, 0))
    start = pl.BlockSpec((1, BLK), lambda i, info: (0, i ^ info[0]))
    lse = pl.BlockSpec((width // HD, BLK), lambda i, info: (0, i ^ info[0]))
    return small, whole, start, lse


def attn_fwd(info, query, keys, values, start):
    width = query.shape[1]
    heads = width // HD
    small, whole, first, lse = attn_specs(width)
    return pl.pallas_call(
        attn_fwd_body,
        out_shape=(jax.ShapeDtypeStruct(query.shape, bf16), jax.ShapeDtypeStruct((heads, LEN), f32)),
        grid_spec=pltpu.PrefetchScalarGridSpec(
            num_scalar_prefetch=1,
            grid=(LEN // BLK,),
            in_specs=[small, whole, whole, first],
            out_specs=[small, lse],
            scratch_shapes=[pltpu.VMEM((heads, LEN, 2 * HD), bf16), pltpu.VMEM((heads, HD + 16, LEN), bf16)],
        ),
        cost_estimate=BRIEF,
        compiler_params=pltpu.CompilerParams(vmem_limit_bytes=GRANT),
        name="attn_fwd",
    )(info, query, keys, values, start)


def attn_bwd(info, query, keys, values, start, out, lse, cot, part=0, parts=1, prior=None):
    width = query.shape[1] // parts
    heads = width // HD
    small = pl.BlockSpec((BLK, width), lambda i, info: (i ^ info[0], part))
    whole = pl.BlockSpec((LEN, width), lambda i, info: (0, part))
    first = pl.BlockSpec((1, BLK), lambda i, info: (0, i ^ info[0]))
    lse_spec = pl.BlockSpec((heads * parts, BLK), lambda i, info: (0, i ^ info[0]))
    more = () if prior is None else (prior,)

    def body(*refs):
        attn_bwd_body(part * heads, *refs[:8], *refs[8 + len(more) :])

    return pl.pallas_call(
        body,
        out_shape=jax.ShapeDtypeStruct((3,) + query.shape, bf16),
        grid_spec=pltpu.PrefetchScalarGridSpec(
            num_scalar_prefetch=1,
            grid=(LEN // BLK,),
            in_specs=[small, whole, whole, first, small, lse_spec, small]
            + [pl.BlockSpec(memory_space=pl.ANY)] * len(more),
            out_specs=pl.BlockSpec((3, LEN, width), lambda i, info: (0, 0, part)),
            scratch_shapes=[
                pltpu.VMEM((heads, LEN, 2 * HD), bf16),
                pltpu.VMEM((heads, LEN, 2 * HD), bf16),
                pltpu.VMEM((LEN, width), f32),
                pltpu.VMEM((LEN, width), f32),
            ],
        ),
        input_output_aliases={8: 0} if more else {},
        cost_estimate=BRIEF,
        compiler_params=pltpu.CompilerParams(vmem_limit_bytes=GRANT),
        name="attn_bwd",
    )(info, query, keys, values, start, out, lse, cot, *more)


def up_body(a_ref, w_ref, b_ref, g_ref, s_ref):
    rows = a_ref[...]
    for part in range(w_ref.shape[1] // 256):
        cols = slice(part * 256, part * 256 + 256)
        u = nn(rows, w_ref[:, cols]) + b_ref[:, cols].astype(f32)
        size = jnp.abs(u)
        t = 1.0 / (1.0 + 0.3275911 * 0.7071067811865476 * size)
        poly = t * (0.5 * 0.254829592 + t * (0.5 * -0.284496736 + t * (0.5 * 1.421413741 + t * (0.5 * -1.453152027 + t * (0.5 * 1.061405429)))))
        bell = jnp.exp(-0.5 * u * u)
        tail = poly * bell
        cdf = jnp.where(u >= 0, 1.0 - tail, tail)
        g_ref[:, cols] = (u * cdf).astype(bf16)
        s_ref[:, cols] = (cdf + u * bell * 0.3989422804014327).astype(bf16)


def up_gelu(rows, weight, bias):
    m, k = rows.shape
    n = weight.shape[1]
    bm = 256
    shape = jax.ShapeDtypeStruct((m, n), bf16)
    tile = pl.BlockSpec((bm, n), lambda i: (i, 0))
    return pl.pallas_call(
        up_body,
        out_shape=(shape, shape),
        grid=(m // bm,),
        in_specs=[pl.BlockSpec((bm, k), lambda i: (i, 0)), pl.BlockSpec((k, n), lambda i: (0, 0)), pl.BlockSpec((1, n), lambda i: (0, 0))],
        out_specs=(tile, tile),
        cost_estimate=BRIEF,
        compiler_params=pltpu.CompilerParams(vmem_limit_bytes=GRANT),
        name="up_gelu",
    )(rows, weight, bias.reshape(1, n))


def const_spec(shape):
    return pl.BlockSpec(shape, lambda i: (0,) * len(shape))


def row_spec(rows, cols):
    return pl.BlockSpec((rows, cols), lambda i: (i, 0))


def project_body(a_ref, w_ref, b_ref, q_ref, k_ref, v_ref):
    rows = a_ref[...]
    q_ref[...] = (nn(rows, w_ref[0]) + b_ref[0:1].astype(f32)).astype(bf16) * jnp.bfloat16(HD**-0.5)
    k_ref[...] = nn(rows, w_ref[1]).astype(bf16)
    v_ref[...] = (nn(rows, w_ref[2]) + b_ref[1:2].astype(f32)).astype(bf16)


def project(rows, weight, bias):
    m, k = rows.shape
    n = weight.shape[2]
    tile = 256
    shape = jax.ShapeDtypeStruct((m, n), bf16)
    return pl.pallas_call(
        project_body,
        out_shape=(shape, shape, shape),
        grid=(m // tile,),
        in_specs=[row_spec(tile, k), const_spec(weight.shape), const_spec(bias.shape)],
        out_specs=[row_spec(tile, n)] * 3,
        cost_estimate=BRIEF,
        compiler_params=pltpu.CompilerParams(vmem_limit_bytes=GRANT),
        name="project",
    )(rows, weight, bias)


def sum_dots(product, lefts, rights):
    stacked = lefts[0].ndim == 3
    m, k = lefts[0].shape[-2:]
    n = rights[0].shape[-1] if product is nn else rights[0].shape[-2]
    terms = len(lefts)
    tile = 256
    steps = m // tile // 2

    def body(*refs):
        total = None
        for left, right in zip(refs[:terms], refs[terms : 2 * terms]):
            for at in range(left.shape[0] if stacked else 1):
                term = product(left[at], right[at]) if stacked else product(left[...], right[...])
                total = term if total is None else total + term
        here, there = refs[2 * terms :]

        @pl.when(pl.program_id(0) < steps)
        def _():
            there[...] = total.astype(bf16)

        @pl.when(pl.program_id(0) >= steps)
        def _():
            here[...] = total

    def turn(i):
        return jnp.where(i < steps, i + steps, i - steps)

    if stacked:
        left_spec = pl.BlockSpec((lefts[0].shape[0], tile, k), lambda i: (0, turn(i), 0))
    else:
        left_spec = pl.BlockSpec((tile, k), lambda i: (turn(i), 0))
    return pl.pallas_call(
        body,
        out_shape=(jax.ShapeDtypeStruct((m // 2, n), f32), jax.ShapeDtypeStruct((m // 2, n), bf16)),
        grid=(2 * steps,),
        in_specs=[left_spec] * terms + [const_spec(r.shape) for r in rights],
        out_specs=[
            pl.BlockSpec((tile, n), lambda i: (jnp.maximum(i - steps, 0), 0)),
            pl.BlockSpec((tile, n), lambda i: (jnp.minimum(i, steps - 1), 0)),
        ],
        cost_estimate=BRIEF,
        compiler_params=pltpu.CompilerParams(vmem_limit_bytes=GRANT),
        name="sum_dots",
    )(*lefts, *rights)


def center_rows(rows):
    center = rows - jnp.mean(rows, axis=-1, keepdims=True)
    scale = lax.rsqrt(jnp.mean(center * center, axis=-1, keepdims=True) + EPS)
    return center * scale, scale


def first_norm_body(x_ref, g_ref, gain_ref, shift_ref, a_ref, sum_ref):
    normal, _ = center_rows(x_ref[...].astype(f32))
    a_ref[...] = (normal * gain_ref[...] + shift_ref[...]).astype(bf16)

    @pl.when(pl.program_id(0) == 0)
    def _():
        sum_ref[...] = jnp.zeros_like(sum_ref)

    sum_ref[...] += jnp.sum(g_ref[...].astype(f32), axis=0, keepdims=True)


def first_norm(tokens, cotangent, gain, shift):
    m, d = tokens.shape
    tile = 128
    return pl.pallas_call(
        first_norm_body,
        out_shape=(jax.ShapeDtypeStruct((m, d), bf16), jax.ShapeDtypeStruct((1, d), f32)),
        grid=(m // tile,),
        in_specs=[row_spec(tile, d), row_spec(tile, d), const_spec((1, d)), const_spec((1, d))],
        out_specs=[row_spec(tile, d), const_spec((1, d))],
        cost_estimate=BRIEF,
        compiler_params=pltpu.CompilerParams(vmem_limit_bytes=GRANT),
        name="first_norm",
    )(tokens, cotangent, gain, shift)


def second_norm_body(x_ref, here_ref, came_ref, b_ref, gain_ref, shift_ref, h_ref, a_ref):
    mixed = x_ref[...].astype(f32) + (here_ref[...] + came_ref[...].astype(f32)) + b_ref[...].astype(f32)
    h_ref[...] = mixed
    normal, _ = center_rows(mixed)
    a_ref[...] = (normal * gain_ref[...] + shift_ref[...]).astype(bf16)


def second_norm(tokens, here, came, bias, gain, shift):
    m, d = tokens.shape
    tile = 128
    return pl.pallas_call(
        second_norm_body,
        out_shape=(jax.ShapeDtypeStruct((m, d), f32), jax.ShapeDtypeStruct((m, d), bf16)),
        grid=(m // tile,),
        in_specs=[row_spec(tile, d)] * 3 + [const_spec((1, d))] * 3,
        out_specs=[row_spec(tile, d)] * 2,
        cost_estimate=BRIEF,
        compiler_params=pltpu.CompilerParams(vmem_limit_bytes=GRANT),
        name="second_norm",
    )(tokens, here, came, bias, gain, shift)


def norm_back_body(v_ref, here_ref, low_came_ref, high_came_ref, gain_ref, res_ref, out_ref, low_ref, sums_ref):
    normal, scale = center_rows(v_ref[...].astype(f32))
    first = pl.program_id(0) < pl.num_programs(0) // 2
    came = jnp.where(first, low_came_ref[...], high_came_ref[...])
    grad = here_ref[...] + came.astype(f32)
    scaled = grad * gain_ref[...]
    inner = jnp.mean(scaled * normal, axis=-1, keepdims=True)
    back = scale * (scaled - jnp.mean(scaled, axis=-1, keepdims=True) - normal * inner)
    back = back + res_ref[...].astype(f32)
    low = back.astype(bf16)
    out_ref[...] = back
    low_ref[...] = low

    @pl.when(pl.program_id(0) == 0)
    def _():
        sums_ref[...] = jnp.zeros_like(sums_ref)

    sums_ref[0:1] += jnp.sum(grad * normal, axis=0, keepdims=True)
    sums_ref[1:2] += jnp.sum(grad, axis=0, keepdims=True)
    sums_ref[2:3] += jnp.sum(low.astype(f32), axis=0, keepdims=True)


def norm_back(values, here, came, gain, residual):
    m, d = values.shape
    tile = 128
    half = m // tile // 2
    low = pl.BlockSpec((tile, d), lambda i: (jnp.minimum(i, half - 1), 0))
    high = pl.BlockSpec((tile, d), lambda i: (jnp.maximum(i - half, 0), 0))
    return pl.pallas_call(
        norm_back_body,
        out_shape=(
            jax.ShapeDtypeStruct((m, d), f32),
            jax.ShapeDtypeStruct((m, d), bf16),
            jax.ShapeDtypeStruct((8, d), f32),
        ),
        grid=(m // tile,),
        in_specs=[row_spec(tile, d)] * 2 + [low, high, const_spec((1, d)), row_spec(tile, d)],
        out_specs=[row_spec(tile, d)] * 2 + [const_spec((8, d))],
        cost_estimate=BRIEF,
        compiler_params=pltpu.CompilerParams(vmem_limit_bytes=GRANT),
        name="norm_back",
    )(values, here, *came, gain, residual)


def back_act_body(z_ref, w_ref, s_ref, du_ref, sum_ref):
    du = (nt(z_ref[...], w_ref[...]) * s_ref[...].astype(f32)).astype(bf16)
    du_ref[...] = du

    @pl.when(pl.program_id(0) == 0)
    def _():
        sum_ref[...] = jnp.zeros_like(sum_ref)

    sum_ref[...] += jnp.sum(du.astype(f32), axis=0, keepdims=True)


def back_act(cotangent, weight, slope):
    m, d = cotangent.shape
    n = weight.shape[0]
    tile = 256
    return pl.pallas_call(
        back_act_body,
        out_shape=(jax.ShapeDtypeStruct((m, n), bf16), jax.ShapeDtypeStruct((1, n), f32)),
        grid=(m // tile,),
        in_specs=[row_spec(tile, d), const_spec((n, d)), row_spec(tile, n)],
        out_specs=[row_spec(tile, n), const_spec((1, n))],
        cost_estimate=BRIEF,
        compiler_params=pltpu.CompilerParams(vmem_limit_bytes=GRANT),
        name="back_act",
    )(cotangent, weight, slope)


def frame_sums_body(a_ref, d_ref, o_ref, g_ref, one_ref, two_ref, sums_ref, a_turned):
    rows, width = g_ref.shape[1], o_ref.shape[1]
    count = rows // width
    a_turned[...] = a_ref[...].T
    for at in range(4 * count):
        kind, part = divmod(at, count)
        out = one_ref if at < 2 * count else two_ref
        if kind < 3:
            block = nn(a_turned[part * width : (part + 1) * width, :], d_ref[kind])
        else:
            block = tn(o_ref[...], g_ref[:, part * width : (part + 1) * width])
        low = (at % (2 * count)) * width
        out[low : low + width, :] = block.astype(bf16)
    two_ref[2 * rows :, :] = jnp.zeros((EXTRA, width), bf16)
    for kind in range(3):
        sums_ref[kind] = jnp.sum(d_ref[kind].astype(f32), axis=0, keepdims=True)


def frame_sums(rows, trio, out, cotangent):
    t, d = rows.shape
    n = trio.shape[2]
    half = jax.ShapeDtypeStruct((2 * d, n), bf16)
    one, two, sums = pl.pallas_call(
        frame_sums_body,
        out_shape=(half, jax.ShapeDtypeStruct((2 * d + EXTRA, n), bf16), jax.ShapeDtypeStruct((3, 1, n), f32)),
        grid=(1,),
        in_specs=[const_spec((t, d)), const_spec((3, t, n)), const_spec((t, n)), const_spec((t, d))],
        out_specs=[const_spec((2 * d, n)), const_spec((2 * d + EXTRA, n)), const_spec((3, 1, n))],
        scratch_shapes=[pltpu.VMEM((d, t), bf16)],
        cost_estimate=BRIEF,
        compiler_params=pltpu.CompilerParams(vmem_limit_bytes=GRANT),
        name="frame_sums",
    )(rows, trio, out, cotangent)
    return (one, two), sums


def frames_body(a_ref, g_ref, out_ref, turned):
    tile = out_ref.shape[0]
    turned[...] = a_ref[...].T
    out_ref[...] = nn(turned[...], g_ref[...]).astype(bf16)


def across_frames(left, right):
    t, m = left.shape
    n = right.shape[1]
    tile = 256
    return pl.pallas_call(
        frames_body,
        out_shape=jax.ShapeDtypeStruct((m, n), bf16),
        grid=(m // tile,),
        in_specs=[pl.BlockSpec((t, tile), lambda i: (0, i)), const_spec((t, n))],
        out_specs=row_spec(tile, n),
        scratch_shapes=[pltpu.VMEM((tile, t), bf16)],
        cost_estimate=BRIEF,
        compiler_params=pltpu.CompilerParams(vmem_limit_bytes=GRANT),
        name="across_frames",
    )(left, right)


def turn_back_body(a_ref, w_ref, out_ref):
    out_ref[...] = nt(a_ref[...], w_ref[...]).astype(bf16)


def turn_back(rows, weight):
    m, k = rows.shape
    n = weight.shape[0]
    tile = 256
    return pl.pallas_call(
        turn_back_body,
        out_shape=jax.ShapeDtypeStruct((m, n), bf16),
        grid=(m // tile,),
        in_specs=[row_spec(tile, k), const_spec((n, k))],
        out_specs=row_spec(tile, n),
        cost_estimate=BRIEF,
        compiler_params=pltpu.CompilerParams(vmem_limit_bytes=GRANT),
        name="turn_back",
    )(rows, weight)


def side_sum_body(info, *refs):
    total = refs[0][0].astype(f32)
    for ref in refs[1:-1]:
        total = total + (ref[0] if len(ref.shape) == 3 else ref[...]).astype(f32)
    refs[-1][...] = total.astype(bf16)


def side_sum(side, own, got, near=None):
    _, rows, cols = own.shape
    tile = rows // 4
    pick_spec = pl.BlockSpec((1, tile, cols), lambda i, info: (info[0], i, 0))
    flat = pl.BlockSpec((tile, cols), lambda i, info: (i, 0))
    args = [own, got] + ([] if near is None else [near])
    return pl.pallas_call(
        side_sum_body,
        out_shape=jax.ShapeDtypeStruct((rows, cols), bf16),
        grid_spec=pltpu.PrefetchScalarGridSpec(
            num_scalar_prefetch=1,
            grid=(4,),
            in_specs=[pick_spec, pick_spec] + [flat] * (len(args) - 2),
            out_specs=flat,
        ),
        cost_estimate=BRIEF,
        compiler_params=pltpu.CompilerParams(vmem_limit_bytes=GRANT),
        name="side_sum",
    )(side[None], *args)


def add_low_body(a_ref, b_ref, out_ref):
    out_ref[...] = (a_ref[...].astype(f32) + b_ref[...].astype(f32)).astype(bf16)


def add_low(left, right):
    rows, cols = left.shape
    tile = rows // 2
    return pl.pallas_call(
        add_low_body,
        out_shape=jax.ShapeDtypeStruct((rows, cols), bf16),
        grid=(2,),
        in_specs=[row_spec(tile, cols)] * 2,
        out_specs=row_spec(tile, cols),
        cost_estimate=BRIEF,
        compiler_params=pltpu.CompilerParams(vmem_limit_bytes=GRANT),
        name="add_low",
    )(left, right)


def quarter_sums_body(info, own_ref, got_ref, near_ref, send_ref, keep_ref):
    total = own_ref[0, 0].astype(f32) + got_ref[0, 0].astype(f32) + near_ref[0].astype(f32)

    @pl.when(pl.program_id(0) == 0)
    def _():
        send_ref[...] = total.astype(bf16)

    @pl.when(pl.program_id(0) == 1)
    def _():
        keep_ref[...] = total.astype(bf16)


def quarter_sums(place, own, got, near):
    _, rows, cols = own.shape
    rows = rows // 2
    tile = rows // 2
    deep = pl.BlockSpec((1, 1, tile, cols), lambda f, i, info: (info[0], info[1] ^ 1 ^ f, i, 0))
    flat = pl.BlockSpec((1, tile, cols), lambda f, i, info: (info[1] ^ 1 ^ f, i, 0))
    shape = jax.ShapeDtypeStruct((rows, cols), bf16)
    return pl.pallas_call(
        quarter_sums_body,
        out_shape=(shape, shape),
        grid_spec=pltpu.PrefetchScalarGridSpec(
            num_scalar_prefetch=1,
            grid=(2, 2),
            in_specs=[deep, deep, flat],
            out_specs=[
                pl.BlockSpec((tile, cols), lambda f, i, info: (jnp.where(f == 0, i, 1), 0)),
                pl.BlockSpec((tile, cols), lambda f, i, info: (jnp.where(f == 0, 0, i), 0)),
            ],
        ),
        cost_estimate=BRIEF,
        compiler_params=pltpu.CompilerParams(vmem_limit_bytes=GRANT),
        name="quarter_sums",
    )(place, own.reshape(2, 2, rows, cols), got.reshape(2, 2, rows, cols), near.reshape(2, rows, cols))


def settle_body(info, mine_ref, other_ref, *rest):
    for at, ref in enumerate((mine_ref, other_ref)):

        @pl.when(pl.program_id(0) == at)
        def _(ref=ref):
            rest[-1][0] = ref[...].astype(f32)


def settle(place, mine, other, flip=0, prior=None, extra=0):
    rows, cols = mine.shape
    tile = rows // 2
    first = pl.BlockSpec((tile, cols), lambda f, i, info: (jnp.where(f == 0, i, 1), 0))
    second = pl.BlockSpec((tile, cols), lambda f, i, info: (jnp.where(f == 0, 0, i), 0))
    more = () if prior is None else (prior.reshape(-1, rows, cols),)
    out = pl.pallas_call(
        settle_body,
        out_shape=jax.ShapeDtypeStruct((4 + extra // rows, rows, cols), f32),
        grid_spec=pltpu.PrefetchScalarGridSpec(
            num_scalar_prefetch=1,
            grid=(2, 2),
            in_specs=[first, second] + [pl.BlockSpec(memory_space=pl.ANY)] * len(more),
            out_specs=pl.BlockSpec(
                (1, tile, cols), lambda f, i, info: (2 * (info[0] ^ f) + (info[1] ^ flip), i, 0)
            ),
        ),
        input_output_aliases={3: 0} if more else {},
        cost_estimate=BRIEF,
        compiler_params=pltpu.CompilerParams(vmem_limit_bytes=GRANT),
        name="settle",
    )(place, mine, other, *more)
    return out.reshape(-1, cols)


def finish_body(h_ref, here_ref, came_ref, b_ref, out_ref):
    out_ref[...] = (h_ref[...] + here_ref[...] + came_ref[...].astype(f32) + b_ref[...].astype(f32)).astype(bf16)


def finish(mixed, here, came, bias):
    m, d = mixed.shape
    tile = 128
    return pl.pallas_call(
        finish_body,
        out_shape=jax.ShapeDtypeStruct((m, d), bf16),
        grid=(m // tile,),
        in_specs=[row_spec(tile, d)] * 3 + [const_spec((1, d))],
        out_specs=row_spec(tile, d),
        cost_estimate=BRIEF,
        compiler_params=pltpu.CompilerParams(vmem_limit_bytes=GRANT),
        name="finish",
    )(mixed, here, came, bias)


def common_body(h_ref, z_ref, x_ref, out_ref):
    out_ref[...] = jnp.zeros_like(out_ref)
    rows = [h_ref[2:3], z_ref[0:1], x_ref[0:1], h_ref[0:1], x_ref[1:2], h_ref[1:2]]
    for at, row in enumerate(rows):
        out_ref[at : at + 1] = row


def common_rows(sums_h, sum_dz, sums_x):
    return pl.pallas_call(
        common_body,
        out_shape=jax.ShapeDtypeStruct(sums_h.shape, f32),
        cost_estimate=BRIEF,
        compiler_params=pltpu.CompilerParams(vmem_limit_bytes=GRANT),
        name="common_rows",
    )(sums_h, sum_dz, sums_x)


def lines_body(trio_ref, up_ref, mine_ref, came_ref, out_ref):
    cols = out_ref.shape[1]
    out_ref[...] = jnp.zeros_like(out_ref)
    out_ref[0:1] = trio_ref[0]
    out_ref[1:2] = trio_ref[2]
    at = 2
    for part in range(up_ref.shape[1] // cols):
        out_ref[at : at + 1] = up_ref[:, part * cols : (part + 1) * cols]
        at += 1
    both = mine_ref[...] + came_ref[...]
    for row in range(6):
        for part in range(both.shape[1] // cols):
            out_ref[at : at + 1] = both[row : row + 1, part * cols : (part + 1) * cols]
            at += 1


def lines_of(trio, up, mine, came):
    return pl.pallas_call(
        lines_body,
        out_shape=jax.ShapeDtypeStruct((EXTRA // 4, trio.shape[2]), f32),
        cost_estimate=BRIEF,
        compiler_params=pltpu.CompilerParams(vmem_limit_bytes=GRANT),
        name="lines_of",
    )(trio, up, mine, came)


def ride_body(mine_ref, came_ref, whole_ref, out_ref, lines):
    lines[...] = jnp.zeros_like(lines)
    lines[: mine_ref.shape[0]] = mine_ref[...] + came_ref[...]
    out_ref[...] = lines[...].astype(bf16)


def ride(whole, mine, came):
    rows, cols = whole.shape
    return pl.pallas_call(
        ride_body,
        out_shape=jax.ShapeDtypeStruct((rows, cols), bf16),
        grid=(1,),
        in_specs=[const_spec(mine.shape), const_spec(came.shape), pl.BlockSpec(memory_space=pl.ANY)],
        out_specs=pl.BlockSpec((EXTRA, cols), lambda i: (rows // EXTRA - 1, 0)),
        scratch_shapes=[pltpu.VMEM((EXTRA, cols), f32)],
        input_output_aliases={2: 0},
        cost_estimate=BRIEF,
        compiler_params=pltpu.CompilerParams(vmem_limit_bytes=GRANT),
        name="ride",
    )(mine, came, whole)


def norm_rows(values, gain, shift):
    center = values - jnp.mean(values, axis=-1, keepdims=True)
    spread = jnp.mean(center * center, axis=-1, keepdims=True)
    return center * lax.rsqrt(spread + EPS) * gain + shift


def split_heads(flat, rows):
    return flat.reshape(rows, LEN, flat.shape[1] // HD, HD)


def block_scores(query, keys, seg_q, seg_k, offset):
    scores = jnp.einsum(
        "rqhd,rkhd->rhqk", query, keys, preferred_element_type=jnp.float32
    ) * HD ** (-0.5)
    q_pos = offset + jnp.arange(query.shape[1], dtype=jnp.int32)
    k_pos = jnp.arange(keys.shape[1], dtype=jnp.int32)
    allowed = (seg_q[:, :, None] == seg_k[:, None, :]) & (
        k_pos[None, None, :] <= q_pos[None, :, None]
    )
    return jnp.where(allowed[:, None], scores, -1e30)


def attention_forward(query, keys, values, seg_all):
    rows = query.shape[0] // LEN
    q4 = split_heads(query, rows)
    k4 = split_heads(keys, rows)
    v4 = split_heads(values, rows)
    seg2 = seg_all.reshape(rows, LEN)
    outputs = []
    totals = []
    for block in range(LEN // QBLK):
        first = block * QBLK
        end = first + QBLK
        scores = block_scores(
            q4[:, first:end], k4[:, :end], seg2[:, first:end], seg2[:, :end], first
        )
        top = jnp.max(scores, axis=-1, keepdims=True)
        expd = jnp.exp(scores - top)
        summed = jnp.sum(expd, axis=-1, keepdims=True)
        weights = (expd / summed).astype(jnp.bfloat16)
        outputs.append(
            jnp.einsum("rhqk,rkhd->rqhd", weights, v4[:, :end], preferred_element_type=jnp.float32)
        )
        totals.append(top + jnp.log(summed))
    attended = jnp.concatenate(outputs, axis=1).reshape(query.shape).astype(jnp.bfloat16)
    return (attended, totals)


def attention_backward(query, keys, values, seg_all, totals, grad_att):
    rows = query.shape[0] // LEN
    q4 = split_heads(query, rows)
    k4 = split_heads(keys, rows)
    v4 = split_heads(values, rows)
    g4 = split_heads(grad_att, rows)
    seg2 = seg_all.reshape(rows, LEN)
    scale = HD ** (-0.5)
    grad_k = jnp.zeros(k4.shape, jnp.float32)
    grad_v = jnp.zeros(v4.shape, jnp.float32)
    grad_q_parts = []
    for block in range(LEN // QBLK):
        first = block * QBLK
        end = first + QBLK
        scores = block_scores(
            q4[:, first:end], k4[:, :end], seg2[:, first:end], seg2[:, :end], first
        )
        probs = jnp.exp(scores - totals[block])
        weights = probs.astype(jnp.bfloat16)
        grad_w = jnp.einsum(
            "rqhd,rkhd->rhqk", g4[:, first:end], v4[:, :end], preferred_element_type=jnp.float32
        )
        delta = jnp.sum(probs * grad_w, axis=-1, keepdims=True)
        grad_s = (probs * (grad_w - delta)).astype(jnp.bfloat16)
        grad_q_parts.append(
            jnp.einsum("rhqk,rkhd->rqhd", grad_s, k4[:, :end], preferred_element_type=jnp.float32)
            * scale
        )
        padding = ((0, 0), (0, LEN - end), (0, 0), (0, 0))
        grad_k = grad_k + jnp.pad(
            jnp.einsum(
                "rhqk,rqhd->rkhd", grad_s, q4[:, first:end], preferred_element_type=jnp.float32
            )
            * scale,
            padding,
        )
        grad_v = grad_v + jnp.pad(
            jnp.einsum(
                "rhqk,rqhd->rkhd", weights, g4[:, first:end], preferred_element_type=jnp.float32
            ),
            padding,
        )
    shape = query.shape
    grad_q = jnp.concatenate(grad_q_parts, axis=1).reshape(shape).astype(jnp.bfloat16)
    return (
        grad_q,
        grad_k.reshape(shape).astype(jnp.bfloat16),
        grad_v.reshape(shape).astype(jnp.bfloat16),
    )


def tensor_parallel_shards(
    tokens,
    segment_ids,
    w_qkv,
    b_qv,
    w_out,
    b_out,
    w_up,
    b_up,
    w_down,
    b_down,
    ln_gain,
    ln_bias,
    out_grad,
):
    resid = tokens.astype(jnp.float32)
    qv_bias = b_qv.astype(jnp.float32)
    up_bias = b_up.astype(jnp.float32)
    local_rows = tokens.shape[0]
    normed, first_back = jax.vjp(norm_rows, resid, ln_gain[0], ln_bias[0])
    lowered = normed.astype(jnp.bfloat16)
    joined, seg_all = (
        lax.all_gather(lowered, "mp", axis=0, tiled=True),
        lax.all_gather(segment_ids, "mp", axis=0, tiled=True),
    )
    query = (jnp.dot(joined, w_qkv[0], preferred_element_type=jnp.float32) + qv_bias[0]).astype(
        jnp.bfloat16
    )
    keys = jnp.dot(joined, w_qkv[1], preferred_element_type=jnp.float32).astype(jnp.bfloat16)
    values = (jnp.dot(joined, w_qkv[2], preferred_element_type=jnp.float32) + qv_bias[1]).astype(
        jnp.bfloat16
    )
    query, keys, values = (query, keys, values)
    attended, totals = attention_forward(query, keys, values, seg_all)
    attn_sum = lax.psum_scatter(
        jnp.dot(attended, w_out, preferred_element_type=jnp.float32).astype(jnp.bfloat16),
        "mp",
        scatter_dimension=0,
        tiled=True,
    ).astype(jnp.float32)
    mixed = resid + attn_sum + b_out.astype(jnp.float32)
    normed2, second_back = jax.vjp(norm_rows, mixed, ln_gain[1], ln_bias[1])
    lowered2 = normed2.astype(jnp.bfloat16)
    joined2 = lax.all_gather(lowered2, "mp", axis=0, tiled=True)
    pre_act = jnp.dot(joined2, w_up, preferred_element_type=jnp.float32) + up_bias
    pre_act, activ = (pre_act, jax.nn.gelu(pre_act, approximate=False).astype(jnp.bfloat16))
    block_out = (
        mixed
        + lax.psum_scatter(
            jnp.dot(activ, w_down, preferred_element_type=jnp.float32).astype(jnp.bfloat16),
            "mp",
            scatter_dimension=0,
            tiled=True,
        ).astype(jnp.float32)
        + b_down.astype(jnp.float32)
    ).astype(jnp.bfloat16)
    grad_y = out_grad.astype(jnp.float32)
    grad_z = lax.all_gather(out_grad, "mp", axis=0, tiled=True)
    grad_down = jnp.einsum("tf,td->fd", activ, grad_z, preferred_element_type=jnp.float32)
    grad_bdown = jnp.sum(grad_z, axis=0, dtype=jnp.float32)
    grad_act = jnp.einsum("td,fd->tf", grad_z, w_down, preferred_element_type=jnp.float32)
    gelu_back = jax.vjp(lambda value: jax.nn.gelu(value, approximate=False), pre_act)[1]
    grad_pre = gelu_back(grad_act)[0].astype(jnp.bfloat16)
    grad_up = jnp.einsum("td,tf->df", joined2, grad_pre, preferred_element_type=jnp.float32)
    grad_bup = jnp.sum(grad_pre, axis=0, dtype=jnp.float32)
    grad_n2 = lax.psum_scatter(
        jnp.einsum("tf,df->td", grad_pre, w_up, preferred_element_type=jnp.float32).astype(
            jnp.bfloat16
        ),
        "mp",
        scatter_dimension=0,
        tiled=True,
    ).astype(jnp.float32)
    grad_h, grad_g2, grad_s2 = second_back(grad_n2)
    grad_h = grad_h + grad_y
    grad_branch = lax.all_gather(grad_h.astype(jnp.bfloat16), "mp", axis=0, tiled=True)
    grad_wout = jnp.einsum("tc,td->cd", attended, grad_branch, preferred_element_type=jnp.float32)
    grad_bout = jnp.sum(grad_branch, axis=0, dtype=jnp.float32)
    grad_att = jnp.einsum(
        "td,cd->tc", grad_branch, w_out, preferred_element_type=jnp.float32
    ).astype(jnp.bfloat16)
    grad_q, grad_k, grad_v = attention_backward(query, keys, values, seg_all, totals, grad_att)
    grad_qkv = jnp.stack(
        [
            jnp.einsum("td,tc->dc", joined, piece, preferred_element_type=jnp.float32)
            for piece in (grad_q, grad_k, grad_v)
        ]
    )
    grad_bqv = jnp.stack(
        [jnp.sum(grad_q, axis=0, dtype=jnp.float32), jnp.sum(grad_v, axis=0, dtype=jnp.float32)]
    )
    summed = jnp.zeros((local_rows * lax.axis_size("mp"), w_qkv.shape[1]), jnp.float32)
    for index, piece in enumerate((grad_q, grad_k, grad_v)):
        summed = summed + jnp.einsum(
            "tc,dc->td", piece, w_qkv[index], preferred_element_type=jnp.float32
        )
    grad_n1 = lax.psum_scatter(
        summed.astype(jnp.bfloat16), "mp", scatter_dimension=0, tiled=True
    ).astype(jnp.float32)
    grad_x, grad_g1, grad_s1 = first_back(grad_n1)
    grad_in = grad_x + grad_h
    weight_totals = (
        lax.psum(grad_qkv.astype(jnp.bfloat16), "dp").astype(jnp.float32),
        lax.psum(grad_bqv.astype(jnp.bfloat16), "dp").astype(jnp.float32),
        lax.psum(grad_wout.astype(jnp.bfloat16), "dp").astype(jnp.float32),
        lax.psum(grad_bout.astype(jnp.bfloat16), "dp").astype(jnp.float32),
        lax.psum(grad_up.astype(jnp.bfloat16), "dp").astype(jnp.float32),
        lax.psum(grad_bup.astype(jnp.bfloat16), "dp").astype(jnp.float32),
        lax.psum(grad_down.astype(jnp.bfloat16), "dp").astype(jnp.float32),
        lax.psum(grad_bdown.astype(jnp.bfloat16), "dp").astype(jnp.float32),
    )
    norm_totals = lax.psum(
        (jnp.stack([grad_g1, grad_g2]), jnp.stack([grad_s1, grad_s2])), ("dp", "mp")
    )
    return (block_out, grad_in) + tuple(weight_totals) + tuple(norm_totals)


def row_per_chip(mesh):
    return mesh.shape["mp"] == 4 and mesh.shape["dp"] == 8


def swap(value, axis):
    return lax.ppermute(value, axis, [(0, 1), (1, 0)])


def core(value):
    return swap(value, "core")


def cross(value):
    return swap(value, "x")


def after(value, *others):
    return lax.optimization_barrier((value,) + others)[0]


def take(value, at):
    return lax.dynamic_index_in_dim(value, at, 0, keepdims=False)


def place(whole, piece, at):
    return lax.dynamic_update_index_in_dim(whole, piece, at, 0)


def quarter_of(weight):
    me = lax.axis_index("y") + 2 * (lax.axis_index("z") & 1)
    return take(weight.reshape(4, -1, weight.shape[-1]), me)


def share(mine):
    out = [swap(mine, "y")]
    for bits in (2, 3):
        out.append(lax.ppermute(mine, ("z", "y"), [(i, i ^ bits) for i in range(8)]))
    return out


def assemble(mine, others):
    me = lax.axis_index("y") + 2 * (lax.axis_index("z") & 1)
    whole = place(jnp.zeros((4,) + mine.shape, mine.dtype), mine, me)
    for bits, piece in zip((1, 2, 3), others):
        whole = place(whole, piece, me ^ bits)
    return whole.reshape(-1, mine.shape[-1])


def swap_z(value, bits):
    return lax.ppermute(value, "z", [(i, i ^ bits) for i in range(4)])


def by_side(value):
    return value.reshape(2, value.shape[0] // 2, value.shape[1])


class Line:
    def __init__(self):
        self.last = None

    def __call__(self, function, *args):
        if self.last is not None:
            args, _ = lax.optimization_barrier((args, self.last))
        out = function(*args)
        self.last = jax.tree.leaves(out)[0]
        return out


def row_per_chip_shards(
    tokens,
    segment_ids,
    w_qkv,
    b_qv,
    w_out,
    b_out,
    w_up,
    b_up,
    w_down,
    b_down,
    ln_gain,
    ln_bias,
    out_grad,
):
    side, here_y = lax.axis_index("core"), lax.axis_index("y")
    place = jnp.stack([here_y, lax.axis_index("z") & 1]).astype(jnp.int32)
    width, wide = b_qv.shape[1], tokens.shape[1]
    gains, shifts = ln_gain[:, None], ln_bias[:, None]
    line = Line()

    def pair(*parts):
        return line(lambda *all: jnp.concatenate(all), *parts)

    qkv_mine = cross(line(quarter_of, w_qkv.reshape(-1, width)))
    a1_own, sum_dz = line(first_norm, tokens, out_grad, gains[0], shifts[0])
    a1_came = core(a1_own)
    seg_other = core(segment_ids)
    small = cross(jnp.concatenate([b_qv.reshape(-1), b_up]))
    up_quarter = line(quarter_of, w_up)
    down_quarter = line(quarter_of, w_down)

    def ranges(mine, other):
        seg = jnp.concatenate([mine, other])
        start = jnp.sum((seg[None, :] < seg[:, None]).astype(jnp.int32), axis=1)[None]
        ordered = jnp.where(side == 0, seg, jnp.concatenate([other, mine]))
        blocks = ordered.reshape(LEN // BLK, BLK)
        low = jnp.sum((blocks[None, :, -1] < blocks[:, None, 0]).astype(jnp.int32), axis=1)
        return start, jnp.concatenate([(side * (LEN // BLK // 2))[None].astype(jnp.int32), low])

    start, info = line(ranges, segment_ids, seg_other)
    a1 = pair(a1_own, a1_came)
    own = tuple(line(project, a1, w_qkv, b_qv))
    qkv_mine, w_out_now, up_quarter, _ = lax.optimization_barrier((qkv_mine, w_out, up_quarter, own[0]))
    qkv_parts = share(qkv_mine)
    out_other = cross(w_out_now)
    up_mine = cross(up_quarter)
    own = own + tuple(line(partial(attn_fwd, info), *own, start))
    up_mine, down_quarter, _ = lax.optimization_barrier((up_mine, down_quarter, own[3]))
    up_parts = share(up_mine)
    down_mine = cross(down_quarter)
    qkv_other = line(assemble, qkv_mine, qkv_parts).reshape(w_qkv.shape)
    other = tuple(line(project, a1, qkv_other, small[: 2 * width].reshape(2, width)))
    other = other + tuple(line(partial(attn_fwd, info), *other, start))
    down_mine, dz_own, _ = lax.optimization_barrier((down_mine, out_grad, other[3]))
    down_parts = share(down_mine)
    dz_came = core(dz_own)

    here, there = line(partial(sum_dots, nn), [own[3], other[3]], [w_out, out_other])
    came = core(there)
    up_other = line(assemble, up_mine, up_parts)
    mixed, a2_own = line(second_norm, tokens, here, came, b_out[None], gains[1], shifts[1])
    a2_came = core(a2_own)
    dz = pair(dz_own, dz_came)
    a2 = pair(a2_own, a2_came)

    def core_halves(value):
        half = value.shape[0] // 2
        return core(value[:half]), core(value[half:])

    act_other, slope_other = line(up_gelu, a2, up_other, small[2 * width :])
    down_got = cross(line(across_frames, act_other, dz))
    act_own, slope_own = line(up_gelu, a2, w_up, b_up)
    down_own = line(across_frames, act_own, dz)
    du_own, sum_up_own = line(back_act, dz, w_down, slope_own)
    down_other = line(assemble, down_mine, down_parts)
    du_other, sum_up_other = line(back_act, dz, down_other, slope_other)
    here, there = line(partial(sum_dots, nt), [du_own, du_other], [w_up, up_other])
    came = core_halves(there)
    up_got = cross(line(across_frames, a2, du_other))
    grad_h, dattn_own, sums_h = line(norm_back, mixed, here, came, gains[1], out_grad)
    dattn_came = core_halves(dattn_own)
    up_own = line(across_frames, a2, du_own)

    def spread_y(own, got):
        return swap(line(side_sum, 1 - here_y, own, got), "y")

    def near_z(own, got, near):
        send, keep = line(quarter_sums, place, own, got, near)
        return keep, swap_z(send, 1)

    def far_z(keep, came):
        low = line(add_low, keep, came)
        return low, swap_z(low, 2)

    def back_z(low, came):
        mine = line(add_low, low, came)
        near = swap_z(mine, 1)
        return (mine, swap(mine, "y")), (near, swap(near, "y"))

    def wait_near(total):
        near, other = total[1]
        return total[0], (line(lambda value: value, near), other)

    def put(pair, prior=None, extra=0):
        fill = partial(settle, flip=0 if prior is None else 1, extra=extra)
        return line(lambda mine, other, prior: fill(place, mine, other, prior=prior), *pair, prior)

    down_own, down_got = by_side(down_own), by_side(down_got)
    down_near = spread_y(down_own, down_got)
    dattn = pair(dattn_own, *dattn_came)

    def back(entry, weight):
        query, keys, values, out, lse = entry
        cot = line(turn_back, dattn, weight)
        trio = line(partial(attn_bwd, info), query, keys, values, start, out, lse, cot)
        return (trio,) + tuple(line(frame_sums, a1, trio, out, dattn))

    trio_other, attn_other, sum_trio_other = back(other, out_other)
    first_got = cross(attn_other[0])
    second_got = cross(attn_other[1])
    down_sum = near_z(down_own, down_got, down_near)
    y_here, y_there = line(partial(sum_dots, nn), [act_own, act_other], [w_down, down_other])
    y_came = core(y_there)
    query, keys, values, out, lse = own
    cot = line(turn_back, dattn, w_out)
    down_sum = far_z(*down_sum)
    up_own, up_got = by_side(up_own), by_side(up_got)
    up_near = spread_y(up_own, up_got)
    trio_own = line(partial(attn_bwd, info), query, keys, values, start, out, lse, cot)
    attn_own, sum_trio_own = line(frame_sums, a1, trio_own, out, dattn)
    first_own, first_got = by_side(attn_own[0]), by_side(first_got)
    down_sum = back_z(*down_sum)
    block_out = line(finish, mixed, y_here, y_came, b_down[None])
    first_near = spread_y(first_own, first_got)
    here, there = line(partial(sum_dots, nt), [trio_own, trio_other], [w_qkv, qkv_other])
    came = core_halves(there)
    up_sum = near_z(up_own, up_got, up_near)
    down_sum = wait_near(down_sum)
    grad_in, _, sums_x = line(norm_back, tokens, here, came, gains[0], grad_h)
    common = line(common_rows, sums_h, sum_dz, sums_x)
    common_came = core(common)

    first_sum = near_z(first_own, first_got, first_near)
    up_sum = far_z(*up_sum)
    lines_came = cross(line(lines_of, sum_trio_other, sum_up_other, common, common_came))
    lines_own = line(lines_of, sum_trio_own, sum_up_own, common, common_came)
    second_own = line(ride, attn_own[1], lines_own, lines_came)
    second_own, second_got = by_side(second_own), by_side(second_got)
    second_near = spread_y(second_own, second_got)
    first_sum = far_z(*first_sum)
    grad_down = put(down_sum[0])
    grad_down = put(down_sum[1], grad_down)
    up_sum = back_z(*up_sum)
    second_sum = near_z(second_own, second_got, second_near)
    first_sum = back_z(*first_sum)
    up_sum = wait_near(up_sum)
    grad_up = put(up_sum[0])
    first_sum = wait_near(first_sum)
    second_sum = far_z(*second_sum)
    first = put(first_sum[0], extra=wide)
    grad_up = put(up_sum[1], grad_up)
    first = put(first_sum[1], first, extra=wide)
    second_sum = back_z(*second_sum)
    second = put(second_sum[0])
    second = put(second_sum[1], second)
    grad_qkv = lax.dynamic_update_slice(first, second[:wide], (2 * wide, 0)).reshape(w_qkv.shape)
    grad_wout = jnp.swapaxes(second[wide : 2 * wide].reshape(-1, w_out.shape[0], width), 0, 1)
    grad_wout = grad_wout.reshape(w_out.shape)
    vector = second[2 * wide :].reshape(-1)
    units = b_up.shape[0]
    ends = [2 * width, units, wide, wide, 2 * wide, 2 * wide]
    cuts = [sum(ends[:i]) for i in range(len(ends) + 1)]
    grad_bqv, grad_bup, grad_bout, grad_bdown, grad_gain, grad_shift = [
        vector[low:high] for low, high in zip(cuts[:-1], cuts[1:])
    ]
    return (
        block_out,
        grad_in,
        grad_qkv,
        grad_bqv.reshape(b_qv.shape),
        grad_wout,
        grad_bout,
        grad_up,
        grad_bup,
        grad_down,
        grad_bdown,
        grad_gain.reshape(ln_gain.shape),
        grad_shift.reshape(ln_bias.shape),
    )


def solution(mesh):
    rows, frames = ("dp", "mp"), "mp"
    body = tensor_parallel_shards
    if row_per_chip(mesh):
        shape = (mesh.shape["dp"] // 2, 2, mesh.shape["mp"] // 2, 2)
        mesh = Mesh(mesh.devices.reshape(shape), ("z", "y", "x", "core"))
        rows, frames = ("z", "y", "x", "core"), ("x", "core")
        body = row_per_chip_shards
    in_specs = (
        P(rows, None),
        P(rows),
        P(None, None, frames),
        P(None, frames),
        P(frames, None),
        P(),
        P(None, frames),
        P(frames),
        P(frames, None),
        P(),
        P(),
        P(),
        P(rows, None),
    )
    out_specs = (
        P(rows, None),
        P(rows, None),
        P(None, None, frames),
        P(None, frames),
        P(frames, None),
        P(),
        P(None, frames),
        P(frames),
        P(frames, None),
        P(),
        P(),
        P(),
    )
    return jax.shard_map(body, mesh=mesh, in_specs=in_specs, out_specs=out_specs, check_vma=False)
```
